256 devices in a mesh: row: 64 (over y, z, x_hi), col: 4 (over x_lo, core).
Axes of the slice: x: 4 (x_hi: 2, x_lo: 2; x = x_hi * 2 + x_lo), y: 4, z: 8, core: 2. Of those that a mesh axis runs over, the one named last changes fastest.
Arguments:
- matrix_slab: float32 [16384, 2048], P('row', 'col'), may hold values from -6 to 6
- sketch_matrix: float32 [144, 16384], P(None, 'row'), may hold values from -0.046875 to 0.046875
- pivots: int32 [1, 128], replicated, may hold values from 128 to 1919, as said below
Outputs:
- sketches: float32 [1, 144, 2048], P(None, None, 'col')
- q_panels: float32 [1, 16384, 128], P(None, 'row')
- r_factors: float32 [1, 128, 2048], P(None, None, 'col')
- first_factors: float32 [1, 128, 128], replicated
- slab_out: float32 [16384, 2048], P('row', 'col')
The draws below stay inside these ranges and needn't reach their ends.
Inputs may be any that keep to these rules, and one draw needn't show every extreme that they name: `pivots`: each row holds 128 different numbers.
All inputs are finite; a program needn't handle non-finite values.
Results may differ from the reference program's by a relative error of at most 0.0003.
Values sent between devices are 32-bit elements; how exact they have to be, the bound alone decides.
A program may use at most 64 MiB of HBM per device.

```python
import math
import jax
import jax.numpy as jnp
from jax import lax

NC = 2048
PANEL = 128
SKETCH = 144
PANELS = 1
M = 16384


def pivot_rows(key):
    rows_list = []
    for panel_index in range(PANELS):
        key_inner = jax.random.fold_in(key, 11 + panel_index)
        key_order = jax.random.fold_in(key, 23 + panel_index)
        inner = jax.random.permutation(key_inner, NC - 2 * PANEL - 2)[:PANEL - 2].astype(jnp.int32) + PANEL + 1
        values = jnp.concatenate([jnp.array([PANEL, NC - PANEL - 1], jnp.int32), inner])
        order = jax.random.permutation(key_order, PANEL)
        rows_list.append(values[order])
    return jnp.stack(rows_list).astype(jnp.int32)


def draw_pivots(key, part):
    return pivot_rows(key)


def variates(key, shape, uniform_law):
    if uniform_law:
        return jax.random.uniform(key, shape, jnp.float32, -1.7320508, 1.7320508)
    return jax.random.normal(key, shape, jnp.float32)


def hadamard_table():
    index = jnp.arange(PANEL, dtype=jnp.int32)
    common = jnp.bitwise_and(index[:, None], index[None, :])
    parity = jnp.zeros((PANEL, PANEL), jnp.int32)
    for bit_index in range(PANEL.bit_length()):
        parity = parity + jnp.bitwise_and(jnp.right_shift(common, bit_index), 1)
    return (1 - 2 * jnp.bitwise_and(parity, 1)).astype(jnp.float32)


def panel_block(key, panel_index, uniform_law, row_gain):
    row_factors = variates(jax.random.fold_in(key, 51 + panel_index), (M, PANEL), uniform_law)
    sign_flips = (2 * jax.random.randint(jax.random.fold_in(key, 61 + panel_index), (PANEL,), 0, 2) - 1).astype(jnp.float32)
    spectrum = 0.5 * jnp.power(jnp.float32(1000.0), -jnp.arange(PANEL, dtype=jnp.float32) / (PANEL - 1))
    scaled = row_factors * row_gain[:, None] * spectrum[None, :]
    mixed = jnp.dot(scaled, hadamard_table(), precision=lax.Precision.HIGHEST, preferred_element_type=jnp.float32)
    return mixed * sign_flips[None, :] * (1.0 / math.sqrt(PANEL))


def build_slab(key, uniform_law, rise):
    pivot_table = pivot_rows(key)
    row_gain = 1.0 + rise * jnp.arange(M, dtype=jnp.float32) / (M - 1)
    background = variates(jax.random.fold_in(key, 41), (M, NC), uniform_law) * row_gain[:, None]
    slab = jnp.clip(background, -6.0, 6.0)
    first_cols = pivot_table[0]
    slab = slab.at[:, first_cols].set(panel_block(key, 0, uniform_law, row_gain))
    if PANELS > 1:
        positions = (PANEL + pivot_table[1]).astype(jnp.int32)
        match = positions[:, None] == first_cols[None, :]
        partner = jnp.sum(match.astype(jnp.int32) * jnp.arange(PANEL, dtype=jnp.int32)[None, :], axis=1)
        moved = jnp.any(match, axis=1)
        second_cols = jnp.where(moved, partner, positions).astype(jnp.int32)
        slab = slab.at[:, second_cols].set(panel_block(key, 1, uniform_law, row_gain))
    return jnp.clip(slab, -6.0, 6.0)


def draw_matrix_slab(key, part):
    return build_slab(key, False, 2.0)


def levels(rng, dims, shards, least, top_value):
    def one(position, parts):
        draws = jax.random.uniform(jax.random.fold_in(jax.random.fold_in(rng, 6), position), (parts,), jnp.float32, least / len(shards), top_value / len(shards))
        return jnp.repeat(jnp.exp(draws), dims[position] // parts).reshape((-1,) + (1,) * (len(dims) - position - 1))

    gain = one(*shards[0])
    for cut in shards[1:]:
        gain = gain * one(*cut)
    return gain


def normal_values(rng, extent, width, limit, split=(), kind=jnp.bfloat16):
    loudness = levels(rng, extent, split, -0.22, 0.18) if split else 1.0
    entries = jax.random.normal(rng, extent, jnp.float32) * width * loudness
    return jnp.minimum(jnp.maximum(entries, -limit), limit).astype(kind)


def setup_inputs(seed: int = 0) -> dict:
    splits = jax.random.split(jax.random.key(seed), 4)
    matrix_slab = draw_matrix_slab(jax.random.fold_in(splits[3], 71), 0)
    sketch_matrix = normal_values(splits[1], (SKETCH, M), M ** -0.5, 0.046875, ((1, 64),), jnp.float32)
    pivots = draw_pivots(jax.random.fold_in(splits[3], 71), 0)
    return {"matrix_slab": matrix_slab, "sketch_matrix": sketch_matrix, "pivots": pivots}


def product(left, right):
    return jnp.dot(left.astype(jnp.float32), right.astype(jnp.float32), precision=lax.Precision.HIGHEST, preferred_element_type=jnp.float32)

def solve_right(lower, rhs):
    return lax.linalg.triangular_solve(lower, rhs, left_side=False, lower=True, transpose_a=True)

def cholesky_qr(panel_cols):
    factor_one = jnp.linalg.cholesky(product(panel_cols.T, panel_cols))
    basis_one = solve_right(factor_one, panel_cols)
    factor_two = jnp.linalg.cholesky(product(basis_one.T, basis_one))
    basis = solve_right(factor_two, basis_one)
    return (basis, product(factor_two.T, factor_one.T), factor_one)

def reference(matrix_slab, sketch_matrix, pivots):
    row_scale = math.sqrt(M)
    columns = jnp.arange(NC, dtype=jnp.int32)
    current = matrix_slab
    sketch_list = []
    q_list = []
    r_list = []
    first_list = []
    for panel_index in range(PANELS):
        panel_start = panel_index * PANEL
        sketch_list.append(product(sketch_matrix, current))
        slot_ids = (panel_start + jnp.arange(PANEL, dtype=jnp.int32)).astype(jnp.int32)
        pivot_ids = (panel_start + pivots[panel_index]).astype(jnp.int32)
        swapped = current.at[:, slot_ids].set(current[:, pivot_ids]).at[:, pivot_ids].set(current[:, slot_ids])
        panel_cols = swapped[:, panel_start:panel_start + PANEL]
        basis, r_factor, factor_one = cholesky_qr(panel_cols)
        projected = product(basis.T, swapped)
        in_slots = (columns >= panel_start) & (columns < panel_start + PANEL)
        r_block = projected.at[:, panel_start:panel_start + PANEL].set(r_factor)
        current = jnp.where(in_slots[None, :], jnp.float32(0.0), swapped - product(basis, projected))
        q_list.append(basis * row_scale)
        r_list.append(r_block / row_scale)
        first_list.append(factor_one.T / row_scale)
    return (jnp.stack(sketch_list), jnp.stack(q_list), jnp.stack(r_list), jnp.stack(first_list), current)
```

```python
import functools
import math

import jax
import jax.numpy as jnp
from jax import lax
from jax.experimental import pallas as pl
from jax.experimental.pallas import tpu as pltpu
from jax.sharding import PartitionSpec as P

PANEL = 128
NYX = 8
NZ = 8
NCOL = 4
MESH = pl.DeviceIdType.MESH
F32 = jnp.float32
BF16 = jnp.bfloat16
VMEM_SPEC = pl.BlockSpec(memory_space=pltpu.VMEM)


def hdot(left, right, contract=(1, 0)):
    return lax.dot_general(
        left,
        right,
        (((contract[0],), (contract[1],)), ((), ())),
        precision=lax.Precision.HIGHEST,
        preferred_element_type=F32,
    )


def bdot(left, right, contract=(1, 0)):
    return lax.dot_general(
        left, right, (((contract[0],), (contract[1],)), ((), ())), preferred_element_type=F32
    )


def select_dot(values, onehot, contract=(1, 0)):
    high = values.astype(BF16)
    rest = values - high.astype(F32)
    mid = rest.astype(BF16)
    low = (rest - mid.astype(F32)).astype(BF16)
    return (bdot(high, onehot, contract) + bdot(mid, onehot, contract)) + bdot(low, onehot, contract)


def two_sum(a, b):
    s = a + b
    t = s - a
    return s, (a - (s - t)) + (b - t)


def gram_levels(x):
    n = x.shape[1]
    sigma = jnp.max(jnp.abs(x), axis=0, keepdims=True) * 131072.0
    parts = []
    rest = x
    for _ in range(4):
        part = (rest + sigma) - sigma
        rest = rest - part
        parts.append(part.astype(BF16))
        sigma = sigma * (1.0 / 128.0)
    cat = jnp.concatenate(parts, axis=1)
    full = bdot(cat, cat, (0, 0))
    block = lambda i, j: full[i * n : (i + 1) * n, j * n : (j + 1) * n]
    return (
        block(0, 0),
        block(0, 1) + block(1, 0),
        (block(0, 2) + block(2, 0)) + block(1, 1),
        (block(0, 3) + block(3, 0)) + (block(1, 2) + block(2, 1)),
        (block(1, 3) + block(3, 1)) + block(2, 2),
    )


def pivot_onehot(piv, col_first, width):
    lanes = lax.broadcasted_iota(jnp.int32, (width, PANEL), 0) + col_first
    return jnp.where(lanes == piv, 1.0, 0.0).astype(BF16)


def swapped_columns(slab, lead, onehot):
    picked = bdot(jnp.ones((8, PANEL), BF16), onehot, (1, 1))[0:1, :]
    return jnp.where(picked > 0.5, select_dot(lead, onehot, (1, 1)), slab)


def remote(src, dst, send, recv, device):
    return pltpu.make_async_remote_copy(
        src_ref=src, dst_ref=dst, send_sem=send, recv_sem=recv, device_id=device, device_id_type=MESH
    )


def gather_kernel(
    slab_ref, sketch_ref, piv_ref,
    p_ref, lead_ref, g_ref, hi_ref, lo_ref, s_ref,
    pk, pp, rc1, rc2, leadbuf,
    wpart, wa, wsum, wb, wfull,
    gpart, ga, gsum, gb, gfull,
    spart, sa, ssum, sb, sb9, sfull,
    sem1, sem_lead, wa_sem, wb_sem, wc_sem, ga_sem, gb_sem, gc_sem, gd_sem,
    sa_sem, sb_sem, sb9_sem, sc_sem, sd_sem,
):
    r = lax.axis_index("row")
    c = lax.axis_index("col")
    z = lax.rem(lax.div(r, 2), NZ)
    q = lax.div(r, 16) * 2 + lax.rem(r, 2)
    width = slab_ref.shape[1]

    def yx_row(t):
        return lax.div(t, 2) * 16 + z * 2 + lax.rem(t, 2)

    def z_row(t):
        return lax.div(r, 16) * 16 + t * 2 + lax.rem(r, 2)

    barrier = pltpu.get_barrier_semaphore()
    for i in range(NYX):
        for j in range(NCOL):
            if i or j:
                pl.semaphore_signal(
                    barrier, inc=1, device_id_type=MESH,
                    device_id=(yx_row(lax.rem(q + i, NYX)), lax.rem(c + j, NCOL)),
                )
    for i in range(1, NZ):
        pl.semaphore_signal(
            barrier, inc=1, device_id=(z_row(lax.rem(z + i, NZ)), c), device_id_type=MESH
        )

    slab = slab_ref[...]
    onehot = pivot_onehot(piv_ref[...], c * width, width)
    pk[...] = select_dot(slab, onehot)
    pl.semaphore_wait(barrier, NYX * NCOL - 1 + NZ - 1)

    core = c + 1 - 2 * lax.rem(c, 2)
    chip = lax.rem(c + 2, NCOL)
    first = remote(pk, rc1, sem1.at[0], sem1.at[1], (r, core))
    first.start()
    sketch = hdot(sketch_ref[...], slab)
    for b in range(4):
        spart[18 * b : 18 * b + 18] = sketch[:, 128 * b : 128 * b + 128].reshape(18, 8, 128)
    first.wait_recv()
    pp[...] = pk[...] + rc1[...]
    second = remote(pp, rc2, sem1.at[2], sem1.at[3], (r, chip))
    second.start()

    lead_copies = [
        remote(leadbuf.at[0], leadbuf.at[1], sem_lead.at[j - 1], sem_lead.at[3], (r, j)) for j in range(1, NCOL)
    ]
    leadbuf[0] = slab[:, :PANEL]

    @pl.when(c == 0)
    def _():
        for copy in lead_copies:
            copy.start()

    second.wait_recv()
    panel = pp[...] + rc2[...]
    p_ref[...] = panel

    lane = lax.broadcasted_iota(jnp.int32, (PANEL, PANEL), 1)
    l0, l1, l2, l3, l4 = gram_levels(panel)
    high, low = two_sum(l0, l1)
    high, low2 = two_sum(high, l2)
    low = (low + low2) + (l3 + l4)
    left = lane < 64
    wpart[0:16] = jnp.where(left, high, pltpu.roll(low, 64, 1)).reshape(16, 8, 128)
    wpart[16:32] = jnp.where(left, pltpu.roll(high, 64, 1), low).reshape(16, 8, 128)

    pending = [first, second]

    def exchange(me, count, row_of, src, dst, send_sems, recv_sems):
        copies = []
        for i in range(1, count):
            t = lax.rem(me + i, count)
            copy = remote(src(t), dst(me), send_sems.at[t], recv_sems.at[me], (row_of(t), c))
            copy.start()
            copies.append(copy)
        pending.extend(copies)

    def arrived(me, count, dst, send_sems, recv_sems):
        for i in range(1, count):
            t = lax.rem(me + i, count)
            remote(dst(t), dst(t), send_sems.at[t], recv_sems.at[t], (r, c)).wait_recv()

    yx = functools.partial(exchange, q, NYX, yx_row)
    zz = functools.partial(exchange, z, NZ, z_row)

    def two_float_total(buf):
        total = buf[0]
        err = jnp.zeros((8, 128), F32)
        for k in range(1, 8):
            total, e = two_sum(total, buf[k])
            err = err + e
        lane8 = lax.broadcasted_iota(jnp.int32, (8, 128), 1)
        return jnp.where(lane8 < 64, total, total + pltpu.roll(err, 64, 1))

    yx(lambda t: wpart.at[c * 8 + t], lambda m: wa.at[m], wa_sem.at[0], wa_sem.at[1])
    yx(
        lambda t: spart.at[pl.ds(9 * t, 9)], lambda m: sa.at[m], sa_sem.at[0], sa_sem.at[1]
    )
    wa[q] = wpart[c * 8 + q]
    sa[q] = spart[pl.ds(9 * q, 9)]

    @pl.when(c != 0)
    def _():
        remote(leadbuf.at[0], leadbuf.at[1], sem_lead.at[0], sem_lead.at[3], (r, c)).wait_recv()

    lead = jnp.where(c == 0, leadbuf[0], leadbuf[1])
    lead_ref[...] = lead
    swapped = swapped_columns(slab, lead, onehot)
    inner = hdot(panel, swapped, (0, 0))
    for b in range(4):
        gpart[16 * b : 16 * b + 16] = inner[:, 128 * b : 128 * b + 128].reshape(16, 8, 128)

    arrived(q, NYX, lambda t: wa.at[t], wa_sem.at[0], wa_sem.at[1])
    wsum[0] = two_float_total(wa)
    zz(lambda t: wsum.at[0], lambda m: wb.at[m], wb_sem.at[0], wb_sem.at[1])
    yx(lambda t: gpart.at[pl.ds(8 * t, 8)], lambda m: ga.at[m], ga_sem.at[0], ga_sem.at[1])
    wb[z] = wsum[0]
    ga[q] = gpart[pl.ds(8 * q, 8)]

    arrived(q, NYX, lambda t: sa.at[t], sa_sem.at[0], sa_sem.at[1])
    total = sa[0]
    for k in range(1, NYX):
        total = total + sa[k]
    ssum[...] = total
    zz(lambda t: ssum.at[t], lambda m: sb.at[m], sb_sem.at[0], sb_sem.at[1])
    zz(lambda t: ssum.at[8], lambda m: sb9.at[m], sb9_sem.at[0], sb9_sem.at[1])
    sb[z] = ssum[z]
    sb9[z] = ssum[8]

    arrived(z, NZ, lambda t: wb.at[t], wb_sem.at[0], wb_sem.at[1])
    mine = c * 8 + q
    wsum[1] = two_float_total(wb)
    for i in range(NYX):
        for j in range(NCOL):
            if i or j:
                t = lax.rem(q + i, NYX)
                d = lax.rem(c + j, NCOL)
                copy = remote(
                    wsum.at[1], wfull.at[mine], wc_sem.at[0, d * 8 + t], wc_sem.at[1, mine], (yx_row(t), d)
                )
                copy.start()
                pending.append(copy)
    wfull[mine] = wsum[1]

    arrived(q, NYX, lambda t: ga.at[t], ga_sem.at[0], ga_sem.at[1])
    total = ga[0]
    for k in range(1, NYX):
        total = total + ga[k]
    gsum[...] = total
    zz(lambda t: gsum.at[t], lambda m: gb.at[m], gb_sem.at[0], gb_sem.at[1])
    gb[z] = gsum[z]

    arrived(z, NZ, lambda t: sb.at[t], sb_sem.at[0], sb_sem.at[1])
    arrived(z, NZ, lambda t: sb9.at[t], sb9_sem.at[0], sb9_sem.at[1])
    total, ninth = sb[0], sb9[0]
    for k in range(1, NZ):
        total = total + sb[k]
        ninth = ninth + sb9[k]
    sfull[q * 9 + z] = total
    sfull[q * 9 + 8] = ninth
    zz(
        lambda t: sfull.at[q * 9 + z], lambda m: sfull.at[q * 9 + m], sc_sem.at[0], sc_sem.at[1]
    )

    arrived(z, NZ, lambda t: gb.at[t], gb_sem.at[0], gb_sem.at[1])
    total = gb[0]
    for k in range(1, NZ):
        total = total + gb[k]
    gfull[q * 8 + z] = total
    zz(
        lambda t: gfull.at[q * 8 + z], lambda m: gfull.at[q * 8 + m], gc_sem.at[0], gc_sem.at[1]
    )

    arrived(z, NZ, lambda t: sfull.at[q * 9 + t], sc_sem.at[0], sc_sem.at[1])
    yx(
        lambda t: sfull.at[pl.ds(q * 9, 9)], lambda m: sfull.at[pl.ds(m * 9, 9)], sd_sem.at[0], sd_sem.at[1]
    )
    arrived(z, NZ, lambda t: gfull.at[q * 8 + t], gc_sem.at[0], gc_sem.at[1])
    yx(
        lambda t: gfull.at[pl.ds(q * 8, 8)], lambda m: gfull.at[pl.ds(m * 8, 8)], gd_sem.at[0], gd_sem.at[1]
    )

    for i in range(NYX):
        for j in range(NCOL):
            if i or j:
                o = lax.rem(c + j, NCOL) * 8 + lax.rem(q + i, NYX)
                remote(wfull.at[o], wfull.at[o], wc_sem.at[0, o], wc_sem.at[1, o], (r, c)).wait_recv()
    first_half = wfull[0:16].reshape(PANEL, PANEL)
    second_half = wfull[16:32].reshape(PANEL, PANEL)
    hi_ref[...] = jnp.where(left, first_half, pltpu.roll(second_half, 64, 1))
    lo_ref[...] = jnp.where(left, pltpu.roll(first_half, 64, 1), second_half)

    arrived(q, NYX, lambda t: sfull.at[pl.ds(t * 9, 9)], sd_sem.at[0], sd_sem.at[1])
    for b in range(4):
        s_ref[0, :, 128 * b : 128 * b + 128] = sfull[18 * b : 18 * b + 18].reshape(144, 128)
    arrived(q, NYX, lambda t: gfull.at[pl.ds(t * 8, 8)], gd_sem.at[0], gd_sem.at[1])
    for b in range(4):
        g_ref[:, 128 * b : 128 * b + 128] = gfull[16 * b : 16 * b + 16].reshape(128, 128)

    for copy in pending:
        copy.wait_send()

    @pl.when(c == 0)
    def _():
        for copy in lead_copies:
            copy.wait_send()


def eliminate(aug):
    sub = lax.broadcasted_iota(jnp.int32, (8, 2 * PANEL), 0)
    sub1 = lax.broadcasted_iota(jnp.int32, (8, 1), 0)
    for b in range(PANEL // 8):
        rows = aug[8 * b : 8 * b + 8, :]
        for i in range(8):
            at = 8 * b + i
            column = rows[:, at : at + 1]
            inv = lax.rsqrt(column[i : i + 1, :])
            pivot_row = rows[i : i + 1, :] * inv
            coef = jnp.where(sub1 > i, column * inv, 0.0)
            rows = jnp.where(sub == i, pivot_row, rows - coef * pivot_row)
        aug[8 * b : 8 * b + 8, :] = rows
        if b < PANEL // 8 - 1:
            update = hdot(rows[:, :PANEL], rows, (0, 0))
            aug[8 * b + 8 :, :] = aug[8 * b + 8 :, :] - update[8 * b + 8 :, :]


def factor_kernel(
    slab_ref, piv_ref, p_ref, lead_ref, g_ref, hi_ref, lo_ref,
    q_ref, r_ref, first_ref, out_ref, aug,
):
    c = lax.axis_index("col")
    width = slab_ref.shape[1]
    rowi = lax.broadcasted_iota(jnp.int32, (PANEL, PANEL), 0)
    coli = lax.broadcasted_iota(jnp.int32, (PANEL, PANEL), 1)
    eye = jnp.where(rowi == coli, 1.0, 0.0).astype(F32)
    upper = coli >= rowi
    lower = coli <= rowi
    scale = 1.0 / 128.0

    high = hi_ref[...]
    aug[:, :PANEL] = high
    aug[:, PANEL:] = eye
    eliminate(aug)
    r_one = jnp.where(upper, aug[:, :PANEL], 0.0)
    x_one = jnp.where(lower, aug[:, PANEL:], 0.0)
    first_ref[0] = r_one * scale

    l0, l1, l2, l3, l4 = gram_levels(r_one)
    d, e1 = two_sum(high, -l0)
    d, e2 = two_sum(d, -l1)
    delta = (d - l2) + (((e1 + e2) + lo_ref[...]) - (l3 + l4))
    gram_two = eye + hdot(hdot(x_one, delta), x_one, (1, 1))
    aug[:, :PANEL] = gram_two
    aug[:, PANEL:] = eye
    eliminate(aug)
    r_two = jnp.where(upper, aug[:, :PANEL], 0.0)
    x_two = jnp.where(lower, aug[:, PANEL:], 0.0)
    r_factor = hdot(r_two, r_one)

    slab = slab_ref[...]
    onehot = pivot_onehot(piv_ref[...], c * width, width)
    swapped = swapped_columns(slab, lead_ref[...], onehot)
    basis = hdot(hdot(p_ref[...], x_one, (1, 1)), x_two, (1, 1))
    projected = hdot(x_two, hdot(x_one, g_ref[...]))
    q_ref[0] = basis * 128.0
    lead_block = c == 0
    r_ref[0, :, :PANEL] = jnp.where(lead_block, r_factor, projected[:, :PANEL]) * scale
    r_ref[0, :, PANEL:] = projected[:, PANEL:] * scale
    rest = swapped - hdot(basis, projected)
    out_ref[:, :PANEL] = jnp.where(lead_block, 0.0, rest[:, :PANEL])
    out_ref[:, PANEL:] = rest[:, PANEL:]


def shards(matrix_slab, sketch_matrix, pivots):
    rows, width = matrix_slab.shape
    sk = sketch_matrix.shape[0]
    dma = pltpu.SemaphoreType.DMA
    tile = lambda *lead: pltpu.VMEM(lead + (8, 128), F32)
    flat = lambda *shape: jax.ShapeDtypeStruct(shape, F32)
    panel, lead, inner, high, low, sketches = pl.pallas_call(
        gather_kernel,
        out_shape=(
            flat(rows, PANEL), flat(rows, PANEL), flat(PANEL, width),
            flat(PANEL, PANEL), flat(PANEL, PANEL), flat(1, sk, width),
        ),
        in_specs=[VMEM_SPEC] * 3,
        out_specs=(VMEM_SPEC,) * 6,
        scratch_shapes=[
            pltpu.VMEM((rows, PANEL), F32), pltpu.VMEM((rows, PANEL), F32),
            pltpu.VMEM((rows, PANEL), F32), pltpu.VMEM((rows, PANEL), F32),
            pltpu.VMEM((2, rows, PANEL), F32),
            tile(32), tile(8), tile(2), tile(8), tile(32),
            tile(64), tile(8, 8), tile(8), tile(8), tile(64),
            tile(72), tile(8, 9), tile(9), tile(8), tile(8), tile(72),
            dma((4,)), dma((4,)), dma((2, 8)), dma((2, 8)), dma((2, 32)),
            dma((2, 8)), dma((2, 8)), dma((2, 8)), dma((2, 8)),
            dma((2, 8)), dma((2, 8)), dma((2, 8)), dma((2, 8)), dma((2, 8)),
        ],
        compiler_params=pltpu.CompilerParams(
            collective_id=0, has_side_effects=True, vmem_limit_bytes=32 * 1024 * 1024
        ),
        name="gather",
    )(matrix_slab, sketch_matrix, pivots)
    q_panels, r_factors, first, slab_out = pl.pallas_call(
        factor_kernel,
        out_shape=(
            flat(1, rows, PANEL), flat(1, PANEL, width), flat(1, PANEL, PANEL), flat(rows, width),
        ),
        in_specs=[VMEM_SPEC] * 7,
        out_specs=(VMEM_SPEC,) * 4,
        scratch_shapes=[pltpu.VMEM((PANEL, 2 * PANEL), F32)],
        compiler_params=pltpu.CompilerParams(vmem_limit_bytes=32 * 1024 * 1024),
        name="factor",
    )(matrix_slab, pivots, panel, lead, inner, high, low)
    return sketches, q_panels, r_factors, first, slab_out


def solution(mesh):
    in_specs = (P("row", "col"), P(None, "row"), P())
    out_specs = (
        P(None, None, "col"),
        P(None, "row", None),
        P(None, None, "col"),
        P(),
        P("row", "col"),
    )
    return jax.shard_map(shards, mesh=mesh, in_specs=in_specs, out_specs=out_specs, check_vma=False)
```

```python
import functools
import math

import jax
import jax.numpy as jnp
from jax import lax
from jax.experimental import pallas as pl
from jax.experimental.pallas import tpu as pltpu
from jax.sharding import PartitionSpec as P

PANEL = 128
NYX = 8
NZ = 8
NCOL = 4
MESH = pl.DeviceIdType.MESH
F32 = jnp.float32
BF16 = jnp.bfloat16
VMEM_SPEC = pl.BlockSpec(memory_space=pltpu.VMEM)


def hdot(left, right, contract=(1, 0)):
    return lax.dot_general(
        left,
        right,
        (((contract[0],), (contract[1],)), ((), ())),
        precision=lax.Precision.HIGHEST,
        preferred_element_type=F32,
    )


def bdot(left, right, contract=(1, 0)):
    return lax.dot_general(
        left, right, (((contract[0],), (contract[1],)), ((), ())), preferred_element_type=F32
    )


def select_dot(values, onehot, contract=(1, 0)):
    high = values.astype(BF16)
    rest = values - high.astype(F32)
    mid = rest.astype(BF16)
    low = (rest - mid.astype(F32)).astype(BF16)
    return (bdot(high, onehot, contract) + bdot(mid, onehot, contract)) + bdot(low, onehot, contract)


def two_sum(a, b):
    s = a + b
    t = s - a
    return s, (a - (s - t)) + (b - t)


def gram_levels(x):
    n = x.shape[1]
    sigma = jnp.max(jnp.abs(x), axis=0, keepdims=True) * 131072.0
    parts = []
    rest = x
    for _ in range(4):
        part = (rest + sigma) - sigma
        rest = rest - part
        parts.append(part.astype(BF16))
        sigma = sigma * (1.0 / 128.0)
    cat = jnp.concatenate(parts, axis=1)
    full = bdot(cat, cat, (0, 0))
    block = lambda i, j: full[i * n : (i + 1) * n, j * n : (j + 1) * n]
    return (
        block(0, 0),
        block(0, 1) + block(1, 0),
        (block(0, 2) + block(2, 0)) + block(1, 1),
        (block(0, 3) + block(3, 0)) + (block(1, 2) + block(2, 1)),
        (block(1, 3) + block(3, 1)) + block(2, 2),
    )


def pivot_onehot(piv, col_first, width):
    lanes = lax.broadcasted_iota(jnp.int32, (width, PANEL), 0) + col_first
    return jnp.where(lanes == piv, 1.0, 0.0).astype(BF16)


def swapped_columns(slab, lead, onehot):
    picked = bdot(jnp.ones((8, PANEL), BF16), onehot, (1, 1))[0:1, :]
    return jnp.where(picked > 0.5, select_dot(lead, onehot, (1, 1)), slab)


def remote(src, dst, send, recv, device):
    return pltpu.make_async_remote_copy(
        src_ref=src, dst_ref=dst, send_sem=send, recv_sem=recv, device_id=device, device_id_type=MESH
    )


def gather_kernel(
    slab_ref, sketch_ref, piv_ref,
    p_ref, lead_ref, g_ref, hi_ref, lo_ref, s_ref,
    pk, pp, rc1, rc2, leadbuf,
    wpart, wa, wsum, wb, wfull,
    gpart, ga, gsum, gb, gfull,
    spart, sa, ssum, sb, sb9, sfull,
    sem1, sem_lead, wa_sem, wb_sem, wc_sem, ga_sem, gb_sem, gc_sem, gd_sem,
    sa_sem, sb_sem, sb9_sem, sc_sem, sd_sem,
):
    r = lax.axis_index("row")
    c = lax.axis_index("col")
    z = lax.rem(lax.div(r, 2), NZ)
    q = lax.div(r, 16) * 2 + lax.rem(r, 2)
    width = slab_ref.shape[1]

    def yx_row(t):
        return lax.div(t, 2) * 16 + z * 2 + lax.rem(t, 2)

    def z_row(t):
        return lax.div(r, 16) * 16 + t * 2 + lax.rem(r, 2)

    barrier = pltpu.get_barrier_semaphore()
    for i in range(NYX):
        for j in range(NCOL):
            if i or j:
                pl.semaphore_signal(
                    barrier, inc=1, device_id_type=MESH,
                    device_id=(yx_row(lax.rem(q + i, NYX)), lax.rem(c + j, NCOL)),
                )
    for i in range(1, NZ):
        pl.semaphore_signal(
            barrier, inc=1, device_id=(z_row(lax.rem(z + i, NZ)), c), device_id_type=MESH
        )

    slab = slab_ref[...]
    onehot = pivot_onehot(piv_ref[...], c * width, width)
    pk[...] = select_dot(slab, onehot)
    pl.semaphore_wait(barrier, NYX * NCOL - 1 + NZ - 1)

    core = c + 1 - 2 * lax.rem(c, 2)
    chip = lax.rem(c + 2, NCOL)
    first = remote(pk, rc1, sem1.at[0], sem1.at[1], (r, core))
    first.start()
    sketch = hdot(sketch_ref[...], slab)
    for b in range(4):
        spart[18 * b : 18 * b + 18] = sketch[:, 128 * b : 128 * b + 128].reshape(18, 8, 128)
    first.wait_recv()
    pp[...] = pk[...] + rc1[...]
    second = remote(pp, rc2, sem1.at[2], sem1.at[3], (r, chip))
    second.start()

    lead_copies = [
        remote(leadbuf.at[0], leadbuf.at[1], sem_lead.at[j - 1], sem_lead.at[3], (r, j)) for j in range(1, NCOL)
    ]
    leadbuf[0] = slab[:, :PANEL]

    @pl.when(c == 0)
    def _():
        for copy in lead_copies:
            copy.start()

    second.wait_recv()
    panel = pp[...] + rc2[...]
    p_ref[...] = panel

    lane = lax.broadcasted_iota(jnp.int32, (PANEL, PANEL), 1)
    l0, l1, l2, l3, l4 = gram_levels(panel)
    high, low = two_sum(l0, l1)
    high, low2 = two_sum(high, l2)
    low = (low + low2) + (l3 + l4)
    left = lane < 64
    wpart[0:16] = jnp.where(left, high, pltpu.roll(low, 64, 1)).reshape(16, 8, 128)
    wpart[16:32] = jnp.where(left, pltpu.roll(high, 64, 1), low).reshape(16, 8, 128)

    pending = [first, second]

    def exchange(me, count, row_of, src, dst, send_sems, recv_sems):
        copies = []
        for i in range(1, count):
            t = lax.rem(me + i, count)
            copy = remote(src(t), dst(me), send_sems.at[t], recv_sems.at[me], (row_of(t), c))
            copy.start()
            copies.append(copy)
        pending.extend(copies)

    def arrived(me, count, dst, send_sems, recv_sems):
        for i in range(1, count):
            t = lax.rem(me + i, count)
            remote(dst(t), dst(t), send_sems.at[t], recv_sems.at[t], (r, c)).wait_recv()

    yx = functools.partial(exchange, q, NYX, yx_row)
    zz = functools.partial(exchange, z, NZ, z_row)

    def two_float_total(buf):
        total = buf[0]
        err = jnp.zeros((8, 128), F32)
        for k in range(1, 8):
            total, e = two_sum(total, buf[k])
            err = err + e
        lane8 = lax.broadcasted_iota(jnp.int32, (8, 128), 1)
        return jnp.where(lane8 < 64, total, total + pltpu.roll(err, 64, 1))

    yx(lambda t: wpart.at[c * 8 + t], lambda m: wa.at[m], wa_sem.at[0], wa_sem.at[1])
    yx(
        lambda t: spart.at[pl.ds(9 * t, 9)], lambda m: sa.at[m], sa_sem.at[0], sa_sem.at[1]
    )
    wa[q] = wpart[c * 8 + q]
    sa[q] = spart[pl.ds(9 * q, 9)]

    @pl.when(c != 0)
    def _():
        remote(leadbuf.at[0], leadbuf.at[1], sem_lead.at[0], sem_lead.at[3], (r, c)).wait_recv()

    lead = jnp.where(c == 0, leadbuf[0], leadbuf[1])
    lead_ref[...] = lead
    swapped = swapped_columns(slab, lead, onehot)
    inner = hdot(panel, swapped, (0, 0))
    for b in range(4):
        gpart[16 * b : 16 * b + 16] = inner[:, 128 * b : 128 * b + 128].reshape(16, 8, 128)

    arrived(q, NYX, lambda t: wa.at[t], wa_sem.at[0], wa_sem.at[1])
    wsum[0] = two_float_total(wa)
    zz(lambda t: wsum.at[0], lambda m: wb.at[m], wb_sem.at[0], wb_sem.at[1])
    yx(lambda t: gpart.at[pl.ds(8 * t, 8)], lambda m: ga.at[m], ga_sem.at[0], ga_sem.at[1])
    wb[z] = wsum[0]
    ga[q] = gpart[pl.ds(8 * q, 8)]

    arrived(q, NYX, lambda t: sa.at[t], sa_sem.at[0], sa_sem.at[1])
    total = sa[0]
    for k in range(1, NYX):
        total = total + sa[k]
    ssum[...] = total
    zz(lambda t: ssum.at[t], lambda m: sb.at[m], sb_sem.at[0], sb_sem.at[1])
    zz(lambda t: ssum.at[8], lambda m: sb9.at[m], sb9_sem.at[0], sb9_sem.at[1])
    sb[z] = ssum[z]
    sb9[z] = ssum[8]

    arrived(z, NZ, lambda t: wb.at[t], wb_sem.at[0], wb_sem.at[1])
    mine = c * 8 + q
    wsum[1] = two_float_total(wb)
    for i in range(NYX):
        for j in range(NCOL):
            if i or j:
                t = lax.rem(q + i, NYX)
                d = lax.rem(c + j, NCOL)
                copy = remote(
                    wsum.at[1], wfull.at[mine], wc_sem.at[0, d * 8 + t], wc_sem.at[1, mine], (yx_row(t), d)
                )
                copy.start()
                pending.append(copy)
    wfull[mine] = wsum[1]

    arrived(q, NYX, lambda t: ga.at[t], ga_sem.at[0], ga_sem.at[1])
    total = ga[0]
    for k in range(1, NYX):
        total = total + ga[k]
    gsum[...] = total
    zz(lambda t: gsum.at[t], lambda m: gb.at[m], gb_sem.at[0], gb_sem.at[1])
    gb[z] = gsum[z]

    arrived(z, NZ, lambda t: sb.at[t], sb_sem.at[0], sb_sem.at[1])
    arrived(z, NZ, lambda t: sb9.at[t], sb9_sem.at[0], sb9_sem.at[1])
    total, ninth = sb[0], sb9[0]
    for k in range(1, NZ):
        total = total + sb[k]
        ninth = ninth + sb9[k]
    sfull[q * 9 + z] = total
    sfull[q * 9 + 8] = ninth
    zz(
        lambda t: sfull.at[q * 9 + z], lambda m: sfull.at[q * 9 + m], sc_sem.at[0], sc_sem.at[1]
    )

    arrived(z, NZ, lambda t: gb.at[t], gb_sem.at[0], gb_sem.at[1])
    total = gb[0]
    for k in range(1, NZ):
        total = total + gb[k]
    gfull[q * 8 + z] = total
    zz(
        lambda t: gfull.at[q * 8 + z], lambda m: gfull.at[q * 8 + m], gc_sem.at[0], gc_sem.at[1]
    )

    arrived(z, NZ, lambda t: sfull.at[q * 9 + t], sc_sem.at[0], sc_sem.at[1])
    yx(
        lambda t: sfull.at[pl.ds(q * 9, 9)], lambda m: sfull.at[pl.ds(m * 9, 9)], sd_sem.at[0], sd_sem.at[1]
    )
    arrived(z, NZ, lambda t: gfull.at[q * 8 + t], gc_sem.at[0], gc_sem.at[1])
    yx(
        lambda t: gfull.at[pl.ds(q * 8, 8)], lambda m: gfull.at[pl.ds(m * 8, 8)], gd_sem.at[0], gd_sem.at[1]
    )

    for i in range(NYX):
        for j in range(NCOL):
            if i or j:
                o = lax.rem(c + j, NCOL) * 8 + lax.rem(q + i, NYX)
                remote(wfull.at[o], wfull.at[o], wc_sem.at[0, o], wc_sem.at[1, o], (r, c)).wait_recv()
    first_half = wfull[0:16].reshape(PANEL, PANEL)
    second_half = wfull[16:32].reshape(PANEL, PANEL)
    hi_ref[...] = jnp.where(left, first_half, pltpu.roll(second_half, 64, 1))
    lo_ref[...] = jnp.where(left, pltpu.roll(first_half, 64, 1), second_half)

    arrived(q, NYX, lambda t: sfull.at[pl.ds(t * 9, 9)], sd_sem.at[0], sd_sem.at[1])
    for b in range(4):
        s_ref[0, :, 128 * b : 128 * b + 128] = sfull[18 * b : 18 * b + 18].reshape(144, 128)
    arrived(q, NYX, lambda t: gfull.at[pl.ds(t * 8, 8)], gd_sem.at[0], gd_sem.at[1])
    for b in range(4):
        g_ref[:, 128 * b : 128 * b + 128] = gfull[16 * b : 16 * b + 16].reshape(128, 128)

    for copy in pending:
        copy.wait_send()

    @pl.when(c == 0)
    def _():
        for copy in lead_copies:
            copy.wait_send()


def tree_sum(terms):
    terms = list(terms)
    while len(terms) > 1:
        pairs = [terms[i] + terms[i + 1] for i in range(0, len(terms) - 1, 2)]
        terms = pairs + terms[len(pairs) * 2 :]
    return terms[0]


def spread(v):
    return jnp.broadcast_to(v, (8, 128))


def block_factor(v, first, sub, lane):
    columns = [spread(v[:, first + j : first + j + 1]) for j in range(8)]
    a = {(i, j): spread(columns[i][j : j + 1, :]) for j in range(8) for i in range(j + 1)}
    m = [[None] * 8 for _ in range(8)]
    for i in range(8):
        inv = lax.rsqrt(a[i, i])
        l = {j: a[i, j] * inv for j in range(i + 1, 8)}
        for j in range(i + 1, 8):
            for k in range(j, 8):
                a[j, k] = a[j, k] - l[j] * l[k]
        for j in range(i):
            m[i][j] = m[i][j] * inv
        m[i][i] = inv
        for k in range(i + 1, 8):
            for j in range(i + 1):
                t = l[k] * m[i][j]
                m[k][j] = -t if m[k][j] is None else m[k][j] - t
    terms = []
    inverse = jnp.zeros((8, 128), F32)
    for j in range(8):
        column = m[7][j]
        for k in range(6, j - 1, -1):
            column = jnp.where(sub <= k, m[k][j], column)
        if j > 0:
            column = jnp.where(sub < j, 0.0, column)
        terms.append(column * spread(v[j : j + 1, :]))
        inverse = jnp.where(lane == first + j, column, inverse)
    solved = tree_sum(terms)
    inside = (lane >= first) & (lane < first + 8)
    return solved, jnp.where(inside, inverse, solved), m


def eliminate(w, r_ref, x_ref):
    sub = lax.broadcasted_iota(jnp.int32, (8, 128), 0)
    lane = lax.broadcasted_iota(jnp.int32, (8, 128), 1)
    count = PANEL // 8
    blocks = [w[8 * b : 8 * b + 8, :] for b in range(count)]
    for b in range(count):
        first = 8 * b
        solved, both, m = block_factor(blocks[b], first, sub, lane)
        upper = jnp.where(lane >= first + sub, solved, 0.0)
        r_ref[first : first + 8, :] = upper
        x_ref[first : first + 8, :] = jnp.where(lane < first + 8, both, 0.0)
        if b == count - 1:
            break
        inside = (lane >= first) & (lane < first + 8)
        rows = blocks[b + 1]
        columns = [spread(rows[:, first + j : first + j + 1]) for j in range(8)]
        updates = []
        for p in range(8):
            coef = tree_sum([m[p][j] * columns[j] for j in range(p + 1)])
            updates.append(coef * spread(both[p : p + 1, :]))
        blocks[b + 1] = jnp.where(inside, 0.0, rows) - tree_sum(updates)
        if b + 2 < count:
            update = hdot(upper, both, (0, 0))
            for k in range(b + 2, count):
                blocks[k] = jnp.where(inside, 0.0, blocks[k]) - update[8 * k : 8 * k + 8, :]


def factor_kernel(
    slab_ref, piv_ref, p_ref, lead_ref, g_ref, hi_ref, lo_ref,
    q_ref, r_ref, first_ref, out_ref, rbuf, xbuf,
):
    c = lax.axis_index("col")
    width = slab_ref.shape[1]
    rowi = lax.broadcasted_iota(jnp.int32, (PANEL, PANEL), 0)
    coli = lax.broadcasted_iota(jnp.int32, (PANEL, PANEL), 1)
    eye = jnp.where(rowi == coli, 1.0, 0.0).astype(F32)
    scale = 1.0 / 128.0

    high = hi_ref[...]
    eliminate(high, rbuf.at[0], xbuf.at[0])
    r_one = rbuf[0]
    x_one = xbuf[0]
    first_ref[0] = r_one * scale

    l0, l1, l2, l3, l4 = gram_levels(r_one)
    d, e1 = two_sum(high, -l0)
    d, e2 = two_sum(d, -l1)
    delta = (d - l2) + (((e1 + e2) + lo_ref[...]) - (l3 + l4))
    gram_two = eye + hdot(hdot(x_one, delta), x_one, (1, 1))
    eliminate(gram_two, rbuf.at[1], xbuf.at[1])
    r_two = rbuf[1]
    x_two = xbuf[1]
    r_factor = hdot(r_two, r_one)

    slab = slab_ref[...]
    onehot = pivot_onehot(piv_ref[...], c * width, width)
    swapped = swapped_columns(slab, lead_ref[...], onehot)
    basis = hdot(hdot(p_ref[...], x_one, (1, 1)), x_two, (1, 1))
    projected = hdot(x_two, hdot(x_one, g_ref[...]))
    q_ref[0] = basis * 128.0
    lead_block = c == 0
    r_ref[0, :, :PANEL] = jnp.where(lead_block, r_factor, projected[:, :PANEL]) * scale
    r_ref[0, :, PANEL:] = projected[:, PANEL:] * scale
    rest = swapped - hdot(basis, projected)
    out_ref[:, :PANEL] = jnp.where(lead_block, 0.0, rest[:, :PANEL])
    out_ref[:, PANEL:] = rest[:, PANEL:]


def shards(matrix_slab, sketch_matrix, pivots):
    rows, width = matrix_slab.shape
    sk = sketch_matrix.shape[0]
    dma = pltpu.SemaphoreType.DMA
    tile = lambda *lead: pltpu.VMEM(lead + (8, 128), F32)
    flat = lambda *shape: jax.ShapeDtypeStruct(shape, F32)
    panel, lead, inner, high, low, sketches = pl.pallas_call(
        gather_kernel,
        out_shape=(
            flat(rows, PANEL), flat(rows, PANEL), flat(PANEL, width),
            flat(PANEL, PANEL), flat(PANEL, PANEL), flat(1, sk, width),
        ),
        in_specs=[VMEM_SPEC] * 3,
        out_specs=(VMEM_SPEC,) * 6,
        scratch_shapes=[
            pltpu.VMEM((rows, PANEL), F32), pltpu.VMEM((rows, PANEL), F32),
            pltpu.VMEM((rows, PANEL), F32), pltpu.VMEM((rows, PANEL), F32),
            pltpu.VMEM((2, rows, PANEL), F32),
            tile(32), tile(8), tile(2), tile(8), tile(32),
            tile(64), tile(8, 8), tile(8), tile(8), tile(64),
            tile(72), tile(8, 9), tile(9), tile(8), tile(8), tile(72),
            dma((4,)), dma((4,)), dma((2, 8)), dma((2, 8)), dma((2, 32)),
            dma((2, 8)), dma((2, 8)), dma((2, 8)), dma((2, 8)),
            dma((2, 8)), dma((2, 8)), dma((2, 8)), dma((2, 8)), dma((2, 8)),
        ],
        compiler_params=pltpu.CompilerParams(
            collective_id=0, has_side_effects=True, vmem_limit_bytes=32 * 1024 * 1024
        ),
        name="gather",
    )(matrix_slab, sketch_matrix, pivots)
    q_panels, r_factors, first, slab_out = pl.pallas_call(
        factor_kernel,
        out_shape=(
            flat(1, rows, PANEL), flat(1, PANEL, width), flat(1, PANEL, PANEL), flat(rows, width),
        ),
        in_specs=[VMEM_SPEC] * 7,
        out_specs=(VMEM_SPEC,) * 4,
        scratch_shapes=[pltpu.VMEM((2, PANEL, PANEL), F32)] * 2,
        compiler_params=pltpu.CompilerParams(vmem_limit_bytes=32 * 1024 * 1024),
        name="factor",
    )(matrix_slab, pivots, panel, lead, inner, high, low)
    return sketches, q_panels, r_factors, first, slab_out


def solution(mesh):
    in_specs = (P("row", "col"), P(None, "row"), P())
    out_specs = (
        P(None, None, "col"),
        P(None, "row", None),
        P(None, None, "col"),
        P(),
        P("row", "col"),
    )
    return jax.shard_map(shards, mesh=mesh, in_specs=in_specs, out_specs=out_specs, check_vma=False)
```

```python
import functools
import math

import jax
import jax.numpy as jnp
from jax import lax
from jax.experimental import pallas as pl
from jax.experimental.pallas import tpu as pltpu
from jax.sharding import PartitionSpec as P

PANEL = 128
NYX = 8
NZ = 8
NCOL = 4
MESH = pl.DeviceIdType.MESH
F32 = jnp.float32
BF16 = jnp.bfloat16
VMEM_SPEC = pl.BlockSpec(memory_space=pltpu.VMEM)


def hdot(left, right, contract=(1, 0)):
    return lax.dot_general(
        left,
        right,
        (((contract[0],), (contract[1],)), ((), ())),
        precision=lax.Precision.HIGHEST,
        preferred_element_type=F32,
    )


def bdot(left, right, contract=(1, 0)):
    return lax.dot_general(
        left, right, (((contract[0],), (contract[1],)), ((), ())), preferred_element_type=F32
    )


def select_dot(values, onehot, contract=(1, 0)):
    high = values.astype(BF16)
    rest = values - high.astype(F32)
    mid = rest.astype(BF16)
    low = (rest - mid.astype(F32)).astype(BF16)
    return (bdot(high, onehot, contract) + bdot(mid, onehot, contract)) + bdot(low, onehot, contract)


def two_sum(a, b):
    s = a + b
    t = s - a
    return s, (a - (s - t)) + (b - t)


def gram_levels(x):
    n = x.shape[1]
    sigma = jnp.max(jnp.abs(x), axis=0, keepdims=True) * 131072.0
    parts = []
    rest = x
    for _ in range(4):
        part = (rest + sigma) - sigma
        rest = rest - part
        parts.append(part.astype(BF16))
        sigma = sigma * (1.0 / 128.0)
    cat = jnp.concatenate(parts, axis=1)
    full = bdot(cat, cat, (0, 0))
    block = lambda i, j: full[i * n : (i + 1) * n, j * n : (j + 1) * n]
    return (
        block(0, 0),
        block(0, 1) + block(1, 0),
        (block(0, 2) + block(2, 0)) + block(1, 1),
        (block(0, 3) + block(3, 0)) + (block(1, 2) + block(2, 1)),
        (block(1, 3) + block(3, 1)) + block(2, 2),
    )


def pivot_onehot(piv, col_first, width):
    lanes = lax.broadcasted_iota(jnp.int32, (width, PANEL), 0) + col_first
    return jnp.where(lanes == piv, 1.0, 0.0).astype(BF16)


def swapped_columns(slab, lead, onehot):
    picked = bdot(jnp.ones((8, PANEL), BF16), onehot, (1, 1))[0:1, :]
    return jnp.where(picked > 0.5, select_dot(lead, onehot, (1, 1)), slab)


def remote(src, dst, send, recv, device):
    return pltpu.make_async_remote_copy(
        src_ref=src, dst_ref=dst, send_sem=send, recv_sem=recv, device_id=device, device_id_type=MESH
    )


def reduce_kernel(
    slab_hbm, sketch_hbm, piv_hbm,
    b_ref, p_ref, g_ref, s_ref, r_out, x_out,
    slab_ref, sketch_ref, piv_ref,
    pk, pp, rc1, rc2, leadbuf,
    wpart, wa, wsum, wb, wfull,
    gpart, ga, gsum, gb, gfull,
    spart, sa, ssum, sb, sb9, sfull,
    sem_in, sem1, sem_lead, wa_sem, wb_sem, wc_sem, ga_sem, gb_sem, gc_sem, gd_sem,
    sa_sem, sb_sem, sb9_sem, sc_sem, sd_sem,
):
    r = lax.axis_index("row")
    c = lax.axis_index("col")
    z = lax.rem(lax.div(r, 2), NZ)
    q = lax.div(r, 16) * 2 + lax.rem(r, 2)
    width = slab_ref.shape[1]
    load_piv = pltpu.make_async_copy(piv_hbm, piv_ref, sem_in.at[0])
    load_slab = pltpu.make_async_copy(slab_hbm, slab_ref, sem_in.at[1])
    load_sketch = pltpu.make_async_copy(sketch_hbm, sketch_ref, sem_in.at[2])
    load_piv.start()
    load_slab.start()
    load_sketch.start()

    def yx_row(t):
        return lax.div(t, 2) * 16 + z * 2 + lax.rem(t, 2)

    def z_row(t):
        return lax.div(r, 16) * 16 + t * 2 + lax.rem(r, 2)

    barrier = pltpu.get_barrier_semaphore()
    for i in range(NYX):
        for j in range(NCOL):
            if i or j:
                pl.semaphore_signal(
                    barrier, inc=1, device_id_type=MESH,
                    device_id=(yx_row(lax.rem(q + i, NYX)), lax.rem(c + j, NCOL)),
                )
    for i in range(1, NZ):
        pl.semaphore_signal(
            barrier, inc=1, device_id=(z_row(lax.rem(z + i, NZ)), c), device_id_type=MESH
        )

    load_piv.wait()
    onehot = pivot_onehot(piv_ref[...], c * width, width)
    load_slab.wait()
    slab = slab_ref[...]
    pk[...] = select_dot(slab, onehot)
    load_sketch.wait()
    pl.semaphore_wait(barrier, NYX * NCOL - 1 + NZ - 1)

    core = c + 1 - 2 * lax.rem(c, 2)
    chip = lax.rem(c + 2, NCOL)
    first = remote(pk, rc1, sem1.at[0], sem1.at[1], (r, core))
    first.start()
    sketch = hdot(sketch_ref[...], slab)
    for b in range(4):
        spart[18 * b : 18 * b + 18] = sketch[:, 128 * b : 128 * b + 128].reshape(18, 8, 128)
    first.wait_recv()
    pp[...] = pk[...] + rc1[...]
    second = remote(pp, rc2, sem1.at[2], sem1.at[3], (r, chip))
    second.start()

    lead_copies = [
        remote(leadbuf.at[0], leadbuf.at[1], sem_lead.at[j - 1], sem_lead.at[3], (r, j)) for j in range(1, NCOL)
    ]
    leadbuf[0] = slab[:, :PANEL]

    @pl.when(c == 0)
    def _():
        for copy in lead_copies:
            copy.start()

    second.wait_recv()
    panel = pp[...] + rc2[...]
    p_ref[...] = panel

    lane = lax.broadcasted_iota(jnp.int32, (PANEL, PANEL), 1)
    l0, l1, l2, l3, l4 = gram_levels(panel)
    high, low = two_sum(l0, l1)
    high, low2 = two_sum(high, l2)
    low = (low + low2) + (l3 + l4)
    left = lane < 64
    wpart[0:16] = jnp.where(left, high, pltpu.roll(low, 64, 1)).reshape(16, 8, 128)
    wpart[16:32] = jnp.where(left, pltpu.roll(high, 64, 1), low).reshape(16, 8, 128)

    pending = [first, second]

    def exchange(me, count, row_of, src, dst, send_sems, recv_sems):
        copies = []
        for i in range(1, count):
            t = lax.rem(me + i, count)
            copy = remote(src(t), dst(me), send_sems.at[t], recv_sems.at[me], (row_of(t), c))
            copy.start()
            copies.append(copy)
        pending.extend(copies)

    def arrived(me, count, dst, send_sems, recv_sems):
        for i in range(1, count):
            t = lax.rem(me + i, count)
            remote(dst(t), dst(t), send_sems.at[t], recv_sems.at[t], (r, c)).wait_recv()

    yx = functools.partial(exchange, q, NYX, yx_row)
    zz = functools.partial(exchange, z, NZ, z_row)

    def two_float_total(buf):
        total = buf[0]
        err = jnp.zeros((8, 128), F32)
        for k in range(1, 8):
            total, e = two_sum(total, buf[k])
            err = err + e
        lane8 = lax.broadcasted_iota(jnp.int32, (8, 128), 1)
        return jnp.where(lane8 < 64, total, total + pltpu.roll(err, 64, 1))

    yx(lambda t: wpart.at[c * 8 + t], lambda m: wa.at[m], wa_sem.at[0], wa_sem.at[1])
    yx(
        lambda t: spart.at[pl.ds(9 * t, 9)], lambda m: sa.at[m], sa_sem.at[0], sa_sem.at[1]
    )
    wa[q] = wpart[c * 8 + q]
    sa[q] = spart[pl.ds(9 * q, 9)]

    @pl.when(c != 0)
    def _():
        remote(leadbuf.at[0], leadbuf.at[1], sem_lead.at[0], sem_lead.at[3], (r, c)).wait_recv()

    lead = jnp.where(c == 0, leadbuf[0], leadbuf[1])
    swapped = swapped_columns(slab, lead, onehot)
    b_ref[...] = swapped
    inner = hdot(panel, swapped, (0, 0))
    for b in range(4):
        gpart[16 * b : 16 * b + 16] = inner[:, 128 * b : 128 * b + 128].reshape(16, 8, 128)

    arrived(q, NYX, lambda t: wa.at[t], wa_sem.at[0], wa_sem.at[1])
    wsum[0] = two_float_total(wa)
    zz(lambda t: wsum.at[0], lambda m: wb.at[m], wb_sem.at[0], wb_sem.at[1])
    yx(lambda t: gpart.at[pl.ds(8 * t, 8)], lambda m: ga.at[m], ga_sem.at[0], ga_sem.at[1])
    wb[z] = wsum[0]
    ga[q] = gpart[pl.ds(8 * q, 8)]

    arrived(q, NYX, lambda t: sa.at[t], sa_sem.at[0], sa_sem.at[1])
    total = sa[0]
    for k in range(1, NYX):
        total = total + sa[k]
    ssum[...] = total
    zz(lambda t: ssum.at[t], lambda m: sb.at[m], sb_sem.at[0], sb_sem.at[1])
    zz(lambda t: ssum.at[8], lambda m: sb9.at[m], sb9_sem.at[0], sb9_sem.at[1])
    sb[z] = ssum[z]
    sb9[z] = ssum[8]

    arrived(z, NZ, lambda t: wb.at[t], wb_sem.at[0], wb_sem.at[1])
    mine = c * 8 + q
    wsum[1] = two_float_total(wb)
    for i in range(NYX):
        for j in range(NCOL):
            if i or j:
                t = lax.rem(q + i, NYX)
                d = lax.rem(c + j, NCOL)
                copy = remote(
                    wsum.at[1], wfull.at[mine], wc_sem.at[0, d * 8 + t], wc_sem.at[1, mine], (yx_row(t), d)
                )
                copy.start()
                pending.append(copy)
    wfull[mine] = wsum[1]

    arrived(q, NYX, lambda t: ga.at[t], ga_sem.at[0], ga_sem.at[1])
    total = ga[0]
    for k in range(1, NYX):
        total = total + ga[k]
    gsum[...] = total
    zz(lambda t: gsum.at[t], lambda m: gb.at[m], gb_sem.at[0], gb_sem.at[1])
    gb[z] = gsum[z]

    arrived(z, NZ, lambda t: sb.at[t], sb_sem.at[0], sb_sem.at[1])
    arrived(z, NZ, lambda t: sb9.at[t], sb9_sem.at[0], sb9_sem.at[1])
    total, ninth = sb[0], sb9[0]
    for k in range(1, NZ):
        total = total + sb[k]
        ninth = ninth + sb9[k]
    sfull[q * 9 + z] = total
    sfull[q * 9 + 8] = ninth
    zz(
        lambda t: sfull.at[q * 9 + z], lambda m: sfull.at[q * 9 + m], sc_sem.at[0], sc_sem.at[1]
    )

    for i in range(NYX):
        for j in range(NCOL):
            if i or j:
                o = lax.rem(c + j, NCOL) * 8 + lax.rem(q + i, NYX)
                remote(wfull.at[o], wfull.at[o], wc_sem.at[0, o], wc_sem.at[1, o], (r, c)).wait_recv()
    first_half = wfull[0:16].reshape(PANEL, PANEL)
    second_half = wfull[16:32].reshape(PANEL, PANEL)
    high = jnp.where(left, first_half, pltpu.roll(second_half, 64, 1))
    low = jnp.where(left, pltpu.roll(first_half, 64, 1), second_half)

    arrived(z, NZ, lambda t: gb.at[t], gb_sem.at[0], gb_sem.at[1])
    total = gb[0]
    for k in range(1, NZ):
        total = total + gb[k]
    gfull[q * 8 + z] = total
    zz(
        lambda t: gfull.at[q * 8 + z], lambda m: gfull.at[q * 8 + m], gc_sem.at[0], gc_sem.at[1]
    )
    arrived(z, NZ, lambda t: sfull.at[q * 9 + t], sc_sem.at[0], sc_sem.at[1])
    yx(
        lambda t: sfull.at[pl.ds(q * 9, 9)], lambda m: sfull.at[pl.ds(m * 9, 9)], sd_sem.at[0], sd_sem.at[1]
    )

    eliminate(high, r_out.at[0], x_out.at[0])
    r_one = r_out[0]
    x_one = x_out[0]

    arrived(z, NZ, lambda t: gfull.at[q * 8 + t], gc_sem.at[0], gc_sem.at[1])
    yx(
        lambda t: gfull.at[pl.ds(q * 8, 8)], lambda m: gfull.at[pl.ds(m * 8, 8)], gd_sem.at[0], gd_sem.at[1]
    )

    rowi = lax.broadcasted_iota(jnp.int32, (PANEL, PANEL), 0)
    eye = jnp.where(rowi == lane, 1.0, 0.0).astype(F32)
    l0, l1, l2, l3, l4 = gram_levels(r_one)
    d, e1 = two_sum(high, -l0)
    d, e2 = two_sum(d, -l1)
    delta = (d - l2) + (((e1 + e2) + low) - (l3 + l4))
    gram_two = eye + hdot(hdot(x_one, delta), x_one, (1, 1))
    eliminate(gram_two, r_out.at[1], x_out.at[1])

    arrived(q, NYX, lambda t: sfull.at[pl.ds(t * 9, 9)], sd_sem.at[0], sd_sem.at[1])
    for b in range(4):
        s_ref[0, :, 128 * b : 128 * b + 128] = sfull[18 * b : 18 * b + 18].reshape(144, 128)
    arrived(q, NYX, lambda t: gfull.at[pl.ds(t * 8, 8)], gd_sem.at[0], gd_sem.at[1])
    for b in range(4):
        g_ref[:, 128 * b : 128 * b + 128] = gfull[16 * b : 16 * b + 16].reshape(128, 128)

    for copy in pending:
        copy.wait_send()

    @pl.when(c == 0)
    def _():
        for copy in lead_copies:
            copy.wait_send()


def tree_sum(terms):
    terms = list(terms)
    while len(terms) > 1:
        pairs = [terms[i] + terms[i + 1] for i in range(0, len(terms) - 1, 2)]
        terms = pairs + terms[len(pairs) * 2 :]
    return terms[0]


def spread(v):
    return jnp.broadcast_to(v, (8, 128))


def block_factor(v, first, sub, lane):
    columns = [spread(v[:, first + j : first + j + 1]) for j in range(8)]
    a = {(i, j): spread(columns[i][j : j + 1, :]) for j in range(8) for i in range(j + 1)}
    m = [[None] * 8 for _ in range(8)]
    for i in range(8):
        inv = lax.rsqrt(a[i, i])
        l = {j: a[i, j] * inv for j in range(i + 1, 8)}
        for j in range(i + 1, 8):
            for k in range(j, 8):
                a[j, k] = a[j, k] - l[j] * l[k]
        for j in range(i):
            m[i][j] = m[i][j] * inv
        m[i][i] = inv
        for k in range(i + 1, 8):
            for j in range(i + 1):
                t = l[k] * m[i][j]
                m[k][j] = -t if m[k][j] is None else m[k][j] - t
    terms = []
    inverse = jnp.zeros((8, 128), F32)
    for j in range(8):
        column = m[7][j]
        for k in range(6, j - 1, -1):
            column = jnp.where(sub <= k, m[k][j], column)
        if j > 0:
            column = jnp.where(sub < j, 0.0, column)
        terms.append(column * spread(v[j : j + 1, :]))
        inverse = jnp.where(lane == first + j, column, inverse)
    solved = tree_sum(terms)
    inside = (lane >= first) & (lane < first + 8)
    return solved, jnp.where(inside, inverse, solved), m


def eliminate(w, r_ref, x_ref):
    sub = lax.broadcasted_iota(jnp.int32, (8, 128), 0)
    lane = lax.broadcasted_iota(jnp.int32, (8, 128), 1)
    count = PANEL // 8
    blocks = [w[8 * b : 8 * b + 8, :] for b in range(count)]
    for b in range(count):
        first = 8 * b
        solved, both, m = block_factor(blocks[b], first, sub, lane)
        upper = jnp.where(lane >= first + sub, solved, 0.0)
        r_ref[first : first + 8, :] = upper
        x_ref[first : first + 8, :] = jnp.where(lane < first + 8, both, 0.0)
        if b == count - 1:
            break
        inside = (lane >= first) & (lane < first + 8)
        rows = blocks[b + 1]
        columns = [spread(rows[:, first + j : first + j + 1]) for j in range(8)]
        updates = []
        for p in range(8):
            coef = tree_sum([m[p][j] * columns[j] for j in range(p + 1)])
            updates.append(coef * spread(both[p : p + 1, :]))
        blocks[b + 1] = jnp.where(inside, 0.0, rows) - tree_sum(updates)
        if b + 2 < count:
            update = hdot(upper, both, (0, 0))
            for k in range(b + 2, count):
                blocks[k] = jnp.where(inside, 0.0, blocks[k]) - update[8 * k : 8 * k + 8, :]


def update_kernel(
    b_ref, p_ref, g_ref, s_in, r_ref, x_ref,
    s_hbm, q_hbm, e_hbm, first_hbm, out_hbm,
    qbuf, ebuf, fbuf, obuf, sem,
):
    lead_block = lax.axis_index("col") == 0
    copies = [pltpu.make_async_copy(s_in, s_hbm, sem.at[0])]
    copies[0].start()
    scale = 1.0 / 128.0

    def store(k, src, dst):
        copy = pltpu.make_async_copy(src, dst, sem.at[k])
        copy.start()
        copies.append(copy)

    r_one = r_ref[0]
    fbuf[...] = r_one * scale
    store(1, fbuf, first_hbm.at[0])
    inverse = hdot(x_ref[1], x_ref[0])
    basis = hdot(p_ref[...], inverse, (1, 1))
    qbuf[...] = basis * 128.0
    store(2, qbuf, q_hbm.at[0])
    r_factor = hdot(r_ref[1], r_one)
    for k in range(4):
        cols = slice(128 * k, 128 * k + 128)
        projected = hdot(inverse, g_ref[:, cols])
        rest = b_ref[:, cols] - hdot(basis, projected)
        if k == 0:
            projected = jnp.where(lead_block, r_factor, projected)
            rest = jnp.where(lead_block, 0.0, rest)
        ebuf[:, cols] = projected * scale
        obuf[:, cols] = rest
        store(3 + k, obuf.at[:, cols], out_hbm.at[:, cols])
    store(7, ebuf, e_hbm.at[0])
    for copy in copies:
        copy.wait()


def shards(matrix_slab, sketch_matrix, pivots):
    rows, width = matrix_slab.shape
    sk = sketch_matrix.shape[0]
    dma = pltpu.SemaphoreType.DMA
    hbm = pl.BlockSpec(memory_space=pltpu.HBM)
    tile = lambda *lead: pltpu.VMEM(lead + (8, 128), F32)
    flat = lambda *shape: jax.ShapeDtypeStruct(shape, F32)
    swapped, panel, inner, sketches, factors, inverses = pl.pallas_call(
        reduce_kernel,
        out_shape=(
            flat(rows, width), flat(rows, PANEL), flat(PANEL, width), flat(1, sk, width),
            flat(2, PANEL, PANEL), flat(2, PANEL, PANEL),
        ),
        in_specs=[hbm] * 3,
        out_specs=(VMEM_SPEC,) * 6,
        scratch_shapes=[
            pltpu.VMEM((rows, width), F32), pltpu.VMEM((sk, rows), F32), pltpu.VMEM((1, PANEL), jnp.int32),
            pltpu.VMEM((rows, PANEL), F32), pltpu.VMEM((rows, PANEL), F32),
            pltpu.VMEM((rows, PANEL), F32), pltpu.VMEM((rows, PANEL), F32),
            pltpu.VMEM((2, rows, PANEL), F32),
            tile(32), tile(8), tile(2), tile(8), tile(32),
            tile(64), tile(8, 8), tile(8), tile(8), tile(64),
            tile(72), tile(8, 9), tile(9), tile(8), tile(8), tile(72),
            dma((3,)), dma((4,)), dma((4,)), dma((2, 8)), dma((2, 8)), dma((2, 32)),
            dma((2, 8)), dma((2, 8)), dma((2, 8)), dma((2, 8)),
            dma((2, 8)), dma((2, 8)), dma((2, 8)), dma((2, 8)), dma((2, 8)),
        ],
        compiler_params=pltpu.CompilerParams(
            collective_id=0, has_side_effects=True, vmem_limit_bytes=32 * 1024 * 1024
        ),
        name="reduce",
    )(matrix_slab, sketch_matrix, pivots)
    return pl.pallas_call(
        update_kernel,
        out_shape=(
            flat(1, sk, width), flat(1, rows, PANEL), flat(1, PANEL, width),
            flat(1, PANEL, PANEL), flat(rows, width),
        ),
        in_specs=[VMEM_SPEC] * 3 + [pl.BlockSpec(memory_space=pl.ANY)] + [VMEM_SPEC] * 2,
        out_specs=(hbm,) * 5,
        scratch_shapes=[
            pltpu.VMEM((rows, PANEL), F32), pltpu.VMEM((PANEL, width), F32),
            pltpu.VMEM((PANEL, PANEL), F32), pltpu.VMEM((rows, width), F32), dma((8,)),
        ],
        compiler_params=pltpu.CompilerParams(vmem_limit_bytes=32 * 1024 * 1024),
        name="update",
    )(swapped, panel, inner, sketches, factors, inverses)


def solution(mesh):
    in_specs = (P("row", "col"), P(None, "row"), P())
    out_specs = (
        P(None, None, "col"),
        P(None, "row", None),
        P(None, None, "col"),
        P(),
        P("row", "col"),
    )
    return jax.shard_map(shards, mesh=mesh, in_specs=in_specs, out_specs=out_specs, check_vma=False)
```

```python
import functools
import math

import jax
import jax.numpy as jnp
from jax import lax
from jax.experimental import pallas as pl
from jax.experimental.pallas import tpu as pltpu
from jax.sharding import PartitionSpec as P

PANEL = 128
NY = 4
NZX = 16
NCOL = 4
MESH = pl.DeviceIdType.MESH
F32 = jnp.float32
BF16 = jnp.bfloat16
VMEM_SPEC = pl.BlockSpec(memory_space=pltpu.VMEM)


def hdot(left, right, contract=(1, 0)):
    return lax.dot_general(
        left,
        right,
        (((contract[0],), (contract[1],)), ((), ())),
        precision=lax.Precision.HIGHEST,
        preferred_element_type=F32,
    )


def bdot(left, right, contract=(1, 0)):
    return lax.dot_general(
        left, right, (((contract[0],), (contract[1],)), ((), ())), preferred_element_type=F32
    )


def select_dot(values, onehot, contract=(1, 0)):
    high = values.astype(BF16)
    rest = values - high.astype(F32)
    mid = rest.astype(BF16)
    low = (rest - mid.astype(F32)).astype(BF16)
    return (bdot(high, onehot, contract) + bdot(mid, onehot, contract)) + bdot(low, onehot, contract)


def two_sum(a, b):
    s = a + b
    t = s - a
    return s, (a - (s - t)) + (b - t)


def gram_levels(x):
    n = x.shape[1]
    sigma = jnp.max(jnp.abs(x), axis=0, keepdims=True) * 131072.0
    parts = []
    rest = x
    for _ in range(4):
        part = (rest + sigma) - sigma
        rest = rest - part
        parts.append(part.astype(BF16))
        sigma = sigma * (1.0 / 128.0)
    cat = jnp.concatenate(parts, axis=1)
    full = bdot(cat, cat, (0, 0))
    block = lambda i, j: full[i * n : (i + 1) * n, j * n : (j + 1) * n]
    return (
        block(0, 0),
        block(0, 1) + block(1, 0),
        (block(0, 2) + block(2, 0)) + block(1, 1),
        (block(0, 3) + block(3, 0)) + (block(1, 2) + block(2, 1)),
        (block(1, 3) + block(3, 1)) + block(2, 2),
    )


def pivot_onehot(piv, col_first, width):
    lanes = lax.broadcasted_iota(jnp.int32, (width, PANEL), 0) + col_first
    return jnp.where(lanes == piv, 1.0, 0.0).astype(BF16)


def swapped_columns(slab, lead, onehot):
    picked = bdot(jnp.ones((8, PANEL), BF16), onehot, (1, 1))[0:1, :]
    return jnp.where(picked > 0.5, select_dot(lead, onehot, (1, 1)), slab)


def remote(src, dst, send, recv, device):
    return pltpu.make_async_remote_copy(
        src_ref=src, dst_ref=dst, send_sem=send, recv_sem=recv, device_id=device, device_id_type=MESH
    )


def reduce_kernel(
    slab_hbm, sketch_hbm, piv_hbm,
    b_ref, p_ref, g_ref, s_ref, r_out, x_out,
    slab_ref, sketch_ref, piv_ref,
    pk, pp, rc1, rc2, leadbuf,
    wpart, wa, wsum, wb, wtot, wfull,
    gpart, ga, gsum, gb, gfull,
    spart, sa, ssum, sb, sbx, sfull,
    sem_in, sem1, sem_lead, wa_sem, wb_sem, wc_sem, ga_sem, gb_sem, gc_sem, gd_sem,
    sa_sem, sb_sem, sbx_sem, sc_sem, sd_sem,
):
    r = lax.axis_index("row")
    c = lax.axis_index("col")
    y = lax.div(r, NZX)
    w = lax.rem(r, NZX)
    width = slab_ref.shape[1]
    load_piv = pltpu.make_async_copy(piv_hbm, piv_ref, sem_in.at[0])
    load_slab = pltpu.make_async_copy(slab_hbm, slab_ref, sem_in.at[1])
    load_sketch = pltpu.make_async_copy(sketch_hbm, sketch_ref, sem_in.at[2])
    load_piv.start()
    load_slab.start()
    load_sketch.start()

    y_peers = [(lax.rem(y + i, NY), i) for i in range(1, NY)]
    zx_peers = [lax.rem(w + i, NZX) for i in range(1, NZX)]
    yc_peers = [
        (lax.rem(y + i, NY), lax.rem(c + j, NCOL)) for i in range(NY) for j in range(NCOL) if i or j
    ]

    barrier = pltpu.get_barrier_semaphore()
    for t in zx_peers:
        pl.semaphore_signal(barrier, inc=1, device_id=(y * NZX + t, c), device_id_type=MESH)
    for t, d in yc_peers:
        pl.semaphore_signal(barrier, inc=1, device_id=(t * NZX + w, d), device_id_type=MESH)

    load_piv.wait()
    onehot = pivot_onehot(piv_ref[...], c * width, width)
    load_slab.wait()
    slab = slab_ref[...]
    pk[...] = select_dot(slab, onehot)
    load_sketch.wait()
    sketch = hdot(sketch_ref[...], slab)
    for b in range(4):
        spart[b] = sketch[:, 128 * b : 128 * b + 128]
    leadbuf[0] = slab[:, :PANEL]
    pl.semaphore_wait(barrier, NZX - 1 + NY * NCOL - 1)

    pending = []

    def send(src, dst, send_sem, recv_sem, device):
        copy = remote(src, dst, send_sem, recv_sem, device)
        copy.start()
        pending.append(copy)

    def to_y(src, dst, sems):
        for t, _ in y_peers:
            send(src(t), dst(y), sems.at[0, t], sems.at[1, y], (t * NZX + w, c))

    def to_zx(src, dst, sems):
        for t in zx_peers:
            send(src(t), dst(w), sems.at[0, t], sems.at[1, w], (y * NZX + t, c))

    def from_y(dst, sems):
        for t, _ in y_peers:
            remote(dst(t), dst(t), sems.at[0, t], sems.at[1, t], (r, c)).wait_recv()

    def from_zx(dst, sems):
        for t in zx_peers:
            remote(dst(t), dst(t), sems.at[0, t], sems.at[1, t], (r, c)).wait_recv()

    def total_of(buf, count):
        return tree_sum([buf[k] for k in range(count)])

    def two_float_total(buf, count):
        total = buf[0]
        err = jnp.zeros_like(total)
        for k in range(1, count):
            total, e = two_sum(total, buf[k])
            err = err + e
        lane16 = lax.broadcasted_iota(jnp.int32, total.shape, 1)
        return jnp.where(lane16 < 64, total, total + pltpu.roll(err, 64, 1))

    core = c + 1 - 2 * lax.rem(c, 2)
    chip = lax.rem(c + 2, NCOL)
    first = remote(pk, rc1, sem1.at[0], sem1.at[1], (r, core))
    first.start()
    to_y(lambda t: spart.at[t], lambda m: sa.at[m], sa_sem)
    sa[y] = spart[y]
    first.wait_recv()
    pp[...] = pk[...] + rc1[...]
    second = remote(pp, rc2, sem1.at[2], sem1.at[3], (r, chip))
    second.start()
    lead_copies = [
        remote(leadbuf.at[0], leadbuf.at[1], sem_lead.at[j - 1], sem_lead.at[3], (r, j)) for j in range(1, NCOL)
    ]

    @pl.when(c == 0)
    def _():
        for copy in lead_copies:
            copy.start()

    second.wait_recv()
    pending.extend([first, second])
    panel = pp[...] + rc2[...]

    lane = lax.broadcasted_iota(jnp.int32, (PANEL, PANEL), 1)
    left = lane < 64
    l0, l1, l2, l3, l4 = gram_levels(panel)
    high, low = two_sum(l0, l1)
    high, low2 = two_sum(high, l2)
    low = (low + low2) + (l3 + l4)
    wpart[0:8] = jnp.where(left, high, pltpu.roll(low, 64, 1)).reshape(8, 16, 128)
    wpart[8:16] = jnp.where(left, pltpu.roll(high, 64, 1), low).reshape(8, 16, 128)
    to_y(lambda t: wpart.at[c * 4 + t], lambda m: wa.at[m], wa_sem)
    wa[y] = wpart[c * 4 + y]
    p_ref[...] = panel

    from_y(lambda t: sa.at[t], sa_sem)
    ssum[...] = total_of(sa, NY)
    to_zx(lambda t: ssum.at[pl.ds(8 * t, 8)], lambda m: sb.at[m], sb_sem)
    to_zx(lambda t: ssum.at[pl.ds(128, 16)], lambda m: sbx.at[m], sbx_sem)
    sb[w] = ssum[pl.ds(pl.multiple_of(8 * w, 8), 8)]
    sbx[w] = ssum[pl.ds(128, 16)]

    @pl.when(c != 0)
    def _():
        remote(leadbuf.at[0], leadbuf.at[1], sem_lead.at[0], sem_lead.at[3], (r, c)).wait_recv()

    lead = jnp.where(c == 0, leadbuf[0], leadbuf[1])
    swapped = swapped_columns(slab, lead, onehot)
    b_ref[...] = swapped
    inner = hdot(panel, swapped, (0, 0))
    for b in range(4):
        gpart[b] = inner[:, 128 * b : 128 * b + 128]
    to_y(lambda t: gpart.at[t], lambda m: ga.at[m], ga_sem)
    ga[y] = gpart[y]

    from_y(lambda t: wa.at[t], wa_sem)
    wsum[...] = two_float_total(wa, NY)
    to_zx(lambda t: wsum, lambda m: wb.at[m], wb_sem)
    wb[w] = wsum[...]

    from_zx(lambda t: sb.at[t], sb_sem)
    from_zx(lambda t: sbx.at[t], sbx_sem)
    tile = lambda t: pl.ds(pl.multiple_of(8 * t, 8), 8)
    sfull[y, tile(w)] = total_of(sb, NZX)
    sfull[y, pl.ds(128, 16)] = total_of(sbx, NZX)
    to_zx(lambda t: sfull.at[y, tile(w)], lambda m: sfull.at[y, tile(m)], sc_sem)

    from_y(lambda t: ga.at[t], ga_sem)
    gsum[...] = total_of(ga, NY)
    to_zx(lambda t: gsum.at[tile(t)], lambda m: gb.at[m], gb_sem)
    gb[w] = gsum[tile(w)]

    from_zx(lambda t: wb.at[t], wb_sem)
    wtot[...] = two_float_total(wb, NZX)
    mine = c * 4 + y
    for t, d in yc_peers:
        send(wtot, wfull.at[mine], wc_sem.at[0, d * 4 + t], wc_sem.at[1, mine], (t * NZX + w, d))
    wfull[mine] = wtot[...]

    from_zx(lambda t: sfull.at[y, tile(t)], sc_sem)
    to_y(lambda t: sfull.at[y], lambda m: sfull.at[m], sd_sem)

    from_zx(lambda t: gb.at[t], gb_sem)
    gfull[y, tile(w)] = total_of(gb, NZX)
    to_zx(lambda t: gfull.at[y, tile(w)], lambda m: gfull.at[y, tile(m)], gc_sem)

    for t, d in yc_peers:
        o = d * 4 + t
        remote(wfull.at[o], wfull.at[o], wc_sem.at[0, o], wc_sem.at[1, o], (r, c)).wait_recv()
    first_half = wfull[0:8].reshape(PANEL, PANEL)
    second_half = wfull[8:16].reshape(PANEL, PANEL)
    high = jnp.where(left, first_half, pltpu.roll(second_half, 64, 1))
    low = jnp.where(left, pltpu.roll(first_half, 64, 1), second_half)

    eliminate(high, r_out.at[0], x_out.at[0])
    r_one = r_out[0]
    x_one = x_out[0]

    from_zx(lambda t: gfull.at[y, tile(t)], gc_sem)
    to_y(lambda t: gfull.at[y], lambda m: gfull.at[m], gd_sem)

    rowi = lax.broadcasted_iota(jnp.int32, (PANEL, PANEL), 0)
    eye = jnp.where(rowi == lane, 1.0, 0.0).astype(F32)
    l0, l1, l2, l3, l4 = gram_levels(r_one)
    d, e1 = two_sum(high, -l0)
    d, e2 = two_sum(d, -l1)
    delta = (d - l2) + (((e1 + e2) + low) - (l3 + l4))
    gram_two = eye + hdot(hdot(x_one, delta), x_one, (1, 1))
    from_y(lambda t: sfull.at[t], sd_sem)
    for b in range(4):
        s_ref[0, :, 128 * b : 128 * b + 128] = sfull[b]
    eliminate(gram_two, r_out.at[1], x_out.at[1])

    from_y(lambda t: gfull.at[t], gd_sem)
    for b in range(4):
        g_ref[:, 128 * b : 128 * b + 128] = gfull[b]

    for copy in pending:
        copy.wait_send()

    @pl.when(c == 0)
    def _():
        for copy in lead_copies:
            copy.wait_send()


def tree_sum(terms):
    terms = list(terms)
    while len(terms) > 1:
        pairs = [terms[i] + terms[i + 1] for i in range(0, len(terms) - 1, 2)]
        terms = pairs + terms[len(pairs) * 2 :]
    return terms[0]


def spread(v):
    return jnp.broadcast_to(v, (8, 128))


def block_factor(v, first, sub, lane):
    columns = [spread(v[:, first + j : first + j + 1]) for j in range(8)]
    a = {(i, j): spread(columns[i][j : j + 1, :]) for j in range(8) for i in range(j + 1)}
    m = [[None] * 8 for _ in range(8)]
    for i in range(8):
        inv = lax.rsqrt(a[i, i])
        l = {j: a[i, j] * inv for j in range(i + 1, 8)}
        for j in range(i + 1, 8):
            for k in range(j, 8):
                a[j, k] = a[j, k] - l[j] * l[k]
        for j in range(i):
            m[i][j] = m[i][j] * inv
        m[i][i] = inv
        for k in range(i + 1, 8):
            for j in range(i + 1):
                t = l[k] * m[i][j]
                m[k][j] = -t if m[k][j] is None else m[k][j] - t
    terms = []
    inverse = jnp.zeros((8, 128), F32)
    for j in range(8):
        column = m[7][j]
        for k in range(6, j - 1, -1):
            column = jnp.where(sub <= k, m[k][j], column)
        if j > 0:
            column = jnp.where(sub < j, 0.0, column)
        terms.append(column * spread(v[j : j + 1, :]))
        inverse = jnp.where(lane == first + j, column, inverse)
    solved = tree_sum(terms)
    inside = (lane >= first) & (lane < first + 8)
    return solved, jnp.where(inside, inverse, solved), m


def eliminate(w, r_ref, x_ref):
    sub = lax.broadcasted_iota(jnp.int32, (8, 128), 0)
    lane = lax.broadcasted_iota(jnp.int32, (8, 128), 1)
    count = PANEL // 8
    blocks = [w[8 * b : 8 * b + 8, :] for b in range(count)]
    for b in range(count):
        first = 8 * b
        solved, both, m = block_factor(blocks[b], first, sub, lane)
        upper = jnp.where(lane >= first + sub, solved, 0.0)
        r_ref[first : first + 8, :] = upper
        x_ref[first : first + 8, :] = jnp.where(lane < first + 8, both, 0.0)
        if b == count - 1:
            break
        inside = (lane >= first) & (lane < first + 8)
        rows = blocks[b + 1]
        columns = [spread(rows[:, first + j : first + j + 1]) for j in range(8)]
        updates = []
        for p in range(8):
            coef = tree_sum([m[p][j] * columns[j] for j in range(p + 1)])
            updates.append(coef * spread(both[p : p + 1, :]))
        blocks[b + 1] = jnp.where(inside, 0.0, rows) - tree_sum(updates)
        if b + 2 < count:
            update = hdot(upper, both, (0, 0))
            for k in range(b + 2, count):
                blocks[k] = jnp.where(inside, 0.0, blocks[k]) - update[8 * k : 8 * k + 8, :]


def update_kernel(
    b_ref, p_ref, g_ref, s_in, r_ref, x_ref,
    s_hbm, q_hbm, e_hbm, first_hbm, out_hbm,
    qbuf, ebuf, fbuf, obuf, sem,
):
    lead_block = lax.axis_index("col") == 0
    copies = [pltpu.make_async_copy(s_in, s_hbm, sem.at[0])]
    copies[0].start()
    scale = 1.0 / 128.0

    def store(k, src, dst):
        copy = pltpu.make_async_copy(src, dst, sem.at[k])
        copy.start()
        copies.append(copy)

    r_one = r_ref[0]
    fbuf[...] = r_one * scale
    store(1, fbuf, first_hbm.at[0])
    inverse = hdot(x_ref[1], x_ref[0])
    basis = hdot(p_ref[...], inverse, (1, 1))
    qbuf[...] = basis * 128.0
    store(2, qbuf, q_hbm.at[0])
    r_factor = hdot(r_ref[1], r_one)
    for k in range(4):
        cols = slice(128 * k, 128 * k + 128)
        projected = hdot(inverse, g_ref[:, cols])
        rest = b_ref[:, cols] - hdot(basis, projected)
        if k == 0:
            projected = jnp.where(lead_block, r_factor, projected)
            rest = jnp.where(lead_block, 0.0, rest)
        ebuf[:, cols] = projected * scale
        obuf[:, cols] = rest
        store(3 + k, obuf.at[:, cols], out_hbm.at[:, cols])
    store(7, ebuf, e_hbm.at[0])
    for copy in copies:
        copy.wait()


def shards(matrix_slab, sketch_matrix, pivots):
    rows, width = matrix_slab.shape
    sk = sketch_matrix.shape[0]
    dma = pltpu.SemaphoreType.DMA
    hbm = pl.BlockSpec(memory_space=pltpu.HBM)
    tile = lambda *lead: pltpu.VMEM(lead + (8, 128), F32)
    block = lambda *lead: pltpu.VMEM(lead + (16, 128), F32)
    square = lambda *lead: pltpu.VMEM(lead + (PANEL, 128), F32)
    tall = lambda *lead: pltpu.VMEM(lead + (sk, 128), F32)
    flat = lambda *shape: jax.ShapeDtypeStruct(shape, F32)
    swapped, panel, inner, sketches, factors, inverses = pl.pallas_call(
        reduce_kernel,
        out_shape=(
            flat(rows, width), flat(rows, PANEL), flat(PANEL, width), flat(1, sk, width),
            flat(2, PANEL, PANEL), flat(2, PANEL, PANEL),
        ),
        in_specs=[hbm] * 3,
        out_specs=(VMEM_SPEC,) * 6,
        scratch_shapes=[
            pltpu.VMEM((rows, width), F32), pltpu.VMEM((sk, rows), F32), pltpu.VMEM((1, PANEL), jnp.int32),
            pltpu.VMEM((rows, PANEL), F32), pltpu.VMEM((rows, PANEL), F32),
            pltpu.VMEM((rows, PANEL), F32), pltpu.VMEM((rows, PANEL), F32),
            pltpu.VMEM((2, rows, PANEL), F32),
            block(16), block(NY), block(), block(NZX), block(), block(16),
            square(NY), square(NY), square(), tile(NZX), square(NY),
            tall(NY), tall(NY), tall(), tile(NZX), block(NZX), tall(NY),
            dma((3,)), dma((4,)), dma((4,)), dma((2, NY)), dma((2, NZX)), dma((2, 16)),
            dma((2, NY)), dma((2, NZX)), dma((2, NZX)), dma((2, NY)),
            dma((2, NY)), dma((2, NZX)), dma((2, NZX)), dma((2, NZX)), dma((2, NY)),
        ],
        compiler_params=pltpu.CompilerParams(
            collective_id=0, has_side_effects=True, vmem_limit_bytes=32 * 1024 * 1024
        ),
        name="reduce",
    )(matrix_slab, sketch_matrix, pivots)
    return pl.pallas_call(
        update_kernel,
        out_shape=(
            flat(1, sk, width), flat(1, rows, PANEL), flat(1, PANEL, width),
            flat(1, PANEL, PANEL), flat(rows, width),
        ),
        in_specs=[VMEM_SPEC] * 3 + [pl.BlockSpec(memory_space=pl.ANY)] + [VMEM_SPEC] * 2,
        out_specs=(hbm,) * 5,
        scratch_shapes=[
            pltpu.VMEM((rows, PANEL), F32), pltpu.VMEM((PANEL, width), F32),
            pltpu.VMEM((PANEL, PANEL), F32), pltpu.VMEM((rows, width), F32), dma((8,)),
        ],
        compiler_params=pltpu.CompilerParams(vmem_limit_bytes=32 * 1024 * 1024),
        name="update",
    )(swapped, panel, inner, sketches, factors, inverses)


def solution(mesh):
    in_specs = (P("row", "col"), P(None, "row"), P())
    out_specs = (
        P(None, None, "col"),
        P(None, "row", None),
        P(None, None, "col"),
        P(),
        P("row", "col"),
    )
    return jax.shard_map(shards, mesh=mesh, in_specs=in_specs, out_specs=out_specs, check_vma=False)
```

```python
import functools
import math

import jax
import jax.numpy as jnp
from jax import lax
from jax.experimental import pallas as pl
from jax.experimental.pallas import tpu as pltpu
from jax.sharding import PartitionSpec as P

PANEL = 128
VMEM_REDUCE = 54400 * 1024
VMEM_UPDATE = 54400 * 1024
NY = 4
NZX = 16
NCOL = 4
MESH = pl.DeviceIdType.MESH
F32 = jnp.float32
BF16 = jnp.bfloat16
VMEM_SPEC = pl.BlockSpec(memory_space=pltpu.VMEM)


def hdot(left, right, contract=(1, 0)):
    return lax.dot_general(
        left,
        right,
        (((contract[0],), (contract[1],)), ((), ())),
        precision=lax.Precision.HIGHEST,
        preferred_element_type=F32,
    )


def bdot(left, right, contract=(1, 0)):
    return lax.dot_general(
        left, right, (((contract[0],), (contract[1],)), ((), ())), preferred_element_type=F32
    )


def select_dot(values, onehot, contract=(1, 0)):
    high = values.astype(BF16)
    rest = values - high.astype(F32)
    mid = rest.astype(BF16)
    low = (rest - mid.astype(F32)).astype(BF16)
    return (bdot(high, onehot, contract) + bdot(mid, onehot, contract)) + bdot(low, onehot, contract)


def two_sum(a, b):
    s = a + b
    t = s - a
    return s, (a - (s - t)) + (b - t)


def gram_levels(x):
    n = x.shape[1]
    sigma = jnp.max(jnp.abs(x), axis=0, keepdims=True) * 131072.0
    parts = []
    rest = x
    for _ in range(4):
        part = (rest + sigma) - sigma
        rest = rest - part
        parts.append(part.astype(BF16))
        sigma = sigma * (1.0 / 128.0)
    cat = jnp.concatenate(parts, axis=1)
    full = bdot(cat, cat, (0, 0))
    block = lambda i, j: full[i * n : (i + 1) * n, j * n : (j + 1) * n]
    return (
        block(0, 0),
        block(0, 1) + block(1, 0),
        (block(0, 2) + block(2, 0)) + block(1, 1),
        (block(0, 3) + block(3, 0)) + (block(1, 2) + block(2, 1)),
        (block(1, 3) + block(3, 1)) + block(2, 2),
    )


def pivot_onehot(piv, col_first, width):
    lanes = lax.broadcasted_iota(jnp.int32, (width, PANEL), 0) + col_first
    return jnp.where(lanes == piv, 1.0, 0.0).astype(BF16)


def swapped_columns(slab, lead, onehot):
    picked = bdot(jnp.ones((8, PANEL), BF16), onehot, (1, 1))[0:1, :]
    return jnp.where(picked > 0.5, select_dot(lead, onehot, (1, 1)), slab)


def remote(src, dst, send, recv, device):
    return pltpu.make_async_remote_copy(
        src_ref=src, dst_ref=dst, send_sem=send, recv_sem=recv, device_id=device, device_id_type=MESH
    )


def reduce_kernel(
    slab_hbm, sketch_hbm, piv_hbm,
    b_hbm, p_ref, gfull, s_hbm, r_out, x_out,
    slab_ref, b_ref, sketch_ref, piv_ref,
    pk, pp, rc1, rc2, leadbuf,
    wpart, wa, wsum, wb, wtot, wfull,
    gpart, ga, gsum, gb,
    spart, sa, ssum, sb, sbx, sfull,
    sem_in, sem_out, sem1, sem_lead, wa_sem, wb_sem, wc_sem, ga_sem, gb_sem, gc_sem, gd_sem,
    sa_sem, sb_sem, sbx_sem, sc_sem, sd_sem,
):
    r = lax.axis_index("row")
    c = lax.axis_index("col")
    y = lax.div(r, NZX)
    w = lax.rem(r, NZX)
    width = slab_ref.shape[1]
    load_piv = pltpu.make_async_copy(piv_hbm, piv_ref, sem_in.at[0])
    load_slab = pltpu.make_async_copy(slab_hbm, slab_ref, sem_in.at[1])
    load_sketch = pltpu.make_async_copy(sketch_hbm, sketch_ref, sem_in.at[2])
    load_piv.start()
    load_slab.start()
    load_sketch.start()

    y_peers = [(lax.rem(y + i, NY), i) for i in range(1, NY)]
    zx_peers = [lax.rem(w + i, NZX) for i in range(1, NZX)]
    yc_peers = [
        (lax.rem(y + i, NY), lax.rem(c + j, NCOL)) for i in range(NY) for j in range(NCOL) if i or j
    ]

    barrier = pltpu.get_barrier_semaphore()
    for t in zx_peers:
        pl.semaphore_signal(barrier, inc=1, device_id=(y * NZX + t, c), device_id_type=MESH)
    for t, d in yc_peers:
        pl.semaphore_signal(barrier, inc=1, device_id=(t * NZX + w, d), device_id_type=MESH)

    load_piv.wait()
    onehot = pivot_onehot(piv_ref[...], c * width, width)
    load_slab.wait()
    slab = slab_ref[...]
    pk[...] = select_dot(slab, onehot)
    load_sketch.wait()
    sketch = hdot(sketch_ref[...], slab)
    for b in range(4):
        spart[b] = sketch[:, 128 * b : 128 * b + 128]
    leadbuf[0] = slab[:, :PANEL]
    pl.semaphore_wait(barrier, NZX - 1 + NY * NCOL - 1)

    pending = []

    def send(src, dst, send_sem, recv_sem, device):
        copy = remote(src, dst, send_sem, recv_sem, device)
        copy.start()
        pending.append(copy)

    def to_y(src, dst, sems):
        for t, _ in y_peers:
            send(src(t), dst(y), sems.at[0, t], sems.at[1, y], (t * NZX + w, c))

    def to_zx(src, dst, sems):
        for t in zx_peers:
            send(src(t), dst(w), sems.at[0, t], sems.at[1, w], (y * NZX + t, c))

    def from_y(dst, sems):
        for t, _ in y_peers:
            remote(dst(t), dst(t), sems.at[0, t], sems.at[1, t], (r, c)).wait_recv()

    def from_zx(dst, sems):
        for t in zx_peers:
            remote(dst(t), dst(t), sems.at[0, t], sems.at[1, t], (r, c)).wait_recv()

    def total_of(buf, count):
        return tree_sum([buf[k] for k in range(count)])

    def two_float_total(buf, count):
        total = buf[0]
        err = jnp.zeros_like(total)
        for k in range(1, count):
            total, e = two_sum(total, buf[k])
            err = err + e
        lane16 = lax.broadcasted_iota(jnp.int32, total.shape, 1)
        return jnp.where(lane16 < 64, total, total + pltpu.roll(err, 64, 1))

    core = c + 1 - 2 * lax.rem(c, 2)
    chip = lax.rem(c + 2, NCOL)
    first = remote(pk, rc1, sem1.at[0], sem1.at[1], (r, core))
    first.start()
    to_y(lambda t: spart.at[t], lambda m: sa.at[m], sa_sem)
    sa[y] = spart[y]
    first.wait_recv()
    pp[...] = pk[...] + rc1[...]
    second = remote(pp, rc2, sem1.at[2], sem1.at[3], (r, chip))
    second.start()
    lead_copies = [
        remote(leadbuf.at[0], leadbuf.at[1], sem_lead.at[j - 1], sem_lead.at[3], (r, j)) for j in range(1, NCOL)
    ]

    @pl.when(c == 0)
    def _():
        for copy in lead_copies:
            copy.start()

    second.wait_recv()
    pending.extend([first, second])
    panel = pp[...] + rc2[...]

    lane = lax.broadcasted_iota(jnp.int32, (PANEL, PANEL), 1)
    left = lane < 64
    l0, l1, l2, l3, l4 = gram_levels(panel)
    high, low = two_sum(l0, l1)
    high, low2 = two_sum(high, l2)
    low = (low + low2) + (l3 + l4)
    wpart[0:8] = jnp.where(left, high, pltpu.roll(low, 64, 1)).reshape(8, 16, 128)
    wpart[8:16] = jnp.where(left, pltpu.roll(high, 64, 1), low).reshape(8, 16, 128)
    to_y(lambda t: wpart.at[c * 4 + t], lambda m: wa.at[m], wa_sem)
    wa[y] = wpart[c * 4 + y]
    p_ref[...] = panel

    from_y(lambda t: sa.at[t], sa_sem)
    ssum[...] = total_of(sa, NY)
    to_zx(lambda t: ssum.at[pl.ds(8 * t, 8)], lambda m: sb.at[m], sb_sem)
    to_zx(lambda t: ssum.at[pl.ds(128, 16)], lambda m: sbx.at[m], sbx_sem)
    sb[w] = ssum[pl.ds(pl.multiple_of(8 * w, 8), 8)]
    sbx[w] = ssum[pl.ds(128, 16)]

    @pl.when(c != 0)
    def _():
        remote(leadbuf.at[0], leadbuf.at[1], sem_lead.at[0], sem_lead.at[3], (r, c)).wait_recv()

    lead = jnp.where(c == 0, leadbuf[0], leadbuf[1])
    swapped = swapped_columns(slab, lead, onehot)
    b_ref[...] = swapped
    store_b = pltpu.make_async_copy(b_ref, b_hbm, sem_out.at[0])
    store_b.start()
    inner = hdot(panel, swapped, (0, 0))
    for b in range(4):
        gpart[b] = inner[:, 128 * b : 128 * b + 128]
    to_y(lambda t: gpart.at[t], lambda m: ga.at[m], ga_sem)
    ga[y] = gpart[y]

    from_y(lambda t: wa.at[t], wa_sem)
    wsum[...] = two_float_total(wa, NY)
    to_zx(lambda t: wsum, lambda m: wb.at[m], wb_sem)
    wb[w] = wsum[...]

    from_zx(lambda t: sb.at[t], sb_sem)
    from_zx(lambda t: sbx.at[t], sbx_sem)
    tile = lambda t: pl.ds(pl.multiple_of(8 * t, 8), 8)
    sfull[y, tile(w)] = total_of(sb, NZX)
    sfull[y, pl.ds(128, 16)] = total_of(sbx, NZX)
    to_zx(lambda t: sfull.at[y, tile(w)], lambda m: sfull.at[y, tile(m)], sc_sem)

    from_y(lambda t: ga.at[t], ga_sem)
    gsum[...] = total_of(ga, NY)
    to_zx(lambda t: gsum.at[tile(t)], lambda m: gb.at[m], gb_sem)
    gb[w] = gsum[tile(w)]

    from_zx(lambda t: wb.at[t], wb_sem)
    wtot[...] = two_float_total(wb, NZX)
    mine = c * 4 + y
    for t, d in yc_peers:
        send(wtot, wfull.at[mine], wc_sem.at[0, d * 4 + t], wc_sem.at[1, mine], (t * NZX + w, d))
    wfull[mine] = wtot[...]

    from_zx(lambda t: sfull.at[y, tile(t)], sc_sem)
    to_y(lambda t: sfull.at[y], lambda m: sfull.at[m], sd_sem)

    from_zx(lambda t: gb.at[t], gb_sem)
    gfull[y, tile(w)] = total_of(gb, NZX)
    to_zx(lambda t: gfull.at[y, tile(w)], lambda m: gfull.at[y, tile(m)], gc_sem)

    for t, d in yc_peers:
        o = d * 4 + t
        remote(wfull.at[o], wfull.at[o], wc_sem.at[0, o], wc_sem.at[1, o], (r, c)).wait_recv()
    first_half = wfull[0:8].reshape(PANEL, PANEL)
    second_half = wfull[8:16].reshape(PANEL, PANEL)
    high = jnp.where(left, first_half, pltpu.roll(second_half, 64, 1))
    low = jnp.where(left, pltpu.roll(first_half, 64, 1), second_half)

    eliminate(high, r_out.at[0], x_out.at[0])
    r_one = r_out[0]
    x_one = x_out[0]

    from_zx(lambda t: gfull.at[y, tile(t)], gc_sem)
    to_y(lambda t: gfull.at[y], lambda m: gfull.at[m], gd_sem)

    rowi = lax.broadcasted_iota(jnp.int32, (PANEL, PANEL), 0)
    eye = jnp.where(rowi == lane, 1.0, 0.0).astype(F32)
    l0, l1, l2, l3, l4 = gram_levels(r_one)
    d, e1 = two_sum(high, -l0)
    d, e2 = two_sum(d, -l1)
    delta = (d - l2) + (((e1 + e2) + low) - (l3 + l4))
    gram_two = eye + hdot(hdot(x_one, delta), x_one, (1, 1))
    from_y(lambda t: sfull.at[t], sd_sem)
    stores = [store_b]
    for b in range(4):
        copy = pltpu.make_async_copy(
            sfull.at[b], s_hbm.at[0, :, 128 * b : 128 * b + 128], sem_out.at[1 + b]
        )
        copy.start()
        stores.append(copy)
    eliminate(gram_two, r_out.at[1], x_out.at[1])

    from_y(lambda t: gfull.at[t], gd_sem)
    for copy in stores:
        copy.wait()
    for copy in pending:
        copy.wait_send()

    @pl.when(c == 0)
    def _():
        for copy in lead_copies:
            copy.wait_send()


def tree_sum(terms):
    terms = list(terms)
    while len(terms) > 1:
        pairs = [terms[i] + terms[i + 1] for i in range(0, len(terms) - 1, 2)]
        terms = pairs + terms[len(pairs) * 2 :]
    return terms[0]


def spread(v):
    return jnp.broadcast_to(v, (8, 128))


def split_three(x):
    high = x.astype(BF16).astype(F32)
    rest = x - high
    mid = rest.astype(BF16).astype(F32)
    return high, mid, rest - mid


def thin_dot(left, right):
    l0, l1, l2 = split_three(left)
    r0, r1, r2 = split_three(right)
    lefts = jnp.concatenate([l0, l0, l1, l0, l1, l2], axis=0).astype(BF16)
    rights = jnp.concatenate([r0, r1, r0, r2, r1, r0], axis=0).astype(BF16)
    return bdot(lefts, rights, (0, 0))


def block_factor(v, first, sub, lane):
    columns = [spread(v[:, first + j : first + j + 1]) for j in range(8)]
    a = {(i, j): spread(columns[i][j : j + 1, :]) for j in range(8) for i in range(j + 1)}
    m = [[None] * 8 for _ in range(8)]
    for i in range(8):
        inv = lax.rsqrt(a[i, i])
        l = {j: a[i, j] * inv for j in range(i + 1, 8)}
        for j in range(i + 1, 8):
            for k in range(j, 8):
                a[j, k] = a[j, k] - l[j] * l[k]
        for j in range(i):
            m[i][j] = m[i][j] * inv
        m[i][i] = inv
        for k in range(i + 1, 8):
            for j in range(i + 1):
                t = l[k] * m[i][j]
                m[k][j] = -t if m[k][j] is None else m[k][j] - t
    terms = []
    inverse = jnp.zeros((8, 128), F32)
    for j in range(8):
        column = m[7][j]
        for k in range(6, j - 1, -1):
            column = jnp.where(sub <= k, m[k][j], column)
        if j > 0:
            column = jnp.where(sub < j, 0.0, column)
        terms.append(column * spread(v[j : j + 1, :]))
        inverse = jnp.where(lane == first + j, column, inverse)
    solved = tree_sum(terms)
    inside = (lane >= first) & (lane < first + 8)
    return solved, jnp.where(inside, inverse, solved), m


def eliminate(w, r_ref, x_ref):
    sub = lax.broadcasted_iota(jnp.int32, (8, 128), 0)
    lane = lax.broadcasted_iota(jnp.int32, (8, 128), 1)
    count = PANEL // 8
    blocks = [w[8 * b : 8 * b + 8, :] for b in range(count)]
    for b in range(count):
        first = 8 * b
        solved, both, m = block_factor(blocks[b], first, sub, lane)
        upper = jnp.where(lane >= first + sub, solved, 0.0)
        r_ref[first : first + 8, :] = upper
        x_ref[first : first + 8, :] = jnp.where(lane < first + 8, both, 0.0)
        if b == count - 1:
            break
        inside = (lane >= first) & (lane < first + 8)
        rows = blocks[b + 1]
        columns = [spread(rows[:, first + j : first + j + 1]) for j in range(8)]
        updates = []
        for p in range(8):
            coef = tree_sum([m[p][j] * columns[j] for j in range(p + 1)])
            updates.append(coef * spread(both[p : p + 1, :]))
        blocks[b + 1] = jnp.where(inside, 0.0, rows) - tree_sum(updates)
        if b + 2 < count:
            update = thin_dot(upper, both)
            for k in range(b + 2, count):
                blocks[k] = jnp.where(inside, 0.0, blocks[k]) - update[8 * k : 8 * k + 8, :]


def update_kernel(
    b_in, p_ref, g_ref, s_in, r_ref, x_ref,
    s_hbm, q_hbm, e_hbm, first_hbm, out_hbm,
    b_ref, qbuf, ebuf, fbuf, obuf, sem,
):
    lead_block = lax.axis_index("col") == 0
    load_b = pltpu.make_async_copy(b_in, b_ref, sem.at[8])
    load_b.start()
    copies = [pltpu.make_async_copy(s_in, s_hbm, sem.at[0])]
    copies[0].start()
    scale = 1.0 / 128.0

    def store(k, src, dst):
        copy = pltpu.make_async_copy(src, dst, sem.at[k])
        copy.start()
        copies.append(copy)

    r_one = r_ref[0]
    fbuf[...] = r_one * scale
    store(1, fbuf, first_hbm.at[0])
    inverse = hdot(x_ref[1], x_ref[0])
    basis = hdot(p_ref[...], inverse, (1, 1))
    qbuf[...] = basis * 128.0
    store(2, qbuf, q_hbm.at[0])
    r_factor = hdot(r_ref[1], r_one)
    load_b.wait()
    for k in range(4):
        cols = slice(128 * k, 128 * k + 128)
        projected = hdot(inverse, g_ref[k])
        rest = b_ref[:, cols] - hdot(basis, projected)
        if k == 0:
            projected = jnp.where(lead_block, r_factor, projected)
            rest = jnp.where(lead_block, 0.0, rest)
        ebuf[:, cols] = projected * scale
        obuf[:, cols] = rest
        store(3 + k, obuf.at[:, cols], out_hbm.at[:, cols])
    store(7, ebuf, e_hbm.at[0])
    for copy in copies:
        copy.wait()


def shards(matrix_slab, sketch_matrix, pivots):
    rows, width = matrix_slab.shape
    sk = sketch_matrix.shape[0]
    dma = pltpu.SemaphoreType.DMA
    hbm = pl.BlockSpec(memory_space=pltpu.HBM)
    tile = lambda *lead: pltpu.VMEM(lead + (8, 128), F32)
    block = lambda *lead: pltpu.VMEM(lead + (16, 128), F32)
    square = lambda *lead: pltpu.VMEM(lead + (PANEL, 128), F32)
    tall = lambda *lead: pltpu.VMEM(lead + (sk, 128), F32)
    flat = lambda *shape: jax.ShapeDtypeStruct(shape, F32)
    swapped, panel, inner, sketches, factors, inverses = pl.pallas_call(
        reduce_kernel,
        out_shape=(
            flat(rows, width), flat(rows, PANEL), flat(4, PANEL, PANEL), flat(1, sk, width),
            flat(2, PANEL, PANEL), flat(2, PANEL, PANEL),
        ),
        in_specs=[hbm] * 3,
        out_specs=(hbm, VMEM_SPEC, VMEM_SPEC, hbm, VMEM_SPEC, VMEM_SPEC),
        scratch_shapes=[
            pltpu.VMEM((rows, width), F32), pltpu.VMEM((rows, width), F32),
            pltpu.VMEM((sk, rows), F32), pltpu.VMEM((1, PANEL), jnp.int32),
            pltpu.VMEM((rows, PANEL), F32), pltpu.VMEM((rows, PANEL), F32),
            pltpu.VMEM((rows, PANEL), F32), pltpu.VMEM((rows, PANEL), F32),
            pltpu.VMEM((2, rows, PANEL), F32),
            block(16), block(NY), block(), block(NZX), block(), block(16),
            square(NY), square(NY), square(), tile(NZX),
            tall(NY), tall(NY), tall(), tile(NZX), block(NZX), tall(NY),
            dma((3,)), dma((5,)), dma((4,)), dma((4,)), dma((2, NY)), dma((2, NZX)), dma((2, 16)),
            dma((2, NY)), dma((2, NZX)), dma((2, NZX)), dma((2, NY)),
            dma((2, NY)), dma((2, NZX)), dma((2, NZX)), dma((2, NZX)), dma((2, NY)),
        ],
        compiler_params=pltpu.CompilerParams(
            collective_id=0, has_side_effects=True, vmem_limit_bytes=VMEM_REDUCE
        ),
        name="reduce",
    )(matrix_slab, sketch_matrix, pivots)
    return pl.pallas_call(
        update_kernel,
        out_shape=(
            flat(1, sk, width), flat(1, rows, PANEL), flat(1, PANEL, width),
            flat(1, PANEL, PANEL), flat(rows, width),
        ),
        in_specs=[hbm, VMEM_SPEC, VMEM_SPEC, hbm, VMEM_SPEC, VMEM_SPEC],
        out_specs=(hbm,) * 5,
        scratch_shapes=[
            pltpu.VMEM((rows, width), F32), pltpu.VMEM((rows, PANEL), F32), pltpu.VMEM((PANEL, width), F32),
            pltpu.VMEM((PANEL, PANEL), F32), pltpu.VMEM((rows, width), F32), dma((9,)),
        ],
        compiler_params=pltpu.CompilerParams(vmem_limit_bytes=VMEM_UPDATE),
        name="update",
    )(swapped, panel, inner, sketches, factors, inverses)


def solution(mesh):
    in_specs = (P("row", "col"), P(None, "row"), P())
    out_specs = (
        P(None, None, "col"),
        P(None, "row", None),
        P(None, None, "col"),
        P(),
        P("row", "col"),
    )
    return jax.shard_map(shards, mesh=mesh, in_specs=in_specs, out_specs=out_specs, check_vma=False)
```

```python
import functools
import math

import jax
import jax.numpy as jnp
from jax import lax
from jax.experimental import pallas as pl
from jax.experimental.pallas import tpu as pltpu
from jax.sharding import PartitionSpec as P

PANEL = 128
VMEM_REDUCE = 32 * 1024 * 1024
VMEM_UPDATE = 32 * 1024 * 1024
NY = 4
NZX = 16
NCOL = 4
MESH = pl.DeviceIdType.MESH
F32 = jnp.float32
BF16 = jnp.bfloat16
VMEM_SPEC = pl.BlockSpec(memory_space=pltpu.VMEM)


def hdot(left, right, contract=(1, 0)):
    return lax.dot_general(
        left,
        right,
        (((contract[0],), (contract[1],)), ((), ())),
        precision=lax.Precision.HIGHEST,
        preferred_element_type=F32,
    )


def bdot(left, right, contract=(1, 0)):
    return lax.dot_general(
        left, right, (((contract[0],), (contract[1],)), ((), ())), preferred_element_type=F32
    )


def select_dot(values, onehot, contract=(1, 0)):
    high = values.astype(BF16)
    rest = values - high.astype(F32)
    mid = rest.astype(BF16)
    low = (rest - mid.astype(F32)).astype(BF16)
    return (bdot(high, onehot, contract) + bdot(mid, onehot, contract)) + bdot(low, onehot, contract)


def two_sum(a, b):
    s = a + b
    t = s - a
    return s, (a - (s - t)) + (b - t)


def gram_levels(x):
    n = x.shape[1]
    sigma = jnp.max(jnp.abs(x), axis=0, keepdims=True) * 131072.0
    parts = []
    rest = x
    for _ in range(4):
        part = (rest + sigma) - sigma
        rest = rest - part
        parts.append(part.astype(BF16))
        sigma = sigma * (1.0 / 128.0)
    cat = jnp.concatenate(parts, axis=1)
    full = bdot(cat, cat, (0, 0))
    block = lambda i, j: full[i * n : (i + 1) * n, j * n : (j + 1) * n]
    return (
        block(0, 0),
        block(0, 1) + block(1, 0),
        (block(0, 2) + block(2, 0)) + block(1, 1),
        (block(0, 3) + block(3, 0)) + (block(1, 2) + block(2, 1)),
        (block(1, 3) + block(3, 1)) + block(2, 2),
    )


def pivot_onehot(piv, col_first, width):
    lanes = lax.broadcasted_iota(jnp.int32, (width, PANEL), 0) + col_first
    return jnp.where(lanes == piv, 1.0, 0.0).astype(BF16)


def swapped_columns(slab, lead, onehot):
    picked = bdot(jnp.ones((8, PANEL), BF16), onehot, (1, 1))[0:1, :]
    return jnp.where(picked > 0.5, select_dot(lead, onehot, (1, 1)), slab)


def remote(src, dst, send, recv, device):
    return pltpu.make_async_remote_copy(
        src_ref=src, dst_ref=dst, send_sem=send, recv_sem=recv, device_id=device, device_id_type=MESH
    )


def reduce_kernel(
    slab_hbm, sketch_hbm, piv_hbm,
    b_ref, p_ref, gfull, sfull, r_out, x_out,
    slab_ref, sketch_ref, piv_ref,
    pk, pp, rc1, rc2, leadbuf,
    wpart, wa, wsum, wb, wtot, wfull,
    gpart, ga, gsum, gb,
    spart, sa, ssum, sb, sbx,
    sem_in, sem1, sem_lead, wa_sem, wb_sem, wc_sem, ga_sem, gb_sem, gc_sem, gd_sem,
    sa_sem, sb_sem, sbx_sem, sc_sem, sd_sem,
):
    r = lax.axis_index("row")
    c = lax.axis_index("col")
    y = lax.div(r, NZX)
    w = lax.rem(r, NZX)
    width = slab_ref.shape[1]
    load_piv = pltpu.make_async_copy(piv_hbm, piv_ref, sem_in.at[0])
    load_slab = pltpu.make_async_copy(slab_hbm, slab_ref, sem_in.at[1])
    load_sketch = pltpu.make_async_copy(sketch_hbm, sketch_ref, sem_in.at[2])
    load_piv.start()
    load_slab.start()
    load_sketch.start()

    y_peers = [(lax.rem(y + i, NY), i) for i in range(1, NY)]
    zx_peers = [lax.rem(w + i, NZX) for i in range(1, NZX)]
    yc_peers = [
        (lax.rem(y + i, NY), lax.rem(c + j, NCOL)) for i in range(NY) for j in range(NCOL) if i or j
    ]

    barrier = pltpu.get_barrier_semaphore()
    for t in zx_peers:
        pl.semaphore_signal(barrier, inc=1, device_id=(y * NZX + t, c), device_id_type=MESH)
    for t, d in yc_peers:
        pl.semaphore_signal(barrier, inc=1, device_id=(t * NZX + w, d), device_id_type=MESH)

    load_piv.wait()
    onehot = pivot_onehot(piv_ref[...], c * width, width)
    load_slab.wait()
    slab = slab_ref[...]
    pk[...] = select_dot(slab, onehot)
    load_sketch.wait()
    sketch = hdot(sketch_ref[...], slab)
    for b in range(4):
        spart[b] = sketch[:, 128 * b : 128 * b + 128]
    leadbuf[0] = slab[:, :PANEL]
    pl.semaphore_wait(barrier, NZX - 1 + NY * NCOL - 1)

    pending = []

    def send(src, dst, send_sem, recv_sem, device):
        copy = remote(src, dst, send_sem, recv_sem, device)
        copy.start()
        pending.append(copy)

    def to_y(src, dst, sems):
        for t, _ in y_peers:
            send(src(t), dst(y), sems.at[0, t], sems.at[1, y], (t * NZX + w, c))

    def to_zx(src, dst, sems):
        for t in zx_peers:
            send(src(t), dst(w), sems.at[0, t], sems.at[1, w], (y * NZX + t, c))

    def from_y(dst, sems):
        for t, _ in y_peers:
            remote(dst(t), dst(t), sems.at[0, t], sems.at[1, t], (r, c)).wait_recv()

    def from_zx(dst, sems):
        for t in zx_peers:
            remote(dst(t), dst(t), sems.at[0, t], sems.at[1, t], (r, c)).wait_recv()

    def total_of(buf, count):
        return tree_sum([buf[k] for k in range(count)])

    def two_float_total(buf, count):
        total = buf[0]
        err = jnp.zeros_like(total)
        for k in range(1, count):
            total, e = two_sum(total, buf[k])
            err = err + e
        lane16 = lax.broadcasted_iota(jnp.int32, total.shape, 1)
        return jnp.where(lane16 < 64, total, total + pltpu.roll(err, 64, 1))

    core = c + 1 - 2 * lax.rem(c, 2)
    chip = lax.rem(c + 2, NCOL)
    first = remote(pk, rc1, sem1.at[0], sem1.at[1], (r, core))
    first.start()
    to_y(lambda t: spart.at[t], lambda m: sa.at[m], sa_sem)
    sa[y] = spart[y]
    first.wait_recv()
    pp[...] = pk[...] + rc1[...]
    second = remote(pp, rc2, sem1.at[2], sem1.at[3], (r, chip))
    second.start()
    lead_copies = [
        remote(leadbuf.at[0], leadbuf.at[1], sem_lead.at[j - 1], sem_lead.at[3], (r, j)) for j in range(1, NCOL)
    ]

    @pl.when(c == 0)
    def _():
        for copy in lead_copies:
            copy.start()

    second.wait_recv()
    pending.extend([first, second])
    panel = pp[...] + rc2[...]

    lane = lax.broadcasted_iota(jnp.int32, (PANEL, PANEL), 1)
    left = lane < 64
    l0, l1, l2, l3, l4 = gram_levels(panel)
    high, low = two_sum(l0, l1)
    high, low2 = two_sum(high, l2)
    low = (low + low2) + (l3 + l4)
    wpart[0:8] = jnp.where(left, high, pltpu.roll(low, 64, 1)).reshape(8, 16, 128)
    wpart[8:16] = jnp.where(left, pltpu.roll(high, 64, 1), low).reshape(8, 16, 128)
    to_y(lambda t: wpart.at[c * 4 + t], lambda m: wa.at[m], wa_sem)
    wa[y] = wpart[c * 4 + y]
    p_ref[...] = panel

    from_y(lambda t: sa.at[t], sa_sem)
    ssum[...] = total_of(sa, NY)
    to_zx(lambda t: ssum.at[pl.ds(8 * t, 8)], lambda m: sb.at[m], sb_sem)
    to_zx(lambda t: ssum.at[pl.ds(128, 16)], lambda m: sbx.at[m], sbx_sem)
    sb[w] = ssum[pl.ds(pl.multiple_of(8 * w, 8), 8)]
    sbx[w] = ssum[pl.ds(128, 16)]

    @pl.when(c != 0)
    def _():
        remote(leadbuf.at[0], leadbuf.at[1], sem_lead.at[0], sem_lead.at[3], (r, c)).wait_recv()

    lead = jnp.where(c == 0, leadbuf[0], leadbuf[1])
    swapped = swapped_columns(slab, lead, onehot)
    b_ref[...] = swapped
    inner = hdot(panel, swapped, (0, 0))
    for b in range(4):
        gpart[b] = inner[:, 128 * b : 128 * b + 128]
    to_y(lambda t: gpart.at[t], lambda m: ga.at[m], ga_sem)
    ga[y] = gpart[y]

    from_y(lambda t: wa.at[t], wa_sem)
    wsum[...] = two_float_total(wa, NY)
    to_zx(lambda t: wsum, lambda m: wb.at[m], wb_sem)
    wb[w] = wsum[...]

    from_zx(lambda t: sb.at[t], sb_sem)
    from_zx(lambda t: sbx.at[t], sbx_sem)
    tile = lambda t: pl.ds(pl.multiple_of(8 * t, 8), 8)
    sfull[y, tile(w)] = total_of(sb, NZX)
    sfull[y, pl.ds(128, 16)] = total_of(sbx, NZX)
    to_zx(lambda t: sfull.at[y, tile(w)], lambda m: sfull.at[y, tile(m)], sc_sem)

    from_y(lambda t: ga.at[t], ga_sem)
    gsum[...] = total_of(ga, NY)
    to_zx(lambda t: gsum.at[tile(t)], lambda m: gb.at[m], gb_sem)
    gb[w] = gsum[tile(w)]

    from_zx(lambda t: wb.at[t], wb_sem)
    wtot[...] = two_float_total(wb, NZX)
    mine = c * 4 + y
    for t, d in yc_peers:
        send(wtot, wfull.at[mine], wc_sem.at[0, d * 4 + t], wc_sem.at[1, mine], (t * NZX + w, d))
    wfull[mine] = wtot[...]

    from_zx(lambda t: sfull.at[y, tile(t)], sc_sem)
    to_y(lambda t: sfull.at[y], lambda m: sfull.at[m], sd_sem)

    from_zx(lambda t: gb.at[t], gb_sem)
    gfull[y, tile(w)] = total_of(gb, NZX)
    to_zx(lambda t: gfull.at[y, tile(w)], lambda m: gfull.at[y, tile(m)], gc_sem)

    for t, d in yc_peers:
        o = d * 4 + t
        remote(wfull.at[o], wfull.at[o], wc_sem.at[0, o], wc_sem.at[1, o], (r, c)).wait_recv()
    first_half = wfull[0:8].reshape(PANEL, PANEL)
    second_half = wfull[8:16].reshape(PANEL, PANEL)
    high = jnp.where(left, first_half, pltpu.roll(second_half, 64, 1))
    low = jnp.where(left, pltpu.roll(first_half, 64, 1), second_half)

    eliminate(high, r_out.at[0], x_out.at[0])
    r_one = r_out[0]
    x_one = x_out[0]

    from_zx(lambda t: gfull.at[y, tile(t)], gc_sem)
    to_y(lambda t: gfull.at[y], lambda m: gfull.at[m], gd_sem)

    rowi = lax.broadcasted_iota(jnp.int32, (PANEL, PANEL), 0)
    eye = jnp.where(rowi == lane, 1.0, 0.0).astype(F32)
    l0, l1, l2, l3, l4 = gram_levels(r_one)
    d, e1 = two_sum(high, -l0)
    d, e2 = two_sum(d, -l1)
    delta = (d - l2) + (((e1 + e2) + low) - (l3 + l4))
    gram_two = eye + hdot(hdot(x_one, delta), x_one, (1, 1))
    from_y(lambda t: sfull.at[t], sd_sem)
    eliminate(gram_two, r_out.at[1], x_out.at[1])

    from_y(lambda t: gfull.at[t], gd_sem)
    for copy in pending:
        copy.wait_send()

    @pl.when(c == 0)
    def _():
        for copy in lead_copies:
            copy.wait_send()


def tree_sum(terms):
    terms = list(terms)
    while len(terms) > 1:
        pairs = [terms[i] + terms[i + 1] for i in range(0, len(terms) - 1, 2)]
        terms = pairs + terms[len(pairs) * 2 :]
    return terms[0]


def spread(v):
    return jnp.broadcast_to(v, (8, 128))


def split_three(x):
    high = x.astype(BF16).astype(F32)
    rest = x - high
    mid = rest.astype(BF16).astype(F32)
    return high, mid, rest - mid


def thin_dot(left, right):
    l0, l1, l2 = split_three(left)
    r0, r1, r2 = split_three(right)
    lefts = jnp.concatenate([l0, l0, l1, l0, l1, l2], axis=0).astype(BF16)
    rights = jnp.concatenate([r0, r1, r0, r2, r1, r0], axis=0).astype(BF16)
    return bdot(lefts, rights, (0, 0))


def block_factor(v, first, sub, lane):
    columns = [spread(v[:, first + j : first + j + 1]) for j in range(8)]
    a = {(i, j): spread(columns[i][j : j + 1, :]) for j in range(8) for i in range(j + 1)}
    m = [[None] * 8 for _ in range(8)]
    for i in range(8):
        inv = lax.rsqrt(a[i, i])
        l = {j: a[i, j] * inv for j in range(i + 1, 8)}
        for j in range(i + 1, 8):
            for k in range(j, 8):
                a[j, k] = a[j, k] - l[j] * l[k]
        for j in range(i):
            m[i][j] = m[i][j] * inv
        m[i][i] = inv
        for k in range(i + 1, 8):
            for j in range(i + 1):
                t = l[k] * m[i][j]
                m[k][j] = -t if m[k][j] is None else m[k][j] - t
    terms = []
    inverse = jnp.zeros((8, 128), F32)
    for j in range(8):
        column = m[7][j]
        for k in range(6, j - 1, -1):
            column = jnp.where(sub <= k, m[k][j], column)
        if j > 0:
            column = jnp.where(sub < j, 0.0, column)
        terms.append(column * spread(v[j : j + 1, :]))
        inverse = jnp.where(lane == first + j, column, inverse)
    solved = tree_sum(terms)
    inside = (lane >= first) & (lane < first + 8)
    return solved, jnp.where(inside, inverse, solved), m


def eliminate(w, r_ref, x_ref):
    sub = lax.broadcasted_iota(jnp.int32, (8, 128), 0)
    lane = lax.broadcasted_iota(jnp.int32, (8, 128), 1)
    count = PANEL // 8
    blocks = [w[8 * b : 8 * b + 8, :] for b in range(count)]
    for b in range(count):
        first = 8 * b
        solved, both, m = block_factor(blocks[b], first, sub, lane)
        upper = jnp.where(lane >= first + sub, solved, 0.0)
        r_ref[first : first + 8, :] = upper
        x_ref[first : first + 8, :] = jnp.where(lane < first + 8, both, 0.0)
        if b == count - 1:
            break
        inside = (lane >= first) & (lane < first + 8)
        rows = blocks[b + 1]
        columns = [spread(rows[:, first + j : first + j + 1]) for j in range(8)]
        updates = []
        for p in range(8):
            coef = tree_sum([m[p][j] * columns[j] for j in range(p + 1)])
            updates.append(coef * spread(both[p : p + 1, :]))
        blocks[b + 1] = jnp.where(inside, 0.0, rows) - tree_sum(updates)
        if b + 2 < count:
            update = thin_dot(upper, both)
            for k in range(b + 2, count):
                blocks[k] = jnp.where(inside, 0.0, blocks[k]) - update[8 * k : 8 * k + 8, :]


def update_kernel(
    b_ref, p_ref, g_ref, s_ref, r_ref, x_ref,
    s_hbm, q_hbm, e_hbm, first_hbm, out_hbm,
    qbuf, ebuf, fbuf, obuf, sem,
):
    lead_block = lax.axis_index("col") == 0
    copies = []
    scale = 1.0 / 128.0

    def store(k, src, dst):
        copy = pltpu.make_async_copy(src, dst, sem.at[k])
        copy.start()
        copies.append(copy)

    for k in range(4):
        store(k, s_ref.at[k], s_hbm.at[0, :, 128 * k : 128 * k + 128])
    r_one = r_ref[0]
    fbuf[...] = r_one * scale
    store(8, fbuf, first_hbm.at[0])
    inverse = hdot(x_ref[1], x_ref[0])
    basis = hdot(p_ref[...], inverse, (1, 1))
    qbuf[...] = basis * 128.0
    store(9, qbuf, q_hbm.at[0])
    r_factor = hdot(r_ref[1], r_one)
    for k in range(4):
        cols = slice(128 * k, 128 * k + 128)
        projected = hdot(inverse, g_ref[k])
        rest = b_ref[:, cols] - hdot(basis, projected)
        if k == 0:
            projected = jnp.where(lead_block, r_factor, projected)
            rest = jnp.where(lead_block, 0.0, rest)
        ebuf[:, cols] = projected * scale
        obuf[:, cols] = rest
        store(4 + k, obuf.at[:, cols], out_hbm.at[:, cols])
    store(10, ebuf, e_hbm.at[0])
    for copy in copies:
        copy.wait()


def shards(matrix_slab, sketch_matrix, pivots):
    rows, width = matrix_slab.shape
    sk = sketch_matrix.shape[0]
    dma = pltpu.SemaphoreType.DMA
    hbm = pl.BlockSpec(memory_space=pltpu.HBM)
    tile = lambda *lead: pltpu.VMEM(lead + (8, 128), F32)
    block = lambda *lead: pltpu.VMEM(lead + (16, 128), F32)
    square = lambda *lead: pltpu.VMEM(lead + (PANEL, 128), F32)
    tall = lambda *lead: pltpu.VMEM(lead + (sk, 128), F32)
    flat = lambda *shape: jax.ShapeDtypeStruct(shape, F32)
    swapped, panel, inner, sketches, factors, inverses = pl.pallas_call(
        reduce_kernel,
        out_shape=(
            flat(rows, width), flat(rows, PANEL), flat(4, PANEL, PANEL), flat(4, sk, PANEL),
            flat(2, PANEL, PANEL), flat(2, PANEL, PANEL),
        ),
        in_specs=[hbm] * 3,
        out_specs=(VMEM_SPEC,) * 6,
        scratch_shapes=[
            pltpu.VMEM((rows, width), F32), pltpu.VMEM((sk, rows), F32), pltpu.VMEM((1, PANEL), jnp.int32),
            pltpu.VMEM((rows, PANEL), F32), pltpu.VMEM((rows, PANEL), F32),
            pltpu.VMEM((rows, PANEL), F32), pltpu.VMEM((rows, PANEL), F32),
            pltpu.VMEM((2, rows, PANEL), F32),
            block(16), block(NY), block(), block(NZX), block(), block(16),
            square(NY), square(NY), square(), tile(NZX),
            tall(NY), tall(NY), tall(), tile(NZX), block(NZX),
            dma((3,)), dma((4,)), dma((4,)), dma((2, NY)), dma((2, NZX)), dma((2, 16)),
            dma((2, NY)), dma((2, NZX)), dma((2, NZX)), dma((2, NY)),
            dma((2, NY)), dma((2, NZX)), dma((2, NZX)), dma((2, NZX)), dma((2, NY)),
        ],
        compiler_params=pltpu.CompilerParams(
            collective_id=0, has_side_effects=True, vmem_limit_bytes=VMEM_REDUCE
        ),
        name="reduce",
    )(*[pltpu.with_memory_space_constraint(a, pltpu.HBM) for a in (matrix_slab, sketch_matrix, pivots)])
    return pl.pallas_call(
        update_kernel,
        out_shape=(
            flat(1, sk, width), flat(1, rows, PANEL), flat(1, PANEL, width),
            flat(1, PANEL, PANEL), flat(rows, width),
        ),
        in_specs=[VMEM_SPEC] * 6,
        out_specs=(hbm,) * 5,
        scratch_shapes=[
            pltpu.VMEM((rows, PANEL), F32), pltpu.VMEM((PANEL, width), F32),
            pltpu.VMEM((PANEL, PANEL), F32), pltpu.VMEM((rows, width), F32), dma((11,)),
        ],
        compiler_params=pltpu.CompilerParams(vmem_limit_bytes=VMEM_UPDATE),
        name="update",
    )(swapped, panel, inner, sketches, factors, inverses)


def solution(mesh):
    in_specs = (P("row", "col"), P(None, "row"), P())
    out_specs = (
        P(None, None, "col"),
        P(None, "row", None),
        P(None, None, "col"),
        P(),
        P("row", "col"),
    )
    return jax.shard_map(shards, mesh=mesh, in_specs=in_specs, out_specs=out_specs, check_vma=False)
```

```python
import functools
import math

import jax
import jax.numpy as jnp
from jax import lax
from jax.experimental import pallas as pl
from jax.experimental.pallas import tpu as pltpu
from jax.sharding import PartitionSpec as P

PANEL = 128
VMEM_REDUCE = 32 * 1024 * 1024
VMEM_UPDATE = 32 * 1024 * 1024
NY = 4
NZX = 16
NCOL = 4
MESH = pl.DeviceIdType.MESH
F32 = jnp.float32
BF16 = jnp.bfloat16
VMEM_SPEC = pl.BlockSpec(memory_space=pltpu.VMEM)


def hdot(left, right, contract=(1, 0)):
    return lax.dot_general(
        left,
        right,
        (((contract[0],), (contract[1],)), ((), ())),
        precision=lax.Precision.HIGHEST,
        preferred_element_type=F32,
    )


def bdot(left, right, contract=(1, 0)):
    return lax.dot_general(
        left, right, (((contract[0],), (contract[1],)), ((), ())), preferred_element_type=F32
    )


def select_dot(values, onehot, contract=(1, 0)):
    high = values.astype(BF16)
    rest = values - high.astype(F32)
    mid = rest.astype(BF16)
    low = (rest - mid.astype(F32)).astype(BF16)
    return (bdot(high, onehot, contract) + bdot(mid, onehot, contract)) + bdot(low, onehot, contract)


def two_sum(a, b):
    s = a + b
    t = s - a
    return s, (a - (s - t)) + (b - t)


def gram_levels(x):
    n = x.shape[1]
    sigma = jnp.max(jnp.abs(x), axis=0, keepdims=True) * 131072.0
    parts = []
    rest = x
    for _ in range(4):
        part = (rest + sigma) - sigma
        rest = rest - part
        parts.append(part.astype(BF16))
        sigma = sigma * (1.0 / 128.0)
    cat = jnp.concatenate(parts, axis=1)
    full = bdot(cat, cat, (0, 0))
    block = lambda i, j: full[i * n : (i + 1) * n, j * n : (j + 1) * n]
    return (
        block(0, 0),
        block(0, 1) + block(1, 0),
        (block(0, 2) + block(2, 0)) + block(1, 1),
        (block(0, 3) + block(3, 0)) + (block(1, 2) + block(2, 1)),
        (block(1, 3) + block(3, 1)) + block(2, 2),
    )


def pivot_onehot(piv, col_first, width):
    lanes = lax.broadcasted_iota(jnp.int32, (width, PANEL), 0) + col_first
    return jnp.where(lanes == piv, 1.0, 0.0).astype(BF16)


def swapped_columns(slab, lead, onehot):
    picked = bdot(jnp.ones((8, PANEL), BF16), onehot, (1, 1))[0:1, :]
    return jnp.where(picked > 0.5, select_dot(lead, onehot, (1, 1)), slab)


def remote(src, dst, send, recv, device):
    return pltpu.make_async_remote_copy(
        src_ref=src, dst_ref=dst, send_sem=send, recv_sem=recv, device_id=device, device_id_type=MESH
    )


def pack_symmetric(high, low):
    row = lax.broadcasted_iota(jnp.int32, (64, 128), 0)
    lane = lax.broadcasted_iota(jnp.int32, (64, 128), 1)
    join = lambda a, b: jnp.where(lane[: a.shape[0]] < 64, a, pltpu.roll(b, 64, 1))
    corner = lambda v: jnp.where(row > lane, v[:64], pltpu.roll(v[64:], 64, 1))
    diagonal = lambda v: jnp.sum(jnp.where(row == lane, v[:64], 0.0), axis=0, keepdims=True)
    packed = jnp.concatenate([join(high[64:], low[64:]), join(corner(high), corner(low))], axis=0)
    return packed, join(diagonal(high), diagonal(low))


def unpack_symmetric(packed, diagonal):
    row = lax.broadcasted_iota(jnp.int32, (64, 128), 0)
    lane = lax.broadcasted_iota(jnp.int32, (64, 128), 1)
    below, corner = packed[:64], packed[64:]
    top = jnp.where(row == lane, diagonal, corner)
    bottom = jnp.where(lane < 64, below, pltpu.roll(corner, 64, 1))
    part = jnp.concatenate([top, bottom], axis=0)
    row = lax.broadcasted_iota(jnp.int32, (128, 128), 0)
    lane = lax.broadcasted_iota(jnp.int32, (128, 128), 1)
    lower = (lane <= row) & ((row < 64) | (lane < 64))
    upper = (row >= 64) & (lane >= row)
    return jnp.where(lower | upper, part, part.T)


def reduce_kernel(
    slab_hbm, sketch_hbm, piv_hbm,
    b_ref, p_ref, gfull, sfull, r_out, x_out,
    slab_ref, sketch_ref, piv_ref,
    pk, pp, rc1, rc2, leadbuf,
    wpart, wa, wsum, wb, wtot, wfull,
    gpart, ga, gsum, gb,
    spart, sa, ssum, sb, sbx,
    sem_in, sem1, sem_p, sem_lead, wa_sem, wb_sem, wc_sem, ga_sem, gb_sem, gc_sem, gd_sem,
    sa_sem, sb_sem, sbx_sem, sc_sem, sd_sem,
):
    r = lax.axis_index("row")
    c = lax.axis_index("col")
    y = lax.div(r, NZX)
    w = lax.rem(r, NZX)
    core = lax.rem(c, 2)
    other_core = c + 1 - 2 * core
    other_chip = lax.rem(c + 2, NCOL)
    width = slab_ref.shape[1]
    load_piv = pltpu.make_async_copy(piv_hbm, piv_ref, sem_in.at[0])
    load_slab = pltpu.make_async_copy(slab_hbm, slab_ref, sem_in.at[1])
    load_sketch = pltpu.make_async_copy(sketch_hbm, sketch_ref, sem_in.at[2])
    load_piv.start()
    load_slab.start()
    load_sketch.start()

    y_peers = [(lax.rem(y + i, NY), i) for i in range(1, NY)]
    zx_peers = [lax.rem(w + i, NZX) for i in range(1, NZX)]
    own = y * 2 + core
    pair_peers = [lax.rem(own + i, 2 * NY) for i in range(1, 2 * NY)]

    def pair_device(t):
        return (lax.div(t, 2) * NZX + w, c - core + lax.rem(t, 2))

    barrier = pltpu.get_barrier_semaphore()
    for t in zx_peers:
        pl.semaphore_signal(barrier, inc=1, device_id=(y * NZX + t, c), device_id_type=MESH)
    for t in pair_peers:
        pl.semaphore_signal(barrier, inc=1, device_id=pair_device(t), device_id_type=MESH)
    for d in (other_chip, other_chip + 1 - 2 * core):
        pl.semaphore_signal(barrier, inc=1, device_id=(r, d), device_id_type=MESH)

    load_piv.wait()
    onehot = pivot_onehot(piv_ref[...], c * width, width)
    load_slab.wait()
    slab = slab_ref[...]
    pk[...] = select_dot(slab, onehot)
    load_sketch.wait()
    sketch = hdot(sketch_ref[...], slab)
    for b in range(4):
        spart[b] = sketch[:, 128 * b : 128 * b + 128]
    leadbuf[0] = slab[:, :PANEL]
    pl.semaphore_wait(barrier, NZX - 1 + 2 * NY - 1 + 2)

    pending = []

    def send(src, dst, send_sem, recv_sem, device):
        copy = remote(src, dst, send_sem, recv_sem, device)
        copy.start()
        pending.append(copy)

    def to_y(src, dst, sems):
        for t, _ in y_peers:
            send(src(t), dst(y), sems.at[0, t], sems.at[1, y], (t * NZX + w, c))

    def to_zx(src, dst, sems):
        for t in zx_peers:
            send(src(t), dst(w), sems.at[0, t], sems.at[1, w], (y * NZX + t, c))

    def from_y(dst, sems):
        for t, _ in y_peers:
            remote(dst(t), dst(t), sems.at[0, t], sems.at[1, t], (r, c)).wait_recv()

    def from_zx(dst, sems):
        for t in zx_peers:
            remote(dst(t), dst(t), sems.at[0, t], sems.at[1, t], (r, c)).wait_recv()

    def total_of(buf, count):
        return tree_sum([buf[k] for k in range(count)])

    def two_float_total(buf, count):
        total = buf[0]
        err = jnp.zeros_like(total)
        for k in range(1, count):
            total, e = two_sum(total, buf[k])
            err = err + e
        lanes = lax.broadcasted_iota(jnp.int32, total.shape, 1)
        return jnp.where(lanes < 64, total, total + pltpu.roll(err, 64, 1))

    mine = pl.ds(pl.multiple_of(128 * core, 128), 128)
    theirs = pl.ds(pl.multiple_of(128 - 128 * core, 128), 128)
    first = remote(pk.at[theirs], rc1, sem1.at[0], sem1.at[1], (r, other_core))
    first.start()
    to_y(lambda t: spart.at[t], lambda m: sa.at[m], sa_sem)
    sa[y] = spart[y]
    first.wait_recv()
    pp[...] = pk[mine] + rc1[...]
    second = remote(pp, rc2, sem1.at[2], sem1.at[3], (r, other_chip))
    second.start()
    lead_copies = [
        remote(leadbuf.at[0], leadbuf.at[1], sem_lead.at[j - 1], sem_lead.at[3], (r, j)) for j in range(1, NCOL)
    ]

    @pl.when(c == 0)
    def _():
        for copy in lead_copies:
            copy.start()

    second.wait_recv()
    pending.extend([first, second])
    half = pp[...] + rc2[...]
    p_ref[mine] = half
    third = remote(p_ref.at[mine], p_ref.at[mine], sem_p.at[0], sem_p.at[1], (r, other_core))
    third.start()
    pending.append(third)

    lane = lax.broadcasted_iota(jnp.int32, (PANEL, PANEL), 1)
    l0, l1, l2, l3, l4 = gram_levels(half)
    high, low = two_sum(l0, l1)
    high, low2 = two_sum(high, l2)
    low = (low + low2) + (l3 + l4)
    packed, diagonal = pack_symmetric(high, low)
    for o in range(2 * NY):
        wpart[o, 0:16] = packed[16 * o : 16 * o + 16]
        wpart[o, 16:17] = diagonal
    for t in pair_peers:
        send(wpart.at[t], wa.at[own], wa_sem.at[0, t], wa_sem.at[1, own], pair_device(t))
    wa[own] = wpart[own]

    from_y(lambda t: sa.at[t], sa_sem)
    ssum[...] = total_of(sa, NY)
    to_zx(lambda t: ssum.at[pl.ds(8 * t, 8)], lambda m: sb.at[m], sb_sem)
    to_zx(lambda t: ssum.at[pl.ds(128, 16)], lambda m: sbx.at[m], sbx_sem)
    sb[w] = ssum[pl.ds(pl.multiple_of(8 * w, 8), 8)]
    sbx[w] = ssum[pl.ds(128, 16)]

    @pl.when(c != 0)
    def _():
        remote(leadbuf.at[0], leadbuf.at[1], sem_lead.at[0], sem_lead.at[3], (r, c)).wait_recv()

    lead = jnp.where(c == 0, leadbuf[0], leadbuf[1])
    remote(p_ref.at[theirs], p_ref.at[theirs], sem_p.at[0], sem_p.at[1], (r, c)).wait_recv()
    panel = p_ref[...]
    swapped = swapped_columns(slab, lead, onehot)
    b_ref[...] = swapped
    inner = hdot(panel, swapped, (0, 0))
    for b in range(4):
        gpart[b] = inner[:, 128 * b : 128 * b + 128]
    to_y(lambda t: gpart.at[t], lambda m: ga.at[m], ga_sem)
    ga[y] = gpart[y]

    for t in pair_peers:
        remote(wa.at[t], wa.at[t], wa_sem.at[0, t], wa_sem.at[1, t], (r, c)).wait_recv()
    wsum[...] = two_float_total(wa, 2 * NY)
    to_zx(lambda t: wsum, lambda m: wb.at[m], wb_sem)
    wb[w] = wsum[...]

    from_zx(lambda t: sb.at[t], sb_sem)
    from_zx(lambda t: sbx.at[t], sbx_sem)
    tile = lambda t: pl.ds(pl.multiple_of(8 * t, 8), 8)
    sfull[y, tile(w)] = total_of(sb, NZX)
    sfull[y, pl.ds(128, 16)] = total_of(sbx, NZX)
    to_zx(lambda t: sfull.at[y, tile(w)], lambda m: sfull.at[y, tile(m)], sc_sem)

    from_y(lambda t: ga.at[t], ga_sem)
    gsum[...] = total_of(ga, NY)
    to_zx(lambda t: gsum.at[tile(t)], lambda m: gb.at[m], gb_sem)
    gb[w] = gsum[tile(w)]

    from_zx(lambda t: wb.at[t], wb_sem)
    wtot[...] = two_float_total(wb, NZX)
    for t in pair_peers:
        send(wtot, wfull.at[own], wc_sem.at[0, t], wc_sem.at[1, own], pair_device(t))
    wfull[own] = wtot[...]

    from_zx(lambda t: sfull.at[y, tile(t)], sc_sem)
    to_y(lambda t: sfull.at[y], lambda m: sfull.at[m], sd_sem)

    from_zx(lambda t: gb.at[t], gb_sem)
    gfull[y, tile(w)] = total_of(gb, NZX)
    to_zx(lambda t: gfull.at[y, tile(w)], lambda m: gfull.at[y, tile(m)], gc_sem)

    for t in pair_peers:
        remote(wfull.at[t], wfull.at[t], wc_sem.at[0, t], wc_sem.at[1, t], (r, c)).wait_recv()
    packed = jnp.concatenate([wfull[o, 0:16] for o in range(2 * NY)], axis=0)
    diagonal = wfull[0, 16:17]
    high = unpack_symmetric(packed, diagonal)
    low = unpack_symmetric(pltpu.roll(packed, 64, 1), pltpu.roll(diagonal, 64, 1))

    eliminate(high, r_out.at[0], x_out.at[0])
    r_one = r_out[0]
    x_one = x_out[0]

    from_zx(lambda t: gfull.at[y, tile(t)], gc_sem)
    to_y(lambda t: gfull.at[y], lambda m: gfull.at[m], gd_sem)

    rowi = lax.broadcasted_iota(jnp.int32, (PANEL, PANEL), 0)
    eye = jnp.where(rowi == lane, 1.0, 0.0).astype(F32)
    l0, l1, l2, l3, l4 = gram_levels(r_one)
    d, e1 = two_sum(high, -l0)
    d, e2 = two_sum(d, -l1)
    delta = (d - l2) + (((e1 + e2) + low) - (l3 + l4))
    gram_two = eye + hdot(hdot(x_one, delta), x_one, (1, 1))
    from_y(lambda t: sfull.at[t], sd_sem)
    eliminate(gram_two, r_out.at[1], x_out.at[1])

    from_y(lambda t: gfull.at[t], gd_sem)
    for copy in pending:
        copy.wait_send()

    @pl.when(c == 0)
    def _():
        for copy in lead_copies:
            copy.wait_send()


def tree_sum(terms):
    terms = list(terms)
    while len(terms) > 1:
        pairs = [terms[i] + terms[i + 1] for i in range(0, len(terms) - 1, 2)]
        terms = pairs + terms[len(pairs) * 2 :]
    return terms[0]


def spread(v):
    return jnp.broadcast_to(v, (8, 128))


def split_three(x):
    high = x.astype(BF16).astype(F32)
    rest = x - high
    mid = rest.astype(BF16).astype(F32)
    return high, mid, rest - mid


def thin_dot(left, right):
    l0, l1, l2 = split_three(left)
    r0, r1, r2 = split_three(right)
    lefts = jnp.concatenate([l0, l0, l1, l0, l1, l2], axis=0).astype(BF16)
    rights = jnp.concatenate([r0, r1, r0, r2, r1, r0], axis=0).astype(BF16)
    return bdot(lefts, rights, (0, 0))


def block_factor(v, first, sub, lane):
    columns = [spread(v[:, first + j : first + j + 1]) for j in range(8)]
    a = {(i, j): spread(columns[i][j : j + 1, :]) for j in range(8) for i in range(j + 1)}
    m = [[None] * 8 for _ in range(8)]
    for i in range(8):
        inv = lax.rsqrt(a[i, i])
        l = {j: a[i, j] * inv for j in range(i + 1, 8)}
        for j in range(i + 1, 8):
            for k in range(j, 8):
                a[j, k] = a[j, k] - l[j] * l[k]
        for j in range(i):
            m[i][j] = m[i][j] * inv
        m[i][i] = inv
        for k in range(i + 1, 8):
            for j in range(i + 1):
                t = l[k] * m[i][j]
                m[k][j] = -t if m[k][j] is None else m[k][j] - t
    terms = []
    inverse = jnp.zeros((8, 128), F32)
    for j in range(8):
        column = m[7][j]
        for k in range(6, j - 1, -1):
            column = jnp.where(sub <= k, m[k][j], column)
        if j > 0:
            column = jnp.where(sub < j, 0.0, column)
        terms.append(column * spread(v[j : j + 1, :]))
        inverse = jnp.where(lane == first + j, column, inverse)
    solved = tree_sum(terms)
    inside = (lane >= first) & (lane < first + 8)
    return solved, jnp.where(inside, inverse, solved), m


def eliminate(w, r_ref, x_ref):
    sub = lax.broadcasted_iota(jnp.int32, (8, 128), 0)
    lane = lax.broadcasted_iota(jnp.int32, (8, 128), 1)
    count = PANEL // 8
    blocks = [w[8 * b : 8 * b + 8, :] for b in range(count)]
    for b in range(count):
        first = 8 * b
        solved, both, m = block_factor(blocks[b], first, sub, lane)
        upper = jnp.where(lane >= first + sub, solved, 0.0)
        r_ref[first : first + 8, :] = upper
        x_ref[first : first + 8, :] = jnp.where(lane < first + 8, both, 0.0)
        if b == count - 1:
            break
        inside = (lane >= first) & (lane < first + 8)
        rows = blocks[b + 1]
        columns = [spread(rows[:, first + j : first + j + 1]) for j in range(8)]
        updates = []
        for p in range(8):
            coef = tree_sum([m[p][j] * columns[j] for j in range(p + 1)])
            updates.append(coef * spread(both[p : p + 1, :]))
        blocks[b + 1] = jnp.where(inside, 0.0, rows) - tree_sum(updates)
        if b + 2 < count:
            update = thin_dot(upper, both)
            for k in range(b + 2, count):
                blocks[k] = jnp.where(inside, 0.0, blocks[k]) - update[8 * k : 8 * k + 8, :]


def update_kernel(
    b_ref, p_ref, g_ref, s_ref, r_ref, x_ref,
    s_hbm, q_hbm, e_hbm, first_hbm, out_hbm,
    qbuf, ebuf, fbuf, obuf, sem,
):
    lead_block = lax.axis_index("col") == 0
    copies = []
    scale = 1.0 / 128.0

    def store(k, src, dst):
        copy = pltpu.make_async_copy(src, dst, sem.at[k])
        copy.start()
        copies.append(copy)

    for k in range(4):
        store(k, s_ref.at[k], s_hbm.at[0, :, 128 * k : 128 * k + 128])
    r_one = r_ref[0]
    fbuf[...] = r_one * scale
    store(8, fbuf, first_hbm.at[0])
    inverse = hdot(x_ref[1], x_ref[0])
    basis = hdot(p_ref[...], inverse, (1, 1))
    qbuf[...] = basis * 128.0
    store(9, qbuf, q_hbm.at[0])
    r_factor = hdot(r_ref[1], r_one)
    for k in range(4):
        cols = slice(128 * k, 128 * k + 128)
        projected = hdot(inverse, g_ref[k])
        rest = b_ref[:, cols] - hdot(basis, projected)
        if k == 0:
            projected = jnp.where(lead_block, r_factor, projected)
            rest = jnp.where(lead_block, 0.0, rest)
        ebuf[:, cols] = projected * scale
        obuf[:, cols] = rest
        store(4 + k, obuf.at[:, cols], out_hbm.at[:, cols])
    store(10, ebuf, e_hbm.at[0])
    for copy in copies:
        copy.wait()


def shards(matrix_slab, sketch_matrix, pivots):
    rows, width = matrix_slab.shape
    sk = sketch_matrix.shape[0]
    dma = pltpu.SemaphoreType.DMA
    hbm = pl.BlockSpec(memory_space=pltpu.HBM)
    tile = lambda *lead: pltpu.VMEM(lead + (8, 128), F32)
    block = lambda *lead: pltpu.VMEM(lead + (16, 128), F32)
    part = lambda *lead: pltpu.VMEM(lead + (17, 128), F32)
    square = lambda *lead: pltpu.VMEM(lead + (PANEL, 128), F32)
    tall = lambda *lead: pltpu.VMEM(lead + (sk, 128), F32)
    flat = lambda *shape: jax.ShapeDtypeStruct(shape, F32)
    swapped, panel, inner, sketches, factors, inverses = pl.pallas_call(
        reduce_kernel,
        out_shape=(
            flat(rows, width), flat(rows, PANEL), flat(4, PANEL, PANEL), flat(4, sk, PANEL),
            flat(2, PANEL, PANEL), flat(2, PANEL, PANEL),
        ),
        in_specs=[hbm] * 3,
        out_specs=(VMEM_SPEC,) * 6,
        scratch_shapes=[
            pltpu.VMEM((rows, width), F32), pltpu.VMEM((sk, rows), F32), pltpu.VMEM((1, PANEL), jnp.int32),
            pltpu.VMEM((rows, PANEL), F32), square(), square(), square(),
            pltpu.VMEM((2, rows, PANEL), F32),
            part(2 * NY), part(2 * NY), part(), part(NZX), part(), part(2 * NY),
            square(NY), square(NY), square(), tile(NZX),
            tall(NY), tall(NY), tall(), tile(NZX), block(NZX),
            dma((3,)), dma((4,)), dma((2,)), dma((4,)), dma((2, 2 * NY)), dma((2, NZX)), dma((2, 2 * NY)),
            dma((2, NY)), dma((2, NZX)), dma((2, NZX)), dma((2, NY)),
            dma((2, NY)), dma((2, NZX)), dma((2, NZX)), dma((2, NZX)), dma((2, NY)),
        ],
        compiler_params=pltpu.CompilerParams(
            collective_id=0, has_side_effects=True, vmem_limit_bytes=VMEM_REDUCE
        ),
        name="reduce",
    )(*[pltpu.with_memory_space_constraint(a, pltpu.HBM) for a in (matrix_slab, sketch_matrix, pivots)])
    return pl.pallas_call(
        update_kernel,
        out_shape=(
            flat(1, sk, width), flat(1, rows, PANEL), flat(1, PANEL, width),
            flat(1, PANEL, PANEL), flat(rows, width),
        ),
        in_specs=[VMEM_SPEC] * 6,
        out_specs=(hbm,) * 5,
        scratch_shapes=[
            pltpu.VMEM((rows, PANEL), F32), pltpu.VMEM((PANEL, width), F32),
            pltpu.VMEM((PANEL, PANEL), F32), pltpu.VMEM((rows, width), F32), dma((11,)),
        ],
        compiler_params=pltpu.CompilerParams(vmem_limit_bytes=VMEM_UPDATE),
        name="update",
    )(swapped, panel, inner, sketches, factors, inverses)


def solution(mesh):
    in_specs = (P("row", "col"), P(None, "row"), P())
    out_specs = (
        P(None, None, "col"),
        P(None, "row", None),
        P(None, None, "col"),
        P(),
        P("row", "col"),
    )
    return jax.shard_map(shards, mesh=mesh, in_specs=in_specs, out_specs=out_specs, check_vma=False)
```

```python
import functools
import math

import jax
import jax.numpy as jnp
from jax import lax
from jax.experimental import pallas as pl
from jax.experimental.pallas import tpu as pltpu
from jax.sharding import PartitionSpec as P

PANEL = 128
VMEM_REDUCE = 32 * 1024 * 1024
VMEM_UPDATE = 32 * 1024 * 1024
NY = 4
NZX = 16
NCOL = 4
MESH = pl.DeviceIdType.MESH
F32 = jnp.float32
BF16 = jnp.bfloat16
VMEM_SPEC = pl.BlockSpec(memory_space=pltpu.VMEM)


def hdot(left, right, contract=(1, 0)):
    return lax.dot_general(
        left,
        right,
        (((contract[0],), (contract[1],)), ((), ())),
        precision=lax.Precision.HIGHEST,
        preferred_element_type=F32,
    )


def bdot(left, right, contract=(1, 0)):
    return lax.dot_general(
        left, right, (((contract[0],), (contract[1],)), ((), ())), preferred_element_type=F32
    )


def select_dot(values, onehot, contract=(1, 0)):
    high = values.astype(BF16)
    rest = values - high.astype(F32)
    mid = rest.astype(BF16)
    low = (rest - mid.astype(F32)).astype(BF16)
    return (bdot(high, onehot, contract) + bdot(mid, onehot, contract)) + bdot(low, onehot, contract)


def two_sum(a, b):
    s = a + b
    t = s - a
    return s, (a - (s - t)) + (b - t)


def gram_levels(x):
    n = x.shape[1]
    sigma = jnp.max(jnp.abs(x), axis=0, keepdims=True) * 131072.0
    parts = []
    rest = x
    for _ in range(4):
        part = (rest + sigma) - sigma
        rest = rest - part
        parts.append(part.astype(BF16))
        sigma = sigma * (1.0 / 128.0)
    cat = jnp.concatenate(parts, axis=1)
    full = bdot(cat, cat, (0, 0))
    block = lambda i, j: full[i * n : (i + 1) * n, j * n : (j + 1) * n]
    return (
        block(0, 0),
        block(0, 1) + block(1, 0),
        (block(0, 2) + block(2, 0)) + block(1, 1),
        (block(0, 3) + block(3, 0)) + (block(1, 2) + block(2, 1)),
        (block(1, 3) + block(3, 1)) + block(2, 2),
    )


def pivot_onehot(piv, col_first, width):
    lanes = lax.broadcasted_iota(jnp.int32, (width, PANEL), 0) + col_first
    return jnp.where(lanes == piv, 1.0, 0.0).astype(BF16)


def swapped_columns(slab, lead, onehot):
    picked = bdot(jnp.ones((8, PANEL), BF16), onehot, (1, 1))[0:1, :]
    return jnp.where(picked > 0.5, select_dot(lead, onehot, (1, 1)), slab)


def remote(src, dst, send, recv, device):
    return pltpu.make_async_remote_copy(
        src_ref=src, dst_ref=dst, send_sem=send, recv_sem=recv, device_id=device, device_id_type=MESH
    )


def pack_symmetric(high, low):
    row = lax.broadcasted_iota(jnp.int32, (64, 128), 0)
    lane = lax.broadcasted_iota(jnp.int32, (64, 128), 1)
    join = lambda a, b: jnp.where(lane[: a.shape[0]] < 64, a, pltpu.roll(b, 64, 1))
    corner = lambda v: jnp.where(row > lane, v[:64], pltpu.roll(v[64:], 64, 1))
    diagonal = lambda v: jnp.sum(jnp.where(row == lane, v[:64], 0.0), axis=0, keepdims=True)
    packed = jnp.concatenate([join(high[64:], low[64:]), join(corner(high), corner(low))], axis=0)
    return packed, join(diagonal(high), diagonal(low))


def unpack_symmetric(packed, diagonal):
    row = lax.broadcasted_iota(jnp.int32, (64, 128), 0)
    lane = lax.broadcasted_iota(jnp.int32, (64, 128), 1)
    below, corner = packed[:64], packed[64:]
    top = jnp.where(row == lane, diagonal, corner)
    bottom = jnp.where(lane < 64, below, pltpu.roll(corner, 64, 1))
    part = jnp.concatenate([top, bottom], axis=0)
    row = lax.broadcasted_iota(jnp.int32, (128, 128), 0)
    lane = lax.broadcasted_iota(jnp.int32, (128, 128), 1)
    lower = (lane <= row) & ((row < 64) | (lane < 64))
    upper = (row >= 64) & (lane >= row)
    return jnp.where(lower | upper, part, part.T)


def reduce_kernel(
    slab_hbm, sketch_hbm, piv_hbm,
    b_ref, p_ref, gfull, sfull, r_out, x_out,
    slab_ref, sketch_ref, piv_ref,
    pk, pp, rc1, rc2, leadbuf,
    wpart, wa, wsum, wb, wtot, wfull,
    gpart, ga, gsum, gb,
    spart, sa, ssum, sb,
    sem_in, sem1, sem_p, sem_lead, wa_sem, wb_sem, wc_sem, ga_sem, gb_sem, gc_sem,
    sa_sem, sb_sem, sc_sem, sd_sem, relay,
):
    r = lax.axis_index("row")
    c = lax.axis_index("col")
    y = lax.div(r, NZX)
    w = lax.rem(r, NZX)
    core = lax.rem(c, 2)
    other_core = c + 1 - 2 * core
    other_chip = lax.rem(c + 2, NCOL)
    width = slab_ref.shape[1]
    load_piv = pltpu.make_async_copy(piv_hbm, piv_ref, sem_in.at[0])
    load_slab = pltpu.make_async_copy(slab_hbm, slab_ref, sem_in.at[1])
    load_sketch = pltpu.make_async_copy(sketch_hbm, sketch_ref, sem_in.at[2])
    load_piv.start()
    load_slab.start()
    load_sketch.start()

    y_peers = [(lax.rem(y + i, NY), i) for i in range(1, NY)]
    zx_peers = [lax.rem(w + i, NZX) for i in range(1, NZX)]
    own = y * 2 + core
    pair_peers = [lax.rem(own + i, 2 * NY) for i in range(1, 2 * NY)]

    def pair_device(t):
        return (lax.div(t, 2) * NZX + w, c - core + lax.rem(t, 2))

    barrier = pltpu.get_barrier_semaphore()
    z_step = lambda k: lax.rem(w + 2 * k + NZX, NZX)
    across = w + 1 - 2 * lax.rem(w, 2)
    for t in (z_step(2), z_step(-2), across, z_step(1), z_step(-1)):
        pl.semaphore_signal(barrier, inc=1, device_id=(y * NZX + t, c), device_id_type=MESH)
    for t in pair_peers:
        pl.semaphore_signal(barrier, inc=1, device_id=pair_device(t), device_id_type=MESH)
    for d in (other_chip, other_chip + 1 - 2 * core):
        pl.semaphore_signal(barrier, inc=1, device_id=(r, d), device_id_type=MESH)

    load_piv.wait()
    onehot = pivot_onehot(piv_ref[...], c * width, width)
    load_slab.wait()
    slab = slab_ref[...]
    pk[...] = select_dot(slab, onehot)
    load_sketch.wait()
    sketch = hdot(sketch_ref[...], slab)
    for b in range(4):
        spart[b] = sketch[:, 128 * b : 128 * b + 128]
    leadbuf[0] = slab[:, :PANEL]
    pl.semaphore_wait(barrier, 5 + 2 * NY - 1 + 2)
    for t in (z_step(2), z_step(-2)):
        pl.semaphore_signal(relay.at[0], inc=1, device_id=(y * NZX + t, c), device_id_type=MESH)

    pending = []

    def send(src, dst, send_sem, recv_sem, device):
        copy = remote(src, dst, send_sem, recv_sem, device)
        copy.start()
        pending.append(copy)

    def to_y(src, dst, sems):
        for t, _ in y_peers:
            send(src(t), dst(y), sems.at[0, t], sems.at[1, y], (t * NZX + w, c))

    def to_zx(src, dst, sems):
        for t in zx_peers:
            send(src(t), dst(w), sems.at[0, t], sems.at[1, w], (y * NZX + t, c))

    def from_y(dst, sems):
        for t, _ in y_peers:
            remote(dst(t), dst(t), sems.at[0, t], sems.at[1, t], (r, c)).wait_recv()

    def from_zx(dst, sems):
        for t in zx_peers:
            remote(dst(t), dst(t), sems.at[0, t], sems.at[1, t], (r, c)).wait_recv()

    def total_of(buf, count):
        return tree_sum([buf[k] for k in range(count)])

    def two_float_total(buf, count):
        total = buf[0]
        err = jnp.zeros_like(total)
        for k in range(1, count):
            total, e = two_sum(total, buf[k])
            err = err + e
        lanes = lax.broadcasted_iota(jnp.int32, total.shape, 1)
        return jnp.where(lanes < 64, total, total + pltpu.roll(err, 64, 1))

    mine = pl.ds(pl.multiple_of(128 * core, 128), 128)
    theirs = pl.ds(pl.multiple_of(128 - 128 * core, 128), 128)
    first = remote(pk.at[theirs], rc1, sem1.at[0], sem1.at[1], (r, other_core))
    first.start()
    to_y(lambda t: spart.at[t], lambda m: sa.at[m], sa_sem)
    sa[y] = spart[y]
    first.wait_recv()
    pp[...] = pk[mine] + rc1[...]
    second = remote(pp, rc2, sem1.at[2], sem1.at[3], (r, other_chip))
    second.start()
    lead_copies = [
        remote(leadbuf.at[0], leadbuf.at[1], sem_lead.at[j - 1], sem_lead.at[3], (r, j)) for j in range(1, NCOL)
    ]

    @pl.when(c == 0)
    def _():
        for copy in lead_copies:
            copy.start()

    second.wait_recv()
    pending.extend([first, second])
    half = pp[...] + rc2[...]
    p_ref[mine] = half
    third = remote(p_ref.at[mine], p_ref.at[mine], sem_p.at[0], sem_p.at[1], (r, other_core))
    third.start()
    pending.append(third)

    pl.semaphore_wait(relay.at[0], 2)
    pl.semaphore_signal(relay.at[1], inc=1, device_id=(y * NZX + across, c), device_id_type=MESH)

    lane = lax.broadcasted_iota(jnp.int32, (PANEL, PANEL), 1)
    l0, l1, l2, l3, l4 = gram_levels(half)
    high, low = two_sum(l0, l1)
    high, low2 = two_sum(high, l2)
    low = (low + low2) + (l3 + l4)
    packed, diagonal = pack_symmetric(high, low)
    for o in range(2 * NY):
        wpart[o, 0:16] = packed[16 * o : 16 * o + 16]
        wpart[o, 16:17] = diagonal
    for t in pair_peers:
        send(wpart.at[t], wa.at[own], wa_sem.at[0, t], wa_sem.at[1, own], pair_device(t))
    wa[own] = wpart[own]

    @pl.when(c != 0)
    def _():
        remote(leadbuf.at[0], leadbuf.at[1], sem_lead.at[0], sem_lead.at[3], (r, c)).wait_recv()

    lead = jnp.where(c == 0, leadbuf[0], leadbuf[1])
    remote(p_ref.at[theirs], p_ref.at[theirs], sem_p.at[0], sem_p.at[1], (r, c)).wait_recv()
    panel = p_ref[...]
    swapped = swapped_columns(slab, lead, onehot)
    b_ref[...] = swapped
    inner = hdot(panel, swapped, (0, 0))
    for b in range(4):
        gpart[b] = inner[:, 128 * b : 128 * b + 128]
    to_y(lambda t: gpart.at[t], lambda m: ga.at[m], ga_sem)
    ga[y] = gpart[y]

    for t in pair_peers:
        remote(wa.at[t], wa.at[t], wa_sem.at[0, t], wa_sem.at[1, t], (r, c)).wait_recv()
    wsum[...] = two_float_total(wa, 2 * NY)
    pl.semaphore_wait(relay.at[1], 1)
    to_zx(lambda t: wsum, lambda m: wb.at[m], wb_sem)
    wb[w] = wsum[...]

    from_y(lambda t: sa.at[t], sa_sem)
    total = total_of(sa, NY)
    for k in range(NZX):
        ssum[k] = total[9 * k : 9 * k + 9]
    to_zx(lambda t: ssum.at[t], lambda m: sb.at[m], sb_sem)
    sb[w] = ssum[w]

    tile = lambda t: pl.ds(pl.multiple_of(8 * t, 8), 8)
    from_y(lambda t: ga.at[t], ga_sem)
    gsum[...] = total_of(ga, NY)
    to_zx(lambda t: gsum.at[tile(t)], lambda m: gb.at[m], gb_sem)
    gb[w] = gsum[tile(w)]

    from_zx(lambda t: wb.at[t], wb_sem)
    wtot[...] = two_float_total(wb, NZX)
    for t in pair_peers:
        send(wtot, wfull.at[own], wc_sem.at[0, t], wc_sem.at[1, own], pair_device(t))
    wfull[own] = wtot[...]

    from_zx(lambda t: sb.at[t], sb_sem)
    sfull[y, w] = total_of(sb, NZX)
    to_zx(lambda t: sfull.at[y, w], lambda m: sfull.at[y, m], sc_sem)

    for t in pair_peers:
        remote(wfull.at[t], wfull.at[t], wc_sem.at[0, t], wc_sem.at[1, t], (r, c)).wait_recv()
    packed = jnp.concatenate([wfull[o, 0:16] for o in range(2 * NY)], axis=0)
    diagonal = wfull[0, 16:17]
    high = unpack_symmetric(packed, diagonal)
    low = unpack_symmetric(pltpu.roll(packed, 64, 1), pltpu.roll(diagonal, 64, 1))

    from_zx(lambda t: gb.at[t], gb_sem)
    gfull[y, tile(w)] = total_of(gb, NZX)
    row_peers = [lax.rem(r + i, NY * NZX) for i in range(1, NY * NZX)]
    for t in row_peers:
        send(gfull.at[y, tile(w)], gfull.at[y, tile(w)], gc_sem.at[0, t], gc_sem.at[1, r], (t, c))

    eliminate(high, r_out.at[0], x_out.at[0])
    r_one = r_out[0]
    x_one = x_out[0]

    from_zx(lambda t: sfull.at[y, t], sc_sem)
    to_y(lambda t: sfull.at[y], lambda m: sfull.at[m], sd_sem)

    rowi = lax.broadcasted_iota(jnp.int32, (PANEL, PANEL), 0)
    eye = jnp.where(rowi == lane, 1.0, 0.0).astype(F32)
    l0, l1, l2, l3, l4 = gram_levels(r_one)
    d, e1 = two_sum(high, -l0)
    d, e2 = two_sum(d, -l1)
    delta = (d - l2) + (((e1 + e2) + low) - (l3 + l4))
    gram_two = eye + hdot(hdot(x_one, delta), x_one, (1, 1))
    eliminate(gram_two, r_out.at[1], x_out.at[1])

    from_y(lambda t: sfull.at[t], sd_sem)
    for t in row_peers:
        piece = gfull.at[lax.div(t, NZX), tile(lax.rem(t, NZX))]
        remote(piece, piece, gc_sem.at[0, t], gc_sem.at[1, t], (r, c)).wait_recv()
    for copy in pending:
        copy.wait_send()

    @pl.when(c == 0)
    def _():
        for copy in lead_copies:
            copy.wait_send()


def tree_sum(terms):
    terms = list(terms)
    while len(terms) > 1:
        pairs = [terms[i] + terms[i + 1] for i in range(0, len(terms) - 1, 2)]
        terms = pairs + terms[len(pairs) * 2 :]
    return terms[0]


def spread(v):
    return jnp.broadcast_to(v, (8, 128))


def split_three(x):
    high = x.astype(BF16).astype(F32)
    rest = x - high
    mid = rest.astype(BF16).astype(F32)
    return high, mid, rest - mid


def thin_dot(left, right):
    l0, l1, l2 = split_three(left)
    r0, r1, r2 = split_three(right)
    lefts = jnp.concatenate([l0, l0, l1, l0, l1, l2], axis=0).astype(BF16)
    rights = jnp.concatenate([r0, r1, r0, r2, r1, r0], axis=0).astype(BF16)
    return bdot(lefts, rights, (0, 0))


def block_factor(v, first, sub, lane):
    columns = [spread(v[:, first + j : first + j + 1]) for j in range(8)]
    a = {(i, j): spread(columns[i][j : j + 1, :]) for j in range(8) for i in range(j + 1)}
    m = [[None] * 8 for _ in range(8)]
    for i in range(8):
        inv = lax.rsqrt(a[i, i])
        l = {j: a[i, j] * inv for j in range(i + 1, 8)}
        for j in range(i + 1, 8):
            for k in range(j, 8):
                a[j, k] = a[j, k] - l[j] * l[k]
        for j in range(i):
            m[i][j] = m[i][j] * inv
        m[i][i] = inv
        for k in range(i + 1, 8):
            for j in range(i + 1):
                t = l[k] * m[i][j]
                m[k][j] = -t if m[k][j] is None else m[k][j] - t
    terms = []
    inverse = jnp.zeros((8, 128), F32)
    for j in range(8):
        column = m[7][j]
        for k in range(6, j - 1, -1):
            column = jnp.where(sub <= k, m[k][j], column)
        if j > 0:
            column = jnp.where(sub < j, 0.0, column)
        terms.append(column * spread(v[j : j + 1, :]))
        inverse = jnp.where(lane == first + j, column, inverse)
    solved = tree_sum(terms)
    inside = (lane >= first) & (lane < first + 8)
    return solved, jnp.where(inside, inverse, solved), m


def eliminate(w, r_ref, x_ref):
    sub = lax.broadcasted_iota(jnp.int32, (8, 128), 0)
    lane = lax.broadcasted_iota(jnp.int32, (8, 128), 1)
    count = PANEL // 8
    blocks = [w[8 * b : 8 * b + 8, :] for b in range(count)]
    for b in range(count):
        first = 8 * b
        solved, both, m = block_factor(blocks[b], first, sub, lane)
        upper = jnp.where(lane >= first + sub, solved, 0.0)
        r_ref[first : first + 8, :] = upper
        x_ref[first : first + 8, :] = jnp.where(lane < first + 8, both, 0.0)
        if b == count - 1:
            break
        inside = (lane >= first) & (lane < first + 8)
        rows = blocks[b + 1]
        columns = [spread(rows[:, first + j : first + j + 1]) for j in range(8)]
        updates = []
        for p in range(8):
            coef = tree_sum([m[p][j] * columns[j] for j in range(p + 1)])
            updates.append(coef * spread(both[p : p + 1, :]))
        blocks[b + 1] = jnp.where(inside, 0.0, rows) - tree_sum(updates)
        if b + 2 < count:
            update = thin_dot(upper, both)
            for k in range(b + 2, count):
                blocks[k] = jnp.where(inside, 0.0, blocks[k]) - update[8 * k : 8 * k + 8, :]


def update_kernel(
    b_ref, p_ref, g_ref, s_ref, r_ref, x_ref,
    s_hbm, q_hbm, e_hbm, first_hbm, out_hbm,
    sbuf, qbuf, ebuf, fbuf, obuf, sem,
):
    lead_block = lax.axis_index("col") == 0
    copies = []
    scale = 1.0 / 128.0

    def store(k, src, dst):
        copy = pltpu.make_async_copy(src, dst, sem.at[k])
        copy.start()
        copies.append(copy)

    for k in range(4):
        for t in range(NZX):
            sbuf[9 * t : 9 * t + 9, 128 * k : 128 * k + 128] = s_ref[k, t]
    store(0, sbuf, s_hbm.at[0])
    r_one = r_ref[0]
    fbuf[...] = r_one * scale
    store(8, fbuf, first_hbm.at[0])
    inverse = hdot(x_ref[1], x_ref[0])
    basis = hdot(p_ref[...], inverse, (1, 1))
    qbuf[...] = basis * 128.0
    store(9, qbuf, q_hbm.at[0])
    r_factor = hdot(r_ref[1], r_one)
    for k in range(4):
        cols = slice(128 * k, 128 * k + 128)
        projected = hdot(inverse, g_ref[k])
        rest = b_ref[:, cols] - hdot(basis, projected)
        if k == 0:
            projected = jnp.where(lead_block, r_factor, projected)
            rest = jnp.where(lead_block, 0.0, rest)
        ebuf[:, cols] = projected * scale
        obuf[:, cols] = rest
        store(4 + k, obuf.at[:, cols], out_hbm.at[:, cols])
    store(10, ebuf, e_hbm.at[0])
    for copy in copies:
        copy.wait()


def shards(matrix_slab, sketch_matrix, pivots):
    rows, width = matrix_slab.shape
    sk = sketch_matrix.shape[0]
    dma = pltpu.SemaphoreType.DMA
    hbm = pl.BlockSpec(memory_space=pltpu.HBM)
    tile = lambda *lead: pltpu.VMEM(lead + (8, 128), F32)
    nine = lambda *lead: pltpu.VMEM(lead + (9, 128), F32)
    part = lambda *lead: pltpu.VMEM(lead + (17, 128), F32)
    square = lambda *lead: pltpu.VMEM(lead + (PANEL, 128), F32)
    tall = lambda *lead: pltpu.VMEM(lead + (sk, 128), F32)
    flat = lambda *shape: jax.ShapeDtypeStruct(shape, F32)
    swapped, panel, inner, sketches, factors, inverses = pl.pallas_call(
        reduce_kernel,
        out_shape=(
            flat(rows, width), flat(rows, PANEL), flat(4, PANEL, PANEL), flat(4, NZX, sk // NZX, PANEL),
            flat(2, PANEL, PANEL), flat(2, PANEL, PANEL),
        ),
        in_specs=[hbm] * 3,
        out_specs=(VMEM_SPEC,) * 6,
        scratch_shapes=[
            pltpu.VMEM((rows, width), F32), pltpu.VMEM((sk, rows), F32), pltpu.VMEM((1, PANEL), jnp.int32),
            pltpu.VMEM((rows, PANEL), F32), square(), square(), square(),
            pltpu.VMEM((2, rows, PANEL), F32),
            part(2 * NY), part(2 * NY), part(), part(NZX), part(), part(2 * NY),
            square(NY), square(NY), square(), tile(NZX),
            tall(NY), tall(NY), nine(NZX), nine(NZX),
            dma((3,)), dma((4,)), dma((2,)), dma((4,)), dma((2, 2 * NY)), dma((2, NZX)), dma((2, 2 * NY)),
            dma((2, NY)), dma((2, NZX)), dma((2, NY * NZX)),
            dma((2, NY)), dma((2, NZX)), dma((2, NZX)), dma((2, NY)), pltpu.SemaphoreType.REGULAR((2,)),
        ],
        compiler_params=pltpu.CompilerParams(
            collective_id=0, has_side_effects=True, vmem_limit_bytes=VMEM_REDUCE
        ),
        name="reduce",
    )(*[pltpu.with_memory_space_constraint(a, pltpu.HBM) for a in (matrix_slab, sketch_matrix, pivots)])
    return pl.pallas_call(
        update_kernel,
        out_shape=(
            flat(1, sk, width), flat(1, rows, PANEL), flat(1, PANEL, width),
            flat(1, PANEL, PANEL), flat(rows, width),
        ),
        in_specs=[VMEM_SPEC] * 6,
        out_specs=(hbm,) * 5,
        scratch_shapes=[
            pltpu.VMEM((sk, width), F32), pltpu.VMEM((rows, PANEL), F32), pltpu.VMEM((PANEL, width), F32),
            pltpu.VMEM((PANEL, PANEL), F32), pltpu.VMEM((rows, width), F32), dma((11,)),
        ],
        compiler_params=pltpu.CompilerParams(vmem_limit_bytes=VMEM_UPDATE),
        name="update",
    )(swapped, panel, inner, sketches, factors, inverses)


def solution(mesh):
    in_specs = (P("row", "col"), P(None, "row"), P())
    out_specs = (
        P(None, None, "col"),
        P(None, "row", None),
        P(None, None, "col"),
        P(),
        P("row", "col"),
    )
    return jax.shard_map(shards, mesh=mesh, in_specs=in_specs, out_specs=out_specs, check_vma=False)
```

```python
import functools
import math

import jax
import jax.numpy as jnp
from jax import lax
from jax.experimental import pallas as pl
from jax.experimental.pallas import tpu as pltpu
from jax.sharding import PartitionSpec as P

PANEL = 128
VMEM_REDUCE = 32 * 1024 * 1024
VMEM_UPDATE = 32 * 1024 * 1024
NY = 4
NZX = 16
NCOL = 4
MESH = pl.DeviceIdType.MESH
F32 = jnp.float32
BF16 = jnp.bfloat16
VMEM_SPEC = pl.BlockSpec(memory_space=pltpu.VMEM)


def hdot(left, right, contract=(1, 0)):
    return lax.dot_general(
        left,
        right,
        (((contract[0],), (contract[1],)), ((), ())),
        precision=lax.Precision.HIGHEST,
        preferred_element_type=F32,
    )


def bdot(left, right, contract=(1, 0)):
    return lax.dot_general(
        left, right, (((contract[0],), (contract[1],)), ((), ())), preferred_element_type=F32
    )


def select_dot(values, onehot, contract=(1, 0)):
    high = values.astype(BF16)
    rest = values - high.astype(F32)
    mid = rest.astype(BF16)
    low = (rest - mid.astype(F32)).astype(BF16)
    return (bdot(high, onehot, contract) + bdot(mid, onehot, contract)) + bdot(low, onehot, contract)


def two_sum(a, b):
    s = a + b
    t = s - a
    return s, (a - (s - t)) + (b - t)


def gram_levels(x):
    n = x.shape[1]
    sigma = jnp.max(jnp.abs(x), axis=0, keepdims=True) * 131072.0
    parts = []
    rest = x
    for _ in range(4):
        part = (rest + sigma) - sigma
        rest = rest - part
        parts.append(part.astype(BF16))
        sigma = sigma * (1.0 / 128.0)
    cat = jnp.concatenate(parts, axis=1)
    full = bdot(cat, cat, (0, 0))
    block = lambda i, j: full[i * n : (i + 1) * n, j * n : (j + 1) * n]
    return (
        block(0, 0),
        block(0, 1) + block(1, 0),
        (block(0, 2) + block(2, 0)) + block(1, 1),
        (block(0, 3) + block(3, 0)) + (block(1, 2) + block(2, 1)),
        (block(1, 3) + block(3, 1)) + block(2, 2),
    )


def pivot_onehot(piv, col_first, width):
    lanes = lax.broadcasted_iota(jnp.int32, (width, PANEL), 0) + col_first
    return jnp.where(lanes == piv, 1.0, 0.0).astype(BF16)


def swapped_columns(slab, lead, onehot):
    picked = bdot(jnp.ones((8, PANEL), BF16), onehot, (1, 1))[0:1, :]
    return jnp.where(picked > 0.5, select_dot(lead, onehot, (1, 1)), slab)


def remote(src, dst, send, recv, device):
    return pltpu.make_async_remote_copy(
        src_ref=src, dst_ref=dst, send_sem=send, recv_sem=recv, device_id=device, device_id_type=MESH
    )


def pack_symmetric(high, low):
    row = lax.broadcasted_iota(jnp.int32, (64, 128), 0)
    lane = lax.broadcasted_iota(jnp.int32, (64, 128), 1)
    join = lambda a, b: jnp.where(lane[: a.shape[0]] < 64, a, pltpu.roll(b, 64, 1))
    corner = lambda v: jnp.where(row > lane, v[:64], pltpu.roll(v[64:], 64, 1))
    diagonal = lambda v: jnp.sum(jnp.where(row == lane, v[:64], 0.0), axis=0, keepdims=True)
    packed = jnp.concatenate([join(high[64:], low[64:]), join(corner(high), corner(low))], axis=0)
    return packed, join(diagonal(high), diagonal(low))


def unpack_symmetric(packed, diagonal):
    row = lax.broadcasted_iota(jnp.int32, (64, 128), 0)
    lane = lax.broadcasted_iota(jnp.int32, (64, 128), 1)
    below, corner = packed[:64], packed[64:]
    top = jnp.where(row == lane, diagonal, corner)
    bottom = jnp.where(lane < 64, below, pltpu.roll(corner, 64, 1))
    part = jnp.concatenate([top, bottom], axis=0)
    row = lax.broadcasted_iota(jnp.int32, (128, 128), 0)
    lane = lax.broadcasted_iota(jnp.int32, (128, 128), 1)
    lower = (lane <= row) & ((row < 64) | (lane < 64))
    upper = (row >= 64) & (lane >= row)
    return jnp.where(lower | upper, part, part.T)


def reduce_kernel(
    slab_hbm, sketch_hbm, piv_hbm,
    b_ref, p_ref, gfull, sfull, r_out, x_out,
    slab_ref, sketch_ref, piv_ref,
    pk, pp, rc1, rc2, leadbuf,
    wpart, wa, wsum, wb, wtot, wfull,
    gpart, ga, gsum, gb,
    spart, sa, ssum, sb,
    sem_in, sem1, sem_p, sem_lead, wa_sem, wb_sem, wc_sem, ga_sem, gb_sem, gc_sem,
    sa_sem, sb_sem, sc_sem, sd_sem, relay,
):
    r = lax.axis_index("row")
    c = lax.axis_index("col")
    y = lax.div(r, NZX)
    w = lax.rem(r, NZX)
    core = lax.rem(c, 2)
    other_core = c + 1 - 2 * core
    other_chip = lax.rem(c + 2, NCOL)
    width = slab_ref.shape[1]
    load_piv = pltpu.make_async_copy(piv_hbm, piv_ref, sem_in.at[0])
    load_slab = pltpu.make_async_copy(slab_hbm, slab_ref, sem_in.at[1])
    load_sketch = pltpu.make_async_copy(sketch_hbm, sketch_ref, sem_in.at[2])
    load_piv.start()
    load_slab.start()
    load_sketch.start()

    y_peers = [(lax.rem(y + i, NY), i) for i in range(1, NY)]
    zx_peers = [lax.rem(w + i, NZX) for i in range(1, NZX)]
    own = y * 2 + core
    pair_peers = [lax.rem(own + i, 2 * NY) for i in range(1, 2 * NY)]

    def pair_device(t):
        return (lax.div(t, 2) * NZX + w, c - core + lax.rem(t, 2))

    barrier = pltpu.get_barrier_semaphore()
    z_step = lambda k: lax.rem(w + 2 * k + NZX, NZX)
    across = w + 1 - 2 * lax.rem(w, 2)
    for t in (z_step(2), z_step(-2), across, z_step(1), z_step(-1)):
        pl.semaphore_signal(barrier, inc=1, device_id=(y * NZX + t, c), device_id_type=MESH)
    for t in pair_peers:
        pl.semaphore_signal(barrier, inc=1, device_id=pair_device(t), device_id_type=MESH)
    for d in (other_chip, other_chip + 1 - 2 * core):
        pl.semaphore_signal(barrier, inc=1, device_id=(r, d), device_id_type=MESH)

    load_piv.wait()
    onehot = pivot_onehot(piv_ref[...], c * width, width)
    load_slab.wait()
    slab = slab_ref[...]
    pk[...] = select_dot(slab, onehot)
    load_sketch.wait()
    sketch = hdot(sketch_ref[...], slab)
    for b in range(4):
        spart[b] = sketch[:, 128 * b : 128 * b + 128]
    leadbuf[0] = slab[:, :PANEL]
    pl.semaphore_wait(barrier, 5 + 2 * NY - 1 + 2)
    for t in (z_step(2), z_step(-2)):
        pl.semaphore_signal(relay.at[0], inc=1, device_id=(y * NZX + t, c), device_id_type=MESH)

    pending = []

    def send(src, dst, send_sem, recv_sem, device):
        copy = remote(src, dst, send_sem, recv_sem, device)
        copy.start()
        pending.append(copy)

    def to_y(src, dst, sems):
        for t, _ in y_peers:
            send(src(t), dst(y), sems.at[0, t], sems.at[1, y], (t * NZX + w, c))

    def to_zx(src, dst, sems):
        for t in zx_peers:
            send(src(t), dst(w), sems.at[0, t], sems.at[1, w], (y * NZX + t, c))

    def from_y(dst, sems):
        for t, _ in y_peers:
            remote(dst(t), dst(t), sems.at[0, t], sems.at[1, t], (r, c)).wait_recv()

    def from_zx(dst, sems):
        for t in zx_peers:
            remote(dst(t), dst(t), sems.at[0, t], sems.at[1, t], (r, c)).wait_recv()

    def total_of(buf, count):
        return tree_sum([buf[k] for k in range(count)])

    def two_float_total(buf, count):
        total = buf[0]
        err = jnp.zeros_like(total)
        for k in range(1, count):
            total, e = two_sum(total, buf[k])
            err = err + e
        lanes = lax.broadcasted_iota(jnp.int32, total.shape, 1)
        return jnp.where(lanes < 64, total, total + pltpu.roll(err, 64, 1))

    mine = pl.ds(pl.multiple_of(128 * core, 128), 128)
    theirs = pl.ds(pl.multiple_of(128 - 128 * core, 128), 128)
    first = remote(pk.at[theirs], rc1, sem1.at[0], sem1.at[1], (r, other_core))
    first.start()
    to_y(lambda t: spart.at[t], lambda m: sa.at[m], sa_sem)
    sa[y] = spart[y]
    first.wait_recv()
    pp[...] = pk[mine] + rc1[...]
    second = remote(pp, rc2, sem1.at[2], sem1.at[3], (r, other_chip))
    second.start()
    lead_copies = [
        remote(leadbuf.at[0], leadbuf.at[1], sem_lead.at[j - 1], sem_lead.at[3], (r, j)) for j in range(1, NCOL)
    ]

    @pl.when(c == 0)
    def _():
        for copy in lead_copies:
            copy.start()

    second.wait_recv()
    pending.extend([first, second])
    half = pp[...] + rc2[...]
    p_ref[mine] = half
    third = remote(p_ref.at[mine], p_ref.at[mine], sem_p.at[0], sem_p.at[1], (r, other_core))
    third.start()
    pending.append(third)

    pl.semaphore_wait(relay.at[0], 2)
    pl.semaphore_signal(relay.at[1], inc=1, device_id=(y * NZX + across, c), device_id_type=MESH)

    lane = lax.broadcasted_iota(jnp.int32, (PANEL, PANEL), 1)
    l0, l1, l2, l3, l4 = gram_levels(half)
    high, low = two_sum(l0, l1)
    high, low2 = two_sum(high, l2)
    low = (low + low2) + (l3 + l4)
    packed, diagonal = pack_symmetric(high, low)
    for o in range(2 * NY):
        wpart[o, 0:16] = packed[16 * o : 16 * o + 16]
        wpart[o, 16:17] = diagonal
    for t in pair_peers:
        send(wpart.at[t], wa.at[own], wa_sem.at[0, t], wa_sem.at[1, own], pair_device(t))
    wa[own] = wpart[own]

    @pl.when(c != 0)
    def _():
        remote(leadbuf.at[0], leadbuf.at[1], sem_lead.at[0], sem_lead.at[3], (r, c)).wait_recv()

    lead = jnp.where(c == 0, leadbuf[0], leadbuf[1])
    remote(p_ref.at[theirs], p_ref.at[theirs], sem_p.at[0], sem_p.at[1], (r, c)).wait_recv()
    panel = p_ref[...]
    swapped = swapped_columns(slab, lead, onehot)
    b_ref[...] = swapped
    inner = hdot(panel, swapped, (0, 0))
    for b in range(4):
        gpart[b] = inner[:, 128 * b : 128 * b + 128]
    to_y(lambda t: gpart.at[t], lambda m: ga.at[m], ga_sem)
    ga[y] = gpart[y]

    pl.semaphore_wait(relay.at[1], 1)
    from_y(lambda t: sa.at[t], sa_sem)
    total = total_of(sa, NY)
    for k in range(NZX):
        ssum[k] = total[9 * k : 9 * k + 9]
    to_zx(lambda t: ssum.at[t], lambda m: sb.at[m], sb_sem)
    sb[w] = ssum[w]

    for t in pair_peers:
        remote(wa.at[t], wa.at[t], wa_sem.at[0, t], wa_sem.at[1, t], (r, c)).wait_recv()
    wsum[...] = two_float_total(wa, 2 * NY)
    to_zx(lambda t: wsum, lambda m: wb.at[m], wb_sem)
    wb[w] = wsum[...]

    tile = lambda t: pl.ds(pl.multiple_of(8 * t, 8), 8)
    from_y(lambda t: ga.at[t], ga_sem)
    gsum[...] = total_of(ga, NY)
    to_zx(lambda t: gsum.at[tile(t)], lambda m: gb.at[m], gb_sem)
    gb[w] = gsum[tile(w)]

    from_zx(lambda t: sb.at[t], sb_sem)
    sfull[y, w] = total_of(sb, NZX)
    to_zx(lambda t: sfull.at[y, w], lambda m: sfull.at[y, m], sc_sem)

    from_zx(lambda t: wb.at[t], wb_sem)
    wtot[...] = two_float_total(wb, NZX)
    for t in pair_peers:
        send(wtot, wfull.at[own], wc_sem.at[0, t], wc_sem.at[1, own], pair_device(t))
    wfull[own] = wtot[...]

    for t in pair_peers:
        remote(wfull.at[t], wfull.at[t], wc_sem.at[0, t], wc_sem.at[1, t], (r, c)).wait_recv()
    packed = jnp.concatenate([wfull[o, 0:16] for o in range(2 * NY)], axis=0)
    diagonal = wfull[0, 16:17]
    high = unpack_symmetric(packed, diagonal)
    low = unpack_symmetric(pltpu.roll(packed, 64, 1), pltpu.roll(diagonal, 64, 1))

    from_zx(lambda t: gb.at[t], gb_sem)
    gfull[y, tile(w)] = total_of(gb, NZX)
    row_peers = [lax.rem(r + i, NY * NZX) for i in range(1, NY * NZX)]
    for t in row_peers:
        send(gfull.at[y, tile(w)], gfull.at[y, tile(w)], gc_sem.at[0, t], gc_sem.at[1, r], (t, c))

    def sketch_home():
        from_zx(lambda t: sfull.at[y, t], sc_sem)
        to_y(lambda t: sfull.at[y], lambda m: sfull.at[m], sd_sem)

    eliminate(high, r_out.at[0], x_out.at[0], {4: sketch_home})
    r_one = r_out[0]
    x_one = x_out[0]

    rowi = lax.broadcasted_iota(jnp.int32, (PANEL, PANEL), 0)
    eye = jnp.where(rowi == lane, 1.0, 0.0).astype(F32)
    l0, l1, l2, l3, l4 = gram_levels(r_one)
    d, e1 = two_sum(high, -l0)
    d, e2 = two_sum(d, -l1)
    delta = (d - l2) + (((e1 + e2) + low) - (l3 + l4))
    gram_two = eye + hdot(hdot(x_one, delta), x_one, (1, 1))
    eliminate(gram_two, r_out.at[1], x_out.at[1])

    from_y(lambda t: sfull.at[t], sd_sem)
    for t in row_peers:
        piece = gfull.at[lax.div(t, NZX), tile(lax.rem(t, NZX))]
        remote(piece, piece, gc_sem.at[0, t], gc_sem.at[1, t], (r, c)).wait_recv()
    for copy in pending:
        copy.wait_send()

    @pl.when(c == 0)
    def _():
        for copy in lead_copies:
            copy.wait_send()


def tree_sum(terms):
    terms = list(terms)
    while len(terms) > 1:
        pairs = [terms[i] + terms[i + 1] for i in range(0, len(terms) - 1, 2)]
        terms = pairs + terms[len(pairs) * 2 :]
    return terms[0]


def spread(v):
    return jnp.broadcast_to(v, (8, 128))


def split_three(x):
    high = x.astype(BF16).astype(F32)
    rest = x - high
    mid = rest.astype(BF16).astype(F32)
    return high, mid, rest - mid


def thin_dot(left, right):
    l0, l1, l2 = split_three(left)
    r0, r1, r2 = split_three(right)
    lefts = jnp.concatenate([l0, l0, l1, l0, l1, l2], axis=0).astype(BF16)
    rights = jnp.concatenate([r0, r1, r0, r2, r1, r0], axis=0).astype(BF16)
    return bdot(lefts, rights, (0, 0))


def block_factor(v, first, sub, lane):
    columns = [spread(v[:, first + j : first + j + 1]) for j in range(8)]
    a = {(i, j): spread(columns[i][j : j + 1, :]) for j in range(8) for i in range(j + 1)}
    m = [[None] * 8 for _ in range(8)]
    for i in range(8):
        inv = lax.rsqrt(a[i, i])
        l = {j: a[i, j] * inv for j in range(i + 1, 8)}
        for j in range(i + 1, 8):
            for k in range(j, 8):
                a[j, k] = a[j, k] - l[j] * l[k]
        for j in range(i):
            m[i][j] = m[i][j] * inv
        m[i][i] = inv
        for k in range(i + 1, 8):
            for j in range(i + 1):
                t = l[k] * m[i][j]
                m[k][j] = -t if m[k][j] is None else m[k][j] - t
    terms = []
    inverse = jnp.zeros((8, 128), F32)
    for j in range(8):
        column = m[7][j]
        for k in range(6, j - 1, -1):
            column = jnp.where(sub <= k, m[k][j], column)
        if j > 0:
            column = jnp.where(sub < j, 0.0, column)
        terms.append(column * spread(v[j : j + 1, :]))
        inverse = jnp.where(lane == first + j, column, inverse)
    solved = tree_sum(terms)
    inside = (lane >= first) & (lane < first + 8)
    return solved, jnp.where(inside, inverse, solved), m


def eliminate(w, r_ref, x_ref, between={}):
    sub = lax.broadcasted_iota(jnp.int32, (8, 128), 0)
    lane = lax.broadcasted_iota(jnp.int32, (8, 128), 1)
    count = PANEL // 8
    blocks = [w[8 * b : 8 * b + 8, :] for b in range(count)]
    for b in range(count):
        if b in between:
            between[b]()
        first = 8 * b
        solved, both, m = block_factor(blocks[b], first, sub, lane)
        upper = jnp.where(lane >= first + sub, solved, 0.0)
        r_ref[first : first + 8, :] = upper
        x_ref[first : first + 8, :] = jnp.where(lane < first + 8, both, 0.0)
        if b == count - 1:
            break
        inside = (lane >= first) & (lane < first + 8)
        rows = blocks[b + 1]
        columns = [spread(rows[:, first + j : first + j + 1]) for j in range(8)]
        updates = []
        for p in range(8):
            coef = tree_sum([m[p][j] * columns[j] for j in range(p + 1)])
            updates.append(coef * spread(both[p : p + 1, :]))
        blocks[b + 1] = jnp.where(inside, 0.0, rows) - tree_sum(updates)
        if b + 2 < count:
            update = thin_dot(upper, both)
            for k in range(b + 2, count):
                blocks[k] = jnp.where(inside, 0.0, blocks[k]) - update[8 * k : 8 * k + 8, :]


def update_kernel(
    b_ref, p_ref, g_ref, s_ref, r_ref, x_ref,
    s_hbm, q_hbm, e_hbm, first_hbm, out_hbm,
    sbuf, qbuf, ebuf, fbuf, obuf, sem,
):
    lead_block = lax.axis_index("col") == 0
    copies = []
    scale = 1.0 / 128.0

    def store(k, src, dst):
        copy = pltpu.make_async_copy(src, dst, sem.at[k])
        copy.start()
        copies.append(copy)

    for k in range(4):
        for t in range(NZX):
            sbuf[9 * t : 9 * t + 9, 128 * k : 128 * k + 128] = s_ref[k, t]
    store(0, sbuf, s_hbm.at[0])
    r_one = r_ref[0]
    fbuf[...] = r_one * scale
    store(8, fbuf, first_hbm.at[0])
    inverse = hdot(x_ref[1], x_ref[0])
    basis = hdot(p_ref[...], inverse, (1, 1))
    qbuf[...] = basis * 128.0
    store(9, qbuf, q_hbm.at[0])
    r_factor = hdot(r_ref[1], r_one)
    for k in range(4):
        cols = slice(128 * k, 128 * k + 128)
        projected = hdot(inverse, g_ref[k])
        rest = b_ref[:, cols] - hdot(basis, projected)
        if k == 0:
            projected = jnp.where(lead_block, r_factor, projected)
            rest = jnp.where(lead_block, 0.0, rest)
        ebuf[:, cols] = projected * scale
        obuf[:, cols] = rest
        store(4 + k, obuf.at[:, cols], out_hbm.at[:, cols])
    store(10, ebuf, e_hbm.at[0])
    for copy in copies:
        copy.wait()


def shards(matrix_slab, sketch_matrix, pivots):
    rows, width = matrix_slab.shape
    sk = sketch_matrix.shape[0]
    dma = pltpu.SemaphoreType.DMA
    hbm = pl.BlockSpec(memory_space=pltpu.HBM)
    tile = lambda *lead: pltpu.VMEM(lead + (8, 128), F32)
    nine = lambda *lead: pltpu.VMEM(lead + (9, 128), F32)
    part = lambda *lead: pltpu.VMEM(lead + (17, 128), F32)
    square = lambda *lead: pltpu.VMEM(lead + (PANEL, 128), F32)
    tall = lambda *lead: pltpu.VMEM(lead + (sk, 128), F32)
    flat = lambda *shape: jax.ShapeDtypeStruct(shape, F32)
    swapped, panel, inner, sketches, factors, inverses = pl.pallas_call(
        reduce_kernel,
        out_shape=(
            flat(rows, width), flat(rows, PANEL), flat(4, PANEL, PANEL), flat(4, NZX, sk // NZX, PANEL),
            flat(2, PANEL, PANEL), flat(2, PANEL, PANEL),
        ),
        in_specs=[hbm] * 3,
        out_specs=(VMEM_SPEC,) * 6,
        scratch_shapes=[
            pltpu.VMEM((rows, width), F32), pltpu.VMEM((sk, rows), F32), pltpu.VMEM((1, PANEL), jnp.int32),
            pltpu.VMEM((rows, PANEL), F32), square(), square(), square(),
            pltpu.VMEM((2, rows, PANEL), F32),
            part(2 * NY), part(2 * NY), part(), part(NZX), part(), part(2 * NY),
            square(NY), square(NY), square(), tile(NZX),
            tall(NY), tall(NY), nine(NZX), nine(NZX),
            dma((3,)), dma((4,)), dma((2,)), dma((4,)), dma((2, 2 * NY)), dma((2, NZX)), dma((2, 2 * NY)),
            dma((2, NY)), dma((2, NZX)), dma((2, NY * NZX)),
            dma((2, NY)), dma((2, NZX)), dma((2, NZX)), dma((2, NY)), pltpu.SemaphoreType.REGULAR((2,)),
        ],
        compiler_params=pltpu.CompilerParams(
            collective_id=0, has_side_effects=True, vmem_limit_bytes=VMEM_REDUCE
        ),
        name="reduce",
    )(*[pltpu.with_memory_space_constraint(a, pltpu.HBM) for a in (matrix_slab, sketch_matrix, pivots)])
    return pl.pallas_call(
        update_kernel,
        out_shape=(
            flat(1, sk, width), flat(1, rows, PANEL), flat(1, PANEL, width),
            flat(1, PANEL, PANEL), flat(rows, width),
        ),
        in_specs=[VMEM_SPEC] * 6,
        out_specs=(hbm,) * 5,
        scratch_shapes=[
            pltpu.VMEM((sk, width), F32), pltpu.VMEM((rows, PANEL), F32), pltpu.VMEM((PANEL, width), F32),
            pltpu.VMEM((PANEL, PANEL), F32), pltpu.VMEM((rows, width), F32), dma((11,)),
        ],
        compiler_params=pltpu.CompilerParams(vmem_limit_bytes=VMEM_UPDATE),
        name="update",
    )(swapped, panel, inner, sketches, factors, inverses)


def solution(mesh):
    in_specs = (P("row", "col"), P(None, "row"), P())
    out_specs = (
        P(None, None, "col"),
        P(None, "row", None),
        P(None, None, "col"),
        P(),
        P("row", "col"),
    )
    return jax.shard_map(shards, mesh=mesh, in_specs=in_specs, out_specs=out_specs, check_vma=False)
```

```python
import functools
import math

import jax
import jax.numpy as jnp
from jax import lax
from jax.experimental import pallas as pl
from jax.experimental.pallas import tpu as pltpu
from jax.sharding import PartitionSpec as P

PANEL = 128
VMEM_REDUCE = 32 * 1024 * 1024
VMEM_UPDATE = 32 * 1024 * 1024
NY = 4
NZX = 16
NCOL = 4
MESH = pl.DeviceIdType.MESH
F32 = jnp.float32
BF16 = jnp.bfloat16
VMEM_SPEC = pl.BlockSpec(memory_space=pltpu.VMEM)


def hdot(left, right, contract=(1, 0)):
    return lax.dot_general(
        left,
        right,
        (((contract[0],), (contract[1],)), ((), ())),
        precision=lax.Precision.HIGHEST,
        preferred_element_type=F32,
    )


def bdot(left, right, contract=(1, 0)):
    return lax.dot_general(
        left, right, (((contract[0],), (contract[1],)), ((), ())), preferred_element_type=F32
    )


def select_dot(values, onehot, contract=(1, 0)):
    high = values.astype(BF16)
    rest = values - high.astype(F32)
    mid = rest.astype(BF16)
    low = (rest - mid.astype(F32)).astype(BF16)
    return (bdot(high, onehot, contract) + bdot(mid, onehot, contract)) + bdot(low, onehot, contract)


def two_sum(a, b):
    s = a + b
    t = s - a
    return s, (a - (s - t)) + (b - t)


def gram_levels(x):
    n = x.shape[1]
    sigma = jnp.max(jnp.abs(x), axis=0, keepdims=True) * 131072.0
    parts = []
    rest = x
    for _ in range(4):
        part = (rest + sigma) - sigma
        rest = rest - part
        parts.append(part.astype(BF16))
        sigma = sigma * (1.0 / 128.0)
    cat = jnp.concatenate(parts, axis=1)
    full = bdot(cat, cat, (0, 0))
    block = lambda i, j: full[i * n : (i + 1) * n, j * n : (j + 1) * n]
    return (
        block(0, 0),
        block(0, 1) + block(1, 0),
        (block(0, 2) + block(2, 0)) + block(1, 1),
        (block(0, 3) + block(3, 0)) + (block(1, 2) + block(2, 1)),
        (block(1, 3) + block(3, 1)) + block(2, 2),
    )


def pivot_onehot(piv, col_first, width):
    lanes = lax.broadcasted_iota(jnp.int32, (width, PANEL), 0) + col_first
    return jnp.where(lanes == piv, 1.0, 0.0).astype(BF16)


def swapped_columns(slab, lead, onehot):
    picked = bdot(jnp.ones((8, PANEL), BF16), onehot, (1, 1))[0:1, :]
    return jnp.where(picked > 0.5, select_dot(lead, onehot, (1, 1)), slab)


def remote(src, dst, send, recv, device):
    return pltpu.make_async_remote_copy(
        src_ref=src, dst_ref=dst, send_sem=send, recv_sem=recv, device_id=device, device_id_type=MESH
    )


def pack_symmetric(high, low):
    row = lax.broadcasted_iota(jnp.int32, (64, 128), 0)
    lane = lax.broadcasted_iota(jnp.int32, (64, 128), 1)
    join = lambda a, b: jnp.where(lane[: a.shape[0]] < 64, a, pltpu.roll(b, 64, 1))
    corner = lambda v: jnp.where(row > lane, v[:64], pltpu.roll(v[64:], 64, 1))
    diagonal = lambda v: jnp.sum(jnp.where(row == lane, v[:64], 0.0), axis=0, keepdims=True)
    packed = jnp.concatenate([join(high[64:], low[64:]), join(corner(high), corner(low))], axis=0)
    return packed, join(diagonal(high), diagonal(low))


def unpack_symmetric(packed, diagonal):
    row = lax.broadcasted_iota(jnp.int32, (64, 128), 0)
    lane = lax.broadcasted_iota(jnp.int32, (64, 128), 1)
    below, corner = packed[:64], packed[64:]
    top = jnp.where(row == lane, diagonal, corner)
    bottom = jnp.where(lane < 64, below, pltpu.roll(corner, 64, 1))
    part = jnp.concatenate([top, bottom], axis=0)
    row = lax.broadcasted_iota(jnp.int32, (128, 128), 0)
    lane = lax.broadcasted_iota(jnp.int32, (128, 128), 1)
    lower = (lane <= row) & ((row < 64) | (lane < 64))
    upper = (row >= 64) & (lane >= row)
    return jnp.where(lower | upper, part, part.T)


def reduce_kernel(
    slab_hbm, sketch_hbm, piv_hbm,
    b_ref, q_ref, gfull, sfull, first_ref, rfac_ref, inv_ref,
    slab_ref, sketch_ref, piv_ref, p_ref, r_out, x_out, held,
    pk, pp, rc1, rc2, leadbuf,
    wpart, wa, wsum, wb, wtot, wfull,
    gpart, ga, gsum, gb,
    spart, sa, ssum, sb,
    sem_in, sem1, sem_p, sem_lead, wa_sem, wb_sem, wc_sem, ga_sem, gb_sem, gc_sem,
    sa_sem, sb_sem, sc_sem, sd_sem, relay,
):
    r = lax.axis_index("row")
    c = lax.axis_index("col")
    y = lax.div(r, NZX)
    w = lax.rem(r, NZX)
    core = lax.rem(c, 2)
    other_core = c + 1 - 2 * core
    other_chip = lax.rem(c + 2, NCOL)
    width = slab_ref.shape[1]
    load_piv = pltpu.make_async_copy(piv_hbm, piv_ref, sem_in.at[0])
    load_slab = pltpu.make_async_copy(slab_hbm, slab_ref, sem_in.at[1])
    load_sketch = pltpu.make_async_copy(sketch_hbm, sketch_ref, sem_in.at[2])
    load_piv.start()
    load_slab.start()
    load_sketch.start()

    y_peers = [(lax.rem(y + i, NY), i) for i in range(1, NY)]
    zx_peers = [lax.rem(w + i, NZX) for i in range(1, NZX)]
    own = y * 2 + core
    pair_peers = [lax.rem(own + i, 2 * NY) for i in range(1, 2 * NY)]

    def pair_device(t):
        return (lax.div(t, 2) * NZX + w, c - core + lax.rem(t, 2))

    barrier = pltpu.get_barrier_semaphore()
    z_step = lambda k: lax.rem(w + 2 * k + NZX, NZX)
    across = w + 1 - 2 * lax.rem(w, 2)
    for t in (z_step(2), z_step(-2), across, z_step(1), z_step(-1)):
        pl.semaphore_signal(barrier, inc=1, device_id=(y * NZX + t, c), device_id_type=MESH)
    for t in pair_peers:
        pl.semaphore_signal(barrier, inc=1, device_id=pair_device(t), device_id_type=MESH)
    for d in (other_chip, other_chip + 1 - 2 * core):
        pl.semaphore_signal(barrier, inc=1, device_id=(r, d), device_id_type=MESH)

    load_piv.wait()
    onehot = pivot_onehot(piv_ref[...], c * width, width)
    load_slab.wait()
    slab = slab_ref[...]
    pk[...] = select_dot(slab, onehot)
    load_sketch.wait()
    sketch = hdot(sketch_ref[...], slab)
    for b in range(4):
        spart[b] = sketch[:, 128 * b : 128 * b + 128]
    leadbuf[0] = slab[:, :PANEL]
    pl.semaphore_wait(barrier, 5 + 2 * NY - 1 + 2)
    for t in (z_step(2), z_step(-2)):
        pl.semaphore_signal(relay.at[0], inc=1, device_id=(y * NZX + t, c), device_id_type=MESH)

    pending = []

    def send(src, dst, send_sem, recv_sem, device):
        copy = remote(src, dst, send_sem, recv_sem, device)
        copy.start()
        pending.append(copy)

    def to_y(src, dst, sems):
        for t, _ in y_peers:
            send(src(t), dst(y), sems.at[0, t], sems.at[1, y], (t * NZX + w, c))

    def to_zx(src, dst, sems):
        for t in zx_peers:
            send(src(t), dst(w), sems.at[0, t], sems.at[1, w], (y * NZX + t, c))

    def from_y(dst, sems):
        for t, _ in y_peers:
            remote(dst(t), dst(t), sems.at[0, t], sems.at[1, t], (r, c)).wait_recv()

    def from_zx(dst, sems):
        for t in zx_peers:
            remote(dst(t), dst(t), sems.at[0, t], sems.at[1, t], (r, c)).wait_recv()

    def total_of(buf, count):
        return tree_sum([buf[k] for k in range(count)])

    def two_float_total(buf, count):
        total = buf[0]
        err = jnp.zeros_like(total)
        for k in range(1, count):
            total, e = two_sum(total, buf[k])
            err = err + e
        lanes = lax.broadcasted_iota(jnp.int32, total.shape, 1)
        return jnp.where(lanes < 64, total, total + pltpu.roll(err, 64, 1))

    mine = pl.ds(pl.multiple_of(128 * core, 128), 128)
    theirs = pl.ds(pl.multiple_of(128 - 128 * core, 128), 128)
    first = remote(pk.at[theirs], rc1, sem1.at[0], sem1.at[1], (r, other_core))
    first.start()
    to_y(lambda t: spart.at[t], lambda m: sa.at[m], sa_sem)
    sa[y] = spart[y]
    first.wait_recv()
    pp[...] = pk[mine] + rc1[...]
    second = remote(pp, rc2, sem1.at[2], sem1.at[3], (r, other_chip))
    second.start()
    lead_copies = [
        remote(leadbuf.at[0], leadbuf.at[1], sem_lead.at[j - 1], sem_lead.at[3], (r, j)) for j in range(1, NCOL)
    ]

    @pl.when(c == 0)
    def _():
        for copy in lead_copies:
            copy.start()

    second.wait_recv()
    pending.extend([first, second])
    half = pp[...] + rc2[...]
    p_ref[mine] = half
    third = remote(p_ref.at[mine], p_ref.at[mine], sem_p.at[0], sem_p.at[1], (r, other_core))
    third.start()
    pending.append(third)

    pl.semaphore_wait(relay.at[0], 2)
    pl.semaphore_signal(relay.at[1], inc=1, device_id=(y * NZX + across, c), device_id_type=MESH)

    lane = lax.broadcasted_iota(jnp.int32, (PANEL, PANEL), 1)
    l0, l1, l2, l3, l4 = gram_levels(half)
    high, low = two_sum(l0, l1)
    high, low2 = two_sum(high, l2)
    low = (low + low2) + (l3 + l4)
    packed, diagonal = pack_symmetric(high, low)
    for o in range(2 * NY):
        wpart[o, 0:16] = packed[16 * o : 16 * o + 16]
        wpart[o, 16:17] = diagonal
    for t in pair_peers:
        send(wpart.at[t], wa.at[own], wa_sem.at[0, t], wa_sem.at[1, own], pair_device(t))
    wa[own] = wpart[own]

    @pl.when(c != 0)
    def _():
        remote(leadbuf.at[0], leadbuf.at[1], sem_lead.at[0], sem_lead.at[3], (r, c)).wait_recv()

    lead = jnp.where(c == 0, leadbuf[0], leadbuf[1])
    remote(p_ref.at[theirs], p_ref.at[theirs], sem_p.at[0], sem_p.at[1], (r, c)).wait_recv()
    panel = p_ref[...]
    swapped = swapped_columns(slab, lead, onehot)
    b_ref[...] = swapped
    inner = hdot(panel, swapped, (0, 0))
    for b in range(4):
        gpart[b] = inner[:, 128 * b : 128 * b + 128]
    to_y(lambda t: gpart.at[t], lambda m: ga.at[m], ga_sem)
    ga[y] = gpart[y]

    pl.semaphore_wait(relay.at[1], 1)
    from_y(lambda t: sa.at[t], sa_sem)
    total = total_of(sa, NY)
    for k in range(NZX):
        ssum[k] = total[9 * k : 9 * k + 9]
    to_zx(lambda t: ssum.at[t], lambda m: sb.at[m], sb_sem)
    sb[w] = ssum[w]

    for t in pair_peers:
        remote(wa.at[t], wa.at[t], wa_sem.at[0, t], wa_sem.at[1, t], (r, c)).wait_recv()
    wsum[...] = two_float_total(wa, 2 * NY)
    to_zx(lambda t: wsum, lambda m: wb.at[m], wb_sem)
    wb[w] = wsum[...]

    tile = lambda t: pl.ds(pl.multiple_of(8 * t, 8), 8)
    from_y(lambda t: ga.at[t], ga_sem)
    gsum[...] = total_of(ga, NY)
    to_zx(lambda t: gsum.at[tile(t)], lambda m: gb.at[m], gb_sem)
    gb[w] = gsum[tile(w)]

    from_zx(lambda t: sb.at[t], sb_sem)
    sfull[y, w] = total_of(sb, NZX)
    to_zx(lambda t: sfull.at[y, w], lambda m: sfull.at[y, m], sc_sem)

    from_zx(lambda t: wb.at[t], wb_sem)
    wtot[...] = two_float_total(wb, NZX)
    for t in pair_peers:
        send(wtot, wfull.at[own], wc_sem.at[0, t], wc_sem.at[1, own], pair_device(t))
    wfull[own] = wtot[...]

    for t in pair_peers:
        remote(wfull.at[t], wfull.at[t], wc_sem.at[0, t], wc_sem.at[1, t], (r, c)).wait_recv()
    packed = jnp.concatenate([wfull[o, 0:16] for o in range(2 * NY)], axis=0)
    diagonal = wfull[0, 16:17]
    high = unpack_symmetric(packed, diagonal)
    low = unpack_symmetric(pltpu.roll(packed, 64, 1), pltpu.roll(diagonal, 64, 1))

    from_zx(lambda t: gb.at[t], gb_sem)
    gfull[y, tile(w)] = total_of(gb, NZX)
    row_peers = [lax.rem(r + i, NY * NZX) for i in range(1, NY * NZX)]
    for t in row_peers:
        send(gfull.at[y, tile(w)], gfull.at[y, tile(w)], gc_sem.at[0, t], gc_sem.at[1, r], (t, c))

    def sketch_home():
        from_zx(lambda t: sfull.at[y, t], sc_sem)
        to_y(lambda t: sfull.at[y], lambda m: sfull.at[m], sd_sem)

    eliminate(high, r_out.at[0], x_out.at[0], held, {4: sketch_home})
    r_one = r_out[0]
    x_one = x_out[0]

    rowi = lax.broadcasted_iota(jnp.int32, (PANEL, PANEL), 0)
    eye = jnp.where(rowi == lane, 1.0, 0.0).astype(F32)
    l0, l1, l2, l3, l4 = gram_levels(r_one)
    d, e1 = two_sum(high, -l0)
    d, e2 = two_sum(d, -l1)
    delta = (d - l2) + (((e1 + e2) + low) - (l3 + l4))
    gram_two = eye + hdot(hdot(x_one, delta), x_one, (1, 1))
    eliminate(gram_two, r_out.at[1], x_out.at[1], held)

    inverse = hdot(x_out[1], x_out[0])
    inv_ref[...] = inverse
    q_ref[...] = hdot(p_ref[...], inverse, (1, 1))
    first_ref[...] = r_out[0] * (1.0 / 128.0)
    rfac_ref[...] = hdot(r_out[1], r_out[0])

    from_y(lambda t: sfull.at[t], sd_sem)
    for t in row_peers:
        piece = gfull.at[lax.div(t, NZX), tile(lax.rem(t, NZX))]
        remote(piece, piece, gc_sem.at[0, t], gc_sem.at[1, t], (r, c)).wait_recv()
    for copy in pending:
        copy.wait_send()

    @pl.when(c == 0)
    def _():
        for copy in lead_copies:
            copy.wait_send()


def tree_sum(terms):
    terms = list(terms)
    while len(terms) > 1:
        pairs = [terms[i] + terms[i + 1] for i in range(0, len(terms) - 1, 2)]
        terms = pairs + terms[len(pairs) * 2 :]
    return terms[0]


def spread(v):
    return jnp.broadcast_to(v, (8, 128))


def split_three(x):
    high = x.astype(BF16).astype(F32)
    rest = x - high
    mid = rest.astype(BF16).astype(F32)
    return high, mid, rest - mid


def thin_dot(left, right):
    l0, l1, l2 = split_three(left)
    r0, r1, r2 = split_three(right)
    lefts = jnp.concatenate([l0, l0, l1, l0, l1, l2], axis=0).astype(BF16)
    rights = jnp.concatenate([r0, r1, r0, r2, r1, r0], axis=0).astype(BF16)
    return bdot(lefts, rights, (0, 0))


def block_factor(v, columns, held, first, sub, lane):
    slot = first % 16
    for i in range(8):
        held[slot + i] = columns[i]
    a = {(i, j): held[slot + i, pl.ds(j, 8, stride=0), :] for j in range(8) for i in range(j + 1)}
    m = [[None] * 8 for _ in range(8)]
    for i in range(8):
        inv = lax.rsqrt(a[i, i])
        l = {j: a[i, j] * inv for j in range(i + 1, 8)}
        for j in range(i + 1, 8):
            for k in range(j, 8):
                a[j, k] = a[j, k] - l[j] * l[k]
        for j in range(i):
            m[i][j] = m[i][j] * inv
        m[i][i] = inv
        for k in range(i + 1, 8):
            for j in range(i + 1):
                t = l[k] * m[i][j]
                m[k][j] = -t if m[k][j] is None else m[k][j] - t
    terms = []
    inverse = jnp.zeros((8, 128), F32)
    for j in range(8):
        column = m[7][j]
        for k in range(6, j - 1, -1):
            column = jnp.where(sub <= k, m[k][j], column)
        if j > 0:
            column = jnp.where(sub < j, 0.0, column)
        terms.append(column * spread(v[j : j + 1, :]))
        inverse = jnp.where(lane == first + j, column, inverse)
    solved = tree_sum(terms)
    inside = (lane >= first) & (lane < first + 8)
    return solved, jnp.where(inside, inverse, solved), m


def eliminate(w, r_ref, x_ref, held, between={}):
    sub = lax.broadcasted_iota(jnp.int32, (8, 128), 0)
    lane = lax.broadcasted_iota(jnp.int32, (8, 128), 1)
    count = PANEL // 8
    blocks = [w[8 * b : 8 * b + 8, :] for b in range(count)]
    spread_next = [spread(blocks[0][:, j : j + 1]) for j in range(8)]
    for b in range(count):
        if b in between:
            between[b]()
        first = 8 * b
        solved, both, m = block_factor(blocks[b], spread_next, held, first, sub, lane)
        upper = jnp.where(lane >= first + sub, solved, 0.0)
        r_ref[first : first + 8, :] = upper
        x_ref[first : first + 8, :] = jnp.where(lane < first + 8, both, 0.0)
        if b == count - 1:
            break
        inside = (lane >= first) & (lane < first + 8)
        rows = blocks[b + 1]
        columns = [spread(rows[:, first + j : first + j + 1]) for j in range(8)]
        updates, coefs = [], []
        for p in range(8):
            coef = tree_sum([m[p][j] * columns[j] for j in range(p + 1)])
            coefs.append(coef)
            updates.append(coef * spread(both[p : p + 1, :]))
        blocks[b + 1] = jnp.where(inside, 0.0, rows) - tree_sum(updates)
        spread_next = [
            spread(rows[:, first + 8 + j : first + 9 + j])
            - tree_sum([coefs[p] * spread(coefs[p][j : j + 1, :]) for p in range(8)])
            for j in range(8)
        ]
        if b + 2 < count:
            update = thin_dot(upper, both)
            for k in range(b + 2, count):
                blocks[k] = jnp.where(inside, 0.0, blocks[k]) - update[8 * k : 8 * k + 8, :]


def update_kernel(
    b_ref, q_ref, g_ref, s_ref, first_ref, rfac_ref, inv_ref,
    s_hbm, q_hbm, e_hbm, first_hbm, out_hbm,
    sbuf, qbuf, ebuf, obuf, sem,
):
    lead_block = lax.axis_index("col") == 0
    copies = []
    scale = 1.0 / 128.0

    def store(k, src, dst):
        copy = pltpu.make_async_copy(src, dst, sem.at[k])
        copy.start()
        copies.append(copy)

    for k in range(4):
        for t in range(NZX):
            sbuf[9 * t : 9 * t + 9, 128 * k : 128 * k + 128] = s_ref[k, t]
    store(0, sbuf, s_hbm.at[0])
    store(8, first_ref, first_hbm.at[0])
    basis = q_ref[...]
    qbuf[...] = basis * 128.0
    store(9, qbuf, q_hbm.at[0])
    r_factor = rfac_ref[...]
    inverse = inv_ref[...]
    for k in range(4):
        cols = slice(128 * k, 128 * k + 128)
        projected = hdot(inverse, g_ref[k])
        rest = b_ref[:, cols] - hdot(basis, projected)
        if k == 0:
            projected = jnp.where(lead_block, r_factor, projected)
            rest = jnp.where(lead_block, 0.0, rest)
        ebuf[:, cols] = projected * scale
        obuf[:, cols] = rest
        store(4 + k, obuf.at[:, cols], out_hbm.at[:, cols])
    store(10, ebuf, e_hbm.at[0])
    for copy in copies:
        copy.wait()


def shards(matrix_slab, sketch_matrix, pivots):
    rows, width = matrix_slab.shape
    sk = sketch_matrix.shape[0]
    dma = pltpu.SemaphoreType.DMA
    hbm = pl.BlockSpec(memory_space=pltpu.HBM)
    tile = lambda *lead: pltpu.VMEM(lead + (8, 128), F32)
    nine = lambda *lead: pltpu.VMEM(lead + (9, 128), F32)
    part = lambda *lead: pltpu.VMEM(lead + (17, 128), F32)
    square = lambda *lead: pltpu.VMEM(lead + (PANEL, 128), F32)
    tall = lambda *lead: pltpu.VMEM(lead + (sk, 128), F32)
    flat = lambda *shape: jax.ShapeDtypeStruct(shape, F32)
    mid = pl.pallas_call(
        reduce_kernel,
        out_shape=(
            flat(rows, width), flat(rows, PANEL), flat(4, PANEL, PANEL), flat(4, NZX, sk // NZX, PANEL),
            flat(PANEL, PANEL), flat(PANEL, PANEL), flat(PANEL, PANEL),
        ),
        in_specs=[hbm] * 3,
        out_specs=(VMEM_SPEC,) * 7,
        scratch_shapes=[
            pltpu.VMEM((rows, width), F32), pltpu.VMEM((sk, rows), F32), pltpu.VMEM((1, PANEL), jnp.int32),
            pltpu.VMEM((rows, PANEL), F32), square(2), square(2), tile(16),
            pltpu.VMEM((rows, PANEL), F32), square(), square(), square(),
            pltpu.VMEM((2, rows, PANEL), F32),
            part(2 * NY), part(2 * NY), part(), part(NZX), part(), part(2 * NY),
            square(NY), square(NY), square(), tile(NZX),
            tall(NY), tall(NY), nine(NZX), nine(NZX),
            dma((3,)), dma((4,)), dma((2,)), dma((4,)), dma((2, 2 * NY)), dma((2, NZX)), dma((2, 2 * NY)),
            dma((2, NY)), dma((2, NZX)), dma((2, NY * NZX)),
            dma((2, NY)), dma((2, NZX)), dma((2, NZX)), dma((2, NY)), pltpu.SemaphoreType.REGULAR((2,)),
        ],
        compiler_params=pltpu.CompilerParams(
            collective_id=0, has_side_effects=True, vmem_limit_bytes=VMEM_REDUCE
        ),
        name="reduce",
    )(*[pltpu.with_memory_space_constraint(a, pltpu.HBM) for a in (matrix_slab, sketch_matrix, pivots)])
    return pl.pallas_call(
        update_kernel,
        out_shape=(
            flat(1, sk, width), flat(1, rows, PANEL), flat(1, PANEL, width),
            flat(1, PANEL, PANEL), flat(rows, width),
        ),
        in_specs=[VMEM_SPEC] * 7,
        out_specs=(hbm,) * 5,
        scratch_shapes=[
            pltpu.VMEM((sk, width), F32), pltpu.VMEM((rows, PANEL), F32), pltpu.VMEM((PANEL, width), F32),
            pltpu.VMEM((rows, width), F32), dma((11,)),
        ],
        compiler_params=pltpu.CompilerParams(vmem_limit_bytes=VMEM_UPDATE),
        name="update",
    )(*mid)


def solution(mesh):
    in_specs = (P("row", "col"), P(None, "row"), P())
    out_specs = (
        P(None, None, "col"),
        P(None, "row", None),
        P(None, None, "col"),
        P(),
        P("row", "col"),
    )
    return jax.shard_map(shards, mesh=mesh, in_specs=in_specs, out_specs=out_specs, check_vma=False)
```

```python
import functools
import math

import jax
import jax.numpy as jnp
from jax import lax
from jax.experimental import pallas as pl
from jax.experimental.pallas import tpu as pltpu
from jax.sharding import PartitionSpec as P

PANEL = 128
VMEM_REDUCE = 32 * 1024 * 1024
VMEM_UPDATE = 32 * 1024 * 1024
NY = 4
NZX = 16
NCOL = 4
MESH = pl.DeviceIdType.MESH
F32 = jnp.float32
BF16 = jnp.bfloat16
VMEM_SPEC = pl.BlockSpec(memory_space=pltpu.VMEM)


def hdot(left, right, contract=(1, 0)):
    return lax.dot_general(
        left,
        right,
        (((contract[0],), (contract[1],)), ((), ())),
        precision=lax.Precision.HIGHEST,
        preferred_element_type=F32,
    )


def bdot(left, right, contract=(1, 0)):
    return lax.dot_general(
        left, right, (((contract[0],), (contract[1],)), ((), ())), preferred_element_type=F32
    )


def select_dot(values, onehot, contract=(1, 0)):
    high = values.astype(BF16)
    rest = values - high.astype(F32)
    mid = rest.astype(BF16)
    low = (rest - mid.astype(F32)).astype(BF16)
    return (bdot(high, onehot, contract) + bdot(mid, onehot, contract)) + bdot(low, onehot, contract)


def two_sum(a, b):
    s = a + b
    t = s - a
    return s, (a - (s - t)) + (b - t)


def gram_levels(x):
    n = x.shape[1]
    sigma = jnp.max(jnp.abs(x), axis=0, keepdims=True) * 131072.0
    parts = []
    rest = x
    for _ in range(4):
        part = (rest + sigma) - sigma
        rest = rest - part
        parts.append(part.astype(BF16))
        sigma = sigma * (1.0 / 128.0)
    cat = jnp.concatenate(parts, axis=1)
    full = bdot(cat, cat, (0, 0))
    block = lambda i, j: full[i * n : (i + 1) * n, j * n : (j + 1) * n]
    return (
        block(0, 0),
        block(0, 1) + block(1, 0),
        (block(0, 2) + block(2, 0)) + block(1, 1),
        (block(0, 3) + block(3, 0)) + (block(1, 2) + block(2, 1)),
        (block(1, 3) + block(3, 1)) + block(2, 2),
    )


def pivot_onehot(piv, col_first, width):
    lanes = lax.broadcasted_iota(jnp.int32, (width, PANEL), 0) + col_first
    return jnp.where(lanes == piv, 1.0, 0.0).astype(BF16)


def swapped_columns(slab, lead, onehot):
    picked = bdot(jnp.ones((8, PANEL), BF16), onehot, (1, 1))[0:1, :]
    return jnp.where(picked > 0.5, select_dot(lead, onehot, (1, 1)), slab)


def remote(src, dst, send, recv, device):
    return pltpu.make_async_remote_copy(
        src_ref=src, dst_ref=dst, send_sem=send, recv_sem=recv, device_id=device, device_id_type=MESH
    )


def pack_symmetric(high, low):
    row = lax.broadcasted_iota(jnp.int32, (64, 128), 0)
    lane = lax.broadcasted_iota(jnp.int32, (64, 128), 1)
    join = lambda a, b: jnp.where(lane[: a.shape[0]] < 64, a, pltpu.roll(b, 64, 1))
    corner = lambda v: jnp.where(row > lane, v[:64], pltpu.roll(v[64:], 64, 1))
    diagonal = lambda v: jnp.sum(jnp.where(row == lane, v[:64], 0.0), axis=0, keepdims=True)
    packed = jnp.concatenate([join(high[64:], low[64:]), join(corner(high), corner(low))], axis=0)
    return packed, join(diagonal(high), diagonal(low))


def unpack_symmetric(packed, diagonal):
    row = lax.broadcasted_iota(jnp.int32, (64, 128), 0)
    lane = lax.broadcasted_iota(jnp.int32, (64, 128), 1)
    below, corner = packed[:64], packed[64:]
    top = jnp.where(row == lane, diagonal, corner)
    bottom = jnp.where(lane < 64, below, pltpu.roll(corner, 64, 1))
    part = jnp.concatenate([top, bottom], axis=0)
    row = lax.broadcasted_iota(jnp.int32, (128, 128), 0)
    lane = lax.broadcasted_iota(jnp.int32, (128, 128), 1)
    lower = (lane <= row) & ((row < 64) | (lane < 64))
    upper = (row >= 64) & (lane >= row)
    return jnp.where(lower | upper, part, part.T)


def reduce_kernel(
    slab_hbm, sketch_hbm, piv_hbm,
    b_ref, q_ref, gfull, sfull, first_ref, rfac_ref, inv_ref,
    slab_ref, sketch_ref, piv_ref, p_ref, r_out, x_out, held,
    pk, pp, rc1, rc2, leadbuf,
    wpart, wa, wsum, wb, wtot, wfull,
    gpart, ga, gsum, gb,
    spart, sa, ssum, sb,
    sem_in, sem1, sem_p, sem_lead, wa_sem, wb_sem, wc_sem, ga_sem, gb_sem, gc_sem,
    sa_sem, sb_sem, sc_sem, sd_sem, relay,
):
    r = lax.axis_index("row")
    c = lax.axis_index("col")
    y = lax.div(r, NZX)
    w = lax.rem(r, NZX)
    core = lax.rem(c, 2)
    other_core = c + 1 - 2 * core
    other_chip = lax.rem(c + 2, NCOL)
    width = slab_ref.shape[1]
    load_piv = pltpu.make_async_copy(piv_hbm, piv_ref, sem_in.at[0])
    load_slab = pltpu.make_async_copy(slab_hbm, slab_ref, sem_in.at[1])
    load_sketch = pltpu.make_async_copy(sketch_hbm, sketch_ref, sem_in.at[2])
    load_piv.start()
    load_slab.start()
    load_sketch.start()

    ring = lambda d, n: min(d, n - d)
    z, x = lax.div(w, 2), lax.rem(w, 2)
    zx_at = lambda dz, dx: lax.rem(z + dz, NZX // 2) * 2 + (1 - x if dx else x)
    by_hops = lambda offsets: sorted(offsets, key=lambda o: -(ring(o[0], NY) + ring(o[1], NZX // 2) + 2 * o[2]))
    y_peers = [(lax.rem(y + dy, NY), dy) for dy in (2, 1, 3)]
    zx_offsets = by_hops([(0, dz, dx) for dz in range(NZX // 2) for dx in range(2) if dz or dx])
    zx_peers = [zx_at(dz, dx) for _, dz, dx in zx_offsets]
    all_offsets = by_hops(
        [(dy, dz, dx) for dy in range(NY) for dz in range(NZX // 2) for dx in range(2) if dy or dz or dx]
    )
    row_peers = [(lax.rem(y + dy, NY), zx_at(dz, dx)) for dy, dz, dx in all_offsets]
    own = y * 2 + core
    pair_peers = [lax.rem(own + i, 2 * NY) for i in (4, 3, 5, 2, 6, 1, 7)]

    def pair_device(t):
        return (lax.div(t, 2) * NZX + w, c - core + lax.rem(t, 2))

    barrier = pltpu.get_barrier_semaphore()
    z_step = lambda k: lax.rem(w + 2 * k + NZX, NZX)
    across = w + 1 - 2 * lax.rem(w, 2)
    for t in (z_step(2), z_step(-2), across, z_step(1), z_step(-1)):
        pl.semaphore_signal(barrier, inc=1, device_id=(y * NZX + t, c), device_id_type=MESH)
    for t in pair_peers:
        pl.semaphore_signal(barrier, inc=1, device_id=pair_device(t), device_id_type=MESH)
    for d in (other_chip, other_chip + 1 - 2 * core):
        pl.semaphore_signal(barrier, inc=1, device_id=(r, d), device_id_type=MESH)

    load_piv.wait()
    onehot = pivot_onehot(piv_ref[...], c * width, width)
    load_slab.wait()
    slab = slab_ref[...]
    pk[...] = select_dot(slab, onehot)
    load_sketch.wait()
    sketch = hdot(sketch_ref[...], slab)
    for b in range(4):
        spart[b] = sketch[:, 128 * b : 128 * b + 128]
    leadbuf[0] = slab[:, :PANEL]
    pl.semaphore_wait(barrier, 5 + 2 * NY - 1 + 2)
    for t in (z_step(2), z_step(-2)):
        pl.semaphore_signal(relay.at[0], inc=1, device_id=(y * NZX + t, c), device_id_type=MESH)

    pending = []

    def send(src, dst, send_sem, recv_sem, device):
        copy = remote(src, dst, send_sem, recv_sem, device)
        copy.start()
        pending.append(copy)

    def to_y(src, dst, sems):
        for t, _ in y_peers:
            send(src(t), dst(y), sems.at[0, t], sems.at[1, y], (t * NZX + w, c))

    def to_zx(src, dst, sems):
        for t in zx_peers:
            send(src(t), dst(w), sems.at[0, t], sems.at[1, w], (y * NZX + t, c))

    def from_y(dst, sems):
        for t, _ in y_peers:
            remote(dst(t), dst(t), sems.at[0, t], sems.at[1, t], (r, c)).wait_recv()

    def from_zx(dst, sems):
        for t in zx_peers:
            remote(dst(t), dst(t), sems.at[0, t], sems.at[1, t], (r, c)).wait_recv()

    def total_of(buf, count):
        return tree_sum([buf[k] for k in range(count)])

    def two_float_total(buf, count):
        total = buf[0]
        err = jnp.zeros_like(total)
        for k in range(1, count):
            total, e = two_sum(total, buf[k])
            err = err + e
        lanes = lax.broadcasted_iota(jnp.int32, total.shape, 1)
        return jnp.where(lanes < 64, total, total + pltpu.roll(err, 64, 1))

    mine = pl.ds(pl.multiple_of(128 * core, 128), 128)
    theirs = pl.ds(pl.multiple_of(128 - 128 * core, 128), 128)
    first = remote(pk.at[theirs], rc1, sem1.at[0], sem1.at[1], (r, other_core))
    first.start()
    to_y(lambda t: spart.at[t], lambda m: sa.at[m], sa_sem)
    sa[y] = spart[y]
    first.wait_recv()
    pp[...] = pk[mine] + rc1[...]
    second = remote(pp, rc2, sem1.at[2], sem1.at[3], (r, other_chip))
    second.start()
    lead_copies = [
        remote(leadbuf.at[0], leadbuf.at[1], sem_lead.at[j - 1], sem_lead.at[3], (r, j)) for j in range(1, NCOL)
    ]

    @pl.when(c == 0)
    def _():
        for copy in lead_copies:
            copy.start()

    second.wait_recv()
    pending.extend([first, second])
    half = pp[...] + rc2[...]
    p_ref[mine] = half
    third = remote(p_ref.at[mine], p_ref.at[mine], sem_p.at[0], sem_p.at[1], (r, other_core))
    third.start()
    pending.append(third)

    pl.semaphore_wait(relay.at[0], 2)
    pl.semaphore_signal(relay.at[1], inc=1, device_id=(y * NZX + across, c), device_id_type=MESH)

    lane = lax.broadcasted_iota(jnp.int32, (PANEL, PANEL), 1)
    l0, l1, l2, l3, l4 = gram_levels(half)
    high, low = two_sum(l0, l1)
    high, low2 = two_sum(high, l2)
    low = (low + low2) + (l3 + l4)
    packed, diagonal = pack_symmetric(high, low)
    for o in range(2 * NY):
        wpart[o, 0:16] = packed[16 * o : 16 * o + 16]
        wpart[o, 16:17] = diagonal
    for t in pair_peers:
        send(wpart.at[t], wa.at[own], wa_sem.at[0, t], wa_sem.at[1, own], pair_device(t))
    wa[own] = wpart[own]

    @pl.when(c != 0)
    def _():
        remote(leadbuf.at[0], leadbuf.at[1], sem_lead.at[0], sem_lead.at[3], (r, c)).wait_recv()

    lead = jnp.where(c == 0, leadbuf[0], leadbuf[1])
    remote(p_ref.at[theirs], p_ref.at[theirs], sem_p.at[0], sem_p.at[1], (r, c)).wait_recv()
    panel = p_ref[...]
    swapped = swapped_columns(slab, lead, onehot)
    b_ref[...] = swapped
    inner = hdot(panel, swapped, (0, 0))
    for b in range(4):
        gpart[b] = inner[:, 128 * b : 128 * b + 128]
    to_y(lambda t: gpart.at[t], lambda m: ga.at[m], ga_sem)
    ga[y] = gpart[y]

    pl.semaphore_wait(relay.at[1], 1)
    from_y(lambda t: sa.at[t], sa_sem)
    total = total_of(sa, NY)
    for k in range(NZX):
        ssum[k] = total[9 * k : 9 * k + 9]
    to_zx(lambda t: ssum.at[t], lambda m: sb.at[m], sb_sem)
    sb[w] = ssum[w]

    for t in pair_peers:
        remote(wa.at[t], wa.at[t], wa_sem.at[0, t], wa_sem.at[1, t], (r, c)).wait_recv()
    wsum[...] = two_float_total(wa, 2 * NY)
    to_zx(lambda t: wsum, lambda m: wb.at[m], wb_sem)
    wb[w] = wsum[...]

    tile = lambda t: pl.ds(pl.multiple_of(8 * t, 8), 8)
    from_y(lambda t: ga.at[t], ga_sem)
    gsum[...] = total_of(ga, NY)
    to_zx(lambda t: gsum.at[tile(t)], lambda m: gb.at[m], gb_sem)
    gb[w] = gsum[tile(w)]

    from_zx(lambda t: wb.at[t], wb_sem)
    wtot[...] = two_float_total(wb, NZX)
    for t in pair_peers:
        send(wtot, wfull.at[own], wc_sem.at[0, t], wc_sem.at[1, own], pair_device(t))
    wfull[own] = wtot[...]

    from_zx(lambda t: sb.at[t], sb_sem)
    sfull[y, w] = total_of(sb, NZX)
    to_zx(lambda t: sfull.at[y, w], lambda m: sfull.at[y, m], sc_sem)

    for t in pair_peers:
        remote(wfull.at[t], wfull.at[t], wc_sem.at[0, t], wc_sem.at[1, t], (r, c)).wait_recv()
    packed = jnp.concatenate([wfull[o, 0:16] for o in range(2 * NY)], axis=0)
    diagonal = wfull[0, 16:17]
    high = unpack_symmetric(packed, diagonal)
    low = unpack_symmetric(pltpu.roll(packed, 64, 1), pltpu.roll(diagonal, 64, 1))

    from_zx(lambda t: gb.at[t], gb_sem)
    gfull[y, tile(w)] = total_of(gb, NZX)
    for ty, tw in row_peers:
        t = ty * NZX + tw
        send(gfull.at[y, tile(w)], gfull.at[y, tile(w)], gc_sem.at[0, t], gc_sem.at[1, r], (t, c))

    def sketch_home():
        from_zx(lambda t: sfull.at[y, t], sc_sem)
        to_y(lambda t: sfull.at[y], lambda m: sfull.at[m], sd_sem)

    eliminate(high, r_out.at[0], x_out.at[0], held, {8: sketch_home})
    r_one = r_out[0]
    x_one = x_out[0]

    rowi = lax.broadcasted_iota(jnp.int32, (PANEL, PANEL), 0)
    eye = jnp.where(rowi == lane, 1.0, 0.0).astype(F32)
    l0, l1, l2, l3, l4 = gram_levels(r_one)
    d, e1 = two_sum(high, -l0)
    d, e2 = two_sum(d, -l1)
    delta = (d - l2) + (((e1 + e2) + low) - (l3 + l4))
    gram_two = eye + hdot(hdot(x_one, delta), x_one, (1, 1))
    eliminate(gram_two, r_out.at[1], x_out.at[1], held)

    inverse = hdot(x_out[1], x_out[0])
    inv_ref[...] = inverse
    q_ref[...] = hdot(p_ref[...], inverse, (1, 1))
    first_ref[...] = r_out[0] * (1.0 / 128.0)
    rfac_ref[...] = hdot(r_out[1], r_out[0])

    from_y(lambda t: sfull.at[t], sd_sem)
    for ty, tw in row_peers:
        t = ty * NZX + tw
        piece = gfull.at[ty, tile(tw)]
        remote(piece, piece, gc_sem.at[0, t], gc_sem.at[1, t], (r, c)).wait_recv()
    for copy in pending:
        copy.wait_send()

    @pl.when(c == 0)
    def _():
        for copy in lead_copies:
            copy.wait_send()


def tree_sum(terms):
    terms = list(terms)
    while len(terms) > 1:
        pairs = [terms[i] + terms[i + 1] for i in range(0, len(terms) - 1, 2)]
        terms = pairs + terms[len(pairs) * 2 :]
    return terms[0]


def spread(v):
    return jnp.broadcast_to(v, (8, 128))


def split_three(x):
    high = x.astype(BF16).astype(F32)
    rest = x - high
    mid = rest.astype(BF16).astype(F32)
    return high, mid, rest - mid


def thin_dot(left, right):
    l0, l1, l2 = split_three(left)
    r0, r1, r2 = split_three(right)
    lefts = jnp.concatenate([l0, l0, l1, l0, l1, l2], axis=0).astype(BF16)
    rights = jnp.concatenate([r0, r1, r0, r2, r1, r0], axis=0).astype(BF16)
    return bdot(lefts, rights, (0, 0))


def block_factor(v, columns, held, first, sub, lane):
    slot = first % 16
    for i in range(8):
        held[slot + i] = columns[i]
    a = {(i, j): held[slot + i, pl.ds(j, 8, stride=0), :] for j in range(8) for i in range(j + 1)}
    m = [[None] * 8 for _ in range(8)]
    for i in range(8):
        inv = lax.rsqrt(a[i, i])
        l = {j: a[i, j] * inv for j in range(i + 1, 8)}
        for j in range(i + 1, 8):
            for k in range(j, 8):
                a[j, k] = a[j, k] - l[j] * l[k]
        for j in range(i):
            m[i][j] = m[i][j] * inv
        m[i][i] = inv
        for k in range(i + 1, 8):
            for j in range(i + 1):
                t = l[k] * m[i][j]
                m[k][j] = -t if m[k][j] is None else m[k][j] - t
    terms = []
    inverse = jnp.zeros((8, 128), F32)
    for j in range(8):
        column = m[7][j]
        for k in range(6, j - 1, -1):
            column = jnp.where(sub <= k, m[k][j], column)
        if j > 0:
            column = jnp.where(sub < j, 0.0, column)
        terms.append(column * spread(v[j : j + 1, :]))
        inverse = jnp.where(lane == first + j, column, inverse)
    solved = tree_sum(terms)
    inside = (lane >= first) & (lane < first + 8)
    return solved, jnp.where(inside, inverse, solved), m


def eliminate(w, r_ref, x_ref, held, between={}):
    sub = lax.broadcasted_iota(jnp.int32, (8, 128), 0)
    lane = lax.broadcasted_iota(jnp.int32, (8, 128), 1)
    count = PANEL // 8
    blocks = [w[8 * b : 8 * b + 8, :] for b in range(count)]
    spread_next = [spread(blocks[0][:, j : j + 1]) for j in range(8)]
    for b in range(count):
        if b in between:
            between[b]()
        first = 8 * b
        solved, both, m = block_factor(blocks[b], spread_next, held, first, sub, lane)
        upper = jnp.where(lane >= first + sub, solved, 0.0)
        r_ref[first : first + 8, :] = upper
        x_ref[first : first + 8, :] = jnp.where(lane < first + 8, both, 0.0)
        if b == count - 1:
            break
        inside = (lane >= first) & (lane < first + 8)
        rows = blocks[b + 1]
        columns = [spread(rows[:, first + j : first + j + 1]) for j in range(8)]
        updates, coefs = [], []
        for p in range(8):
            coef = tree_sum([m[p][j] * columns[j] for j in range(p + 1)])
            coefs.append(coef)
            updates.append(coef * spread(both[p : p + 1, :]))
        blocks[b + 1] = jnp.where(inside, 0.0, rows) - tree_sum(updates)
        spread_next = [
            spread(rows[:, first + 8 + j : first + 9 + j])
            - tree_sum([coefs[p] * spread(coefs[p][j : j + 1, :]) for p in range(8)])
            for j in range(8)
        ]
        if b + 2 < count:
            update = thin_dot(upper, both)
            for k in range(b + 2, count):
                blocks[k] = jnp.where(inside, 0.0, blocks[k]) - update[8 * k : 8 * k + 8, :]


def update_kernel(
    b_ref, q_ref, g_ref, s_ref, first_ref, rfac_ref, inv_ref,
    s_hbm, q_hbm, e_hbm, first_hbm, out_hbm,
    sbuf, qbuf, ebuf, obuf, sem,
):
    lead_block = lax.axis_index("col") == 0
    copies = []
    scale = 1.0 / 128.0

    def store(k, src, dst):
        copy = pltpu.make_async_copy(src, dst, sem.at[k])
        copy.start()
        copies.append(copy)

    for k in range(4):
        for t in range(NZX):
            sbuf[9 * t : 9 * t + 9, 128 * k : 128 * k + 128] = s_ref[k, t]
    store(0, sbuf, s_hbm.at[0])
    store(8, first_ref, first_hbm.at[0])
    basis = q_ref[...]
    qbuf[...] = basis * 128.0
    store(9, qbuf, q_hbm.at[0])
    r_factor = rfac_ref[...]
    inverse = inv_ref[...]
    for k in range(4):
        cols = slice(128 * k, 128 * k + 128)
        projected = hdot(inverse, g_ref[k])
        rest = b_ref[:, cols] - hdot(basis, projected)
        if k == 0:
            projected = jnp.where(lead_block, r_factor, projected)
            rest = jnp.where(lead_block, 0.0, rest)
        ebuf[:, cols] = projected * scale
        obuf[:, cols] = rest
        store(4 + k, obuf.at[:, cols], out_hbm.at[:, cols])
    store(10, ebuf, e_hbm.at[0])
    for copy in copies:
        copy.wait()


def shards(matrix_slab, sketch_matrix, pivots):
    rows, width = matrix_slab.shape
    sk = sketch_matrix.shape[0]
    dma = pltpu.SemaphoreType.DMA
    hbm = pl.BlockSpec(memory_space=pltpu.HBM)
    tile = lambda *lead: pltpu.VMEM(lead + (8, 128), F32)
    nine = lambda *lead: pltpu.VMEM(lead + (9, 128), F32)
    part = lambda *lead: pltpu.VMEM(lead + (17, 128), F32)
    square = lambda *lead: pltpu.VMEM(lead + (PANEL, 128), F32)
    tall = lambda *lead: pltpu.VMEM(lead + (sk, 128), F32)
    flat = lambda *shape: jax.ShapeDtypeStruct(shape, F32)
    mid = pl.pallas_call(
        reduce_kernel,
        out_shape=(
            flat(rows, width), flat(rows, PANEL), flat(4, PANEL, PANEL), flat(4, NZX, sk // NZX, PANEL),
            flat(PANEL, PANEL), flat(PANEL, PANEL), flat(PANEL, PANEL),
        ),
        in_specs=[hbm] * 3,
        out_specs=(VMEM_SPEC,) * 7,
        scratch_shapes=[
            pltpu.VMEM((rows, width), F32), pltpu.VMEM((sk, rows), F32), pltpu.VMEM((1, PANEL), jnp.int32),
            pltpu.VMEM((rows, PANEL), F32), square(2), square(2), tile(16),
            pltpu.VMEM((rows, PANEL), F32), square(), square(), square(),
            pltpu.VMEM((2, rows, PANEL), F32),
            part(2 * NY), part(2 * NY), part(), part(NZX), part(), part(2 * NY),
            square(NY), square(NY), square(), tile(NZX),
            tall(NY), tall(NY), nine(NZX), nine(NZX),
            dma((3,)), dma((4,)), dma((2,)), dma((4,)), dma((2, 2 * NY)), dma((2, NZX)), dma((2, 2 * NY)),
            dma((2, NY)), dma((2, NZX)), dma((2, NY * NZX)),
            dma((2, NY)), dma((2, NZX)), dma((2, NZX)), dma((2, NY)), pltpu.SemaphoreType.REGULAR((2,)),
        ],
        compiler_params=pltpu.CompilerParams(
            collective_id=0, has_side_effects=True, vmem_limit_bytes=VMEM_REDUCE
        ),
        name="reduce",
    )(*[pltpu.with_memory_space_constraint(a, pltpu.HBM) for a in (matrix_slab, sketch_matrix, pivots)])
    return pl.pallas_call(
        update_kernel,
        out_shape=(
            flat(1, sk, width), flat(1, rows, PANEL), flat(1, PANEL, width),
            flat(1, PANEL, PANEL), flat(rows, width),
        ),
        in_specs=[VMEM_SPEC] * 7,
        out_specs=(hbm,) * 5,
        scratch_shapes=[
            pltpu.VMEM((sk, width), F32), pltpu.VMEM((rows, PANEL), F32), pltpu.VMEM((PANEL, width), F32),
            pltpu.VMEM((rows, width), F32), dma((11,)),
        ],
        compiler_params=pltpu.CompilerParams(vmem_limit_bytes=VMEM_UPDATE),
        name="update",
    )(*mid)


def solution(mesh):
    in_specs = (P("row", "col"), P(None, "row"), P())
    out_specs = (
        P(None, None, "col"),
        P(None, "row", None),
        P(None, None, "col"),
        P(),
        P("row", "col"),
    )
    return jax.shard_map(shards, mesh=mesh, in_specs=in_specs, out_specs=out_specs, check_vma=False)
```

```python
import functools
import math

import jax
import jax.numpy as jnp
from jax import lax
from jax.experimental import pallas as pl
from jax.experimental.pallas import tpu as pltpu
from jax.sharding import PartitionSpec as P

PANEL = 128
VMEM_REDUCE = 32 * 1024 * 1024
VMEM_UPDATE = 32 * 1024 * 1024
NY = 4
NZX = 16
NCOL = 4
MESH = pl.DeviceIdType.MESH
F32 = jnp.float32
BF16 = jnp.bfloat16
VMEM_SPEC = pl.BlockSpec(memory_space=pltpu.VMEM)


def hdot(left, right, contract=(1, 0)):
    return lax.dot_general(
        left,
        right,
        (((contract[0],), (contract[1],)), ((), ())),
        precision=lax.Precision.HIGHEST,
        preferred_element_type=F32,
    )


def bdot(left, right, contract=(1, 0)):
    return lax.dot_general(
        left, right, (((contract[0],), (contract[1],)), ((), ())), preferred_element_type=F32
    )


def select_dot(values, onehot, contract=(1, 0)):
    high = values.astype(BF16)
    rest = values - high.astype(F32)
    mid = rest.astype(BF16)
    low = (rest - mid.astype(F32)).astype(BF16)
    return (bdot(high, onehot, contract) + bdot(mid, onehot, contract)) + bdot(low, onehot, contract)


def two_sum(a, b):
    s = a + b
    t = s - a
    return s, (a - (s - t)) + (b - t)


def gram_levels(x):
    n = x.shape[1]
    sigma = jnp.max(jnp.abs(x), axis=0, keepdims=True) * 131072.0
    parts = []
    rest = x
    for _ in range(4):
        part = (rest + sigma) - sigma
        rest = rest - part
        parts.append(part.astype(BF16))
        sigma = sigma * (1.0 / 128.0)
    cat = jnp.concatenate(parts, axis=1)
    full = bdot(cat, cat, (0, 0))
    block = lambda i, j: full[i * n : (i + 1) * n, j * n : (j + 1) * n]
    return (
        block(0, 0),
        block(0, 1) + block(1, 0),
        (block(0, 2) + block(2, 0)) + block(1, 1),
        (block(0, 3) + block(3, 0)) + (block(1, 2) + block(2, 1)),
        (block(1, 3) + block(3, 1)) + block(2, 2),
    )


def pivot_onehot(piv, col_first, width):
    lanes = lax.broadcasted_iota(jnp.int32, (width, PANEL), 0) + col_first
    return jnp.where(lanes == piv, 1.0, 0.0).astype(BF16)


def swapped_columns(slab, lead, onehot):
    picked = bdot(jnp.ones((8, PANEL), BF16), onehot, (1, 1))[0:1, :]
    return jnp.where(picked > 0.5, select_dot(lead, onehot, (1, 1)), slab)


def remote(src, dst, send, recv, device):
    return pltpu.make_async_remote_copy(
        src_ref=src, dst_ref=dst, send_sem=send, recv_sem=recv, device_id=device, device_id_type=MESH
    )


def pack_symmetric(high, low):
    row = lax.broadcasted_iota(jnp.int32, (64, 128), 0)
    lane = lax.broadcasted_iota(jnp.int32, (64, 128), 1)
    join = lambda a, b: jnp.where(lane[: a.shape[0]] < 64, a, pltpu.roll(b, 64, 1))
    corner = lambda v: jnp.where(row > lane, v[:64], pltpu.roll(v[64:], 64, 1))
    diagonal = lambda v: jnp.sum(jnp.where(row == lane, v[:64], 0.0), axis=0, keepdims=True)
    packed = jnp.concatenate([join(high[64:], low[64:]), join(corner(high), corner(low))], axis=0)
    return packed, join(diagonal(high), diagonal(low))


def unpack_symmetric(packed, diagonal):
    row = lax.broadcasted_iota(jnp.int32, (64, 128), 0)
    lane = lax.broadcasted_iota(jnp.int32, (64, 128), 1)
    below, corner = packed[:64], packed[64:]
    top = jnp.where(row == lane, diagonal, corner)
    bottom = jnp.where(lane < 64, below, pltpu.roll(corner, 64, 1))
    part = jnp.concatenate([top, bottom], axis=0)
    row = lax.broadcasted_iota(jnp.int32, (128, 128), 0)
    lane = lax.broadcasted_iota(jnp.int32, (128, 128), 1)
    lower = (lane <= row) & ((row < 64) | (lane < 64))
    upper = (row >= 64) & (lane >= row)
    return jnp.where(lower | upper, part, part.T)


def reduce_kernel(
    slab_hbm, sketch_hbm, piv_hbm,
    b_ref, q_ref, gfull, s_ref, first_ref, rfac_ref, inv_ref, panel_ref,
    slab_ref, sketch_ref, piv_ref, p_ref, r_out, x_out, held,
    pk, pp, rc1, rc2, leadbuf,
    wpart, wa, wsum, wb, wtot, wfull,
    gpart, ga, gsum, gb,
    spart, sa, ssum, sb, sfull,
    sem_in, sem1, sem_p, sem_lead, wa_sem, wb_sem, wc_sem, ga_sem, gb_sem, gc_sem,
    sa_sem, sb_sem, sc_sem, sd_sem, relay,
):
    r = lax.axis_index("row")
    c = lax.axis_index("col")
    y = lax.div(r, NZX)
    w = lax.rem(r, NZX)
    core = lax.rem(c, 2)
    other_core = c + 1 - 2 * core
    other_chip = lax.rem(c + 2, NCOL)
    width = slab_ref.shape[1]
    load_piv = pltpu.make_async_copy(piv_hbm, piv_ref, sem_in.at[0])
    load_slab = pltpu.make_async_copy(slab_hbm, slab_ref, sem_in.at[1])
    load_sketch = pltpu.make_async_copy(sketch_hbm, sketch_ref, sem_in.at[2])
    load_piv.start()
    load_slab.start()
    load_sketch.start()

    ring = lambda d, n: min(d, n - d)
    z, x = lax.div(w, 2), lax.rem(w, 2)
    zx_at = lambda dz, dx: lax.rem(z + dz, NZX // 2) * 2 + (1 - x if dx else x)
    by_hops = lambda offsets: sorted(offsets, key=lambda o: -(ring(o[0], NY) + ring(o[1], NZX // 2) + 2 * o[2]))
    y_peers = [(lax.rem(y + dy, NY), dy) for dy in (2, 1, 3)]
    zx_offsets = by_hops([(0, dz, dx) for dz in range(NZX // 2) for dx in range(2) if dz or dx])
    zx_peers = [zx_at(dz, dx) for _, dz, dx in zx_offsets]
    all_offsets = by_hops(
        [(dy, dz, dx) for dy in range(NY) for dz in range(NZX // 2) for dx in range(2) if dy or dz or dx]
    )
    row_peers = [(lax.rem(y + dy, NY), zx_at(dz, dx)) for dy, dz, dx in all_offsets]
    own = y * 2 + core
    pair_peers = [lax.rem(own + i, 2 * NY) for i in (4, 3, 5, 2, 6, 1, 7)]

    def pair_device(t):
        return (lax.div(t, 2) * NZX + w, c - core + lax.rem(t, 2))

    barrier = pltpu.get_barrier_semaphore()
    z_step = lambda k: lax.rem(w + 2 * k + NZX, NZX)
    across = w + 1 - 2 * lax.rem(w, 2)
    for t in (z_step(2), z_step(-2), across, z_step(1), z_step(-1)):
        pl.semaphore_signal(barrier, inc=1, device_id=(y * NZX + t, c), device_id_type=MESH)
    for t in pair_peers:
        pl.semaphore_signal(barrier, inc=1, device_id=pair_device(t), device_id_type=MESH)
    for d in (other_chip, other_chip + 1 - 2 * core):
        pl.semaphore_signal(barrier, inc=1, device_id=(r, d), device_id_type=MESH)

    load_piv.wait()
    onehot = pivot_onehot(piv_ref[...], c * width, width)
    load_slab.wait()
    slab = slab_ref[...]
    pk[...] = select_dot(slab, onehot)
    load_sketch.wait()
    sketch = hdot(sketch_ref[...], slab)
    for b in range(4):
        spart[b] = sketch[:, 128 * b : 128 * b + 128]
    leadbuf[0] = slab[:, :PANEL]
    pl.semaphore_wait(barrier, 5 + 2 * NY - 1 + 2)
    for t in (z_step(2), z_step(-2)):
        pl.semaphore_signal(relay.at[0], inc=1, device_id=(y * NZX + t, c), device_id_type=MESH)

    pending = []

    def send(src, dst, send_sem, recv_sem, device):
        copy = remote(src, dst, send_sem, recv_sem, device)
        copy.start()
        pending.append(copy)

    def to_y(src, dst, sems):
        for t, _ in y_peers:
            send(src(t), dst(y), sems.at[0, t], sems.at[1, y], (t * NZX + w, c))

    def to_zx(src, dst, sems):
        for t in zx_peers:
            send(src(t), dst(w), sems.at[0, t], sems.at[1, w], (y * NZX + t, c))

    def from_y(dst, sems):
        for t, _ in y_peers:
            remote(dst(t), dst(t), sems.at[0, t], sems.at[1, t], (r, c)).wait_recv()

    def from_zx(dst, sems):
        for t in zx_peers:
            remote(dst(t), dst(t), sems.at[0, t], sems.at[1, t], (r, c)).wait_recv()

    def total_of(buf, count):
        return tree_sum([buf[k] for k in range(count)])

    def two_float_total(buf, count):
        total = buf[0]
        err = jnp.zeros_like(total)
        for k in range(1, count):
            total, e = two_sum(total, buf[k])
            err = err + e
        lanes = lax.broadcasted_iota(jnp.int32, total.shape, 1)
        return jnp.where(lanes < 64, total, total + pltpu.roll(err, 64, 1))

    mine = pl.ds(pl.multiple_of(128 * core, 128), 128)
    theirs = pl.ds(pl.multiple_of(128 - 128 * core, 128), 128)
    first = remote(pk.at[theirs], rc1, sem1.at[0], sem1.at[1], (r, other_core))
    first.start()
    to_y(lambda t: spart.at[t], lambda m: sa.at[m], sa_sem)
    sa[y] = spart[y]
    first.wait_recv()
    pp[...] = pk[mine] + rc1[...]
    second = remote(pp, rc2, sem1.at[2], sem1.at[3], (r, other_chip))
    second.start()
    lead_copies = [
        remote(leadbuf.at[0], leadbuf.at[1], sem_lead.at[j - 1], sem_lead.at[3], (r, j)) for j in range(1, NCOL)
    ]

    @pl.when(c == 0)
    def _():
        for copy in lead_copies:
            copy.start()

    second.wait_recv()
    pending.extend([first, second])
    half = pp[...] + rc2[...]
    p_ref[mine] = half
    third = remote(p_ref.at[mine], p_ref.at[mine], sem_p.at[0], sem_p.at[1], (r, other_core))
    third.start()
    pending.append(third)

    pl.semaphore_wait(relay.at[0], 2)
    pl.semaphore_signal(relay.at[1], inc=1, device_id=(y * NZX + across, c), device_id_type=MESH)

    lane = lax.broadcasted_iota(jnp.int32, (PANEL, PANEL), 1)
    l0, l1, l2, l3, l4 = gram_levels(half)
    high, low = two_sum(l0, l1)
    high, low2 = two_sum(high, l2)
    low = (low + low2) + (l3 + l4)
    packed, diagonal = pack_symmetric(high, low)
    for o in range(2 * NY):
        wpart[o, 0:16] = packed[16 * o : 16 * o + 16]
        wpart[o, 16:17] = diagonal
    for t in pair_peers:
        send(wpart.at[t], wa.at[own], wa_sem.at[0, t], wa_sem.at[1, own], pair_device(t))
    wa[own] = wpart[own]

    @pl.when(c != 0)
    def _():
        remote(leadbuf.at[0], leadbuf.at[1], sem_lead.at[0], sem_lead.at[3], (r, c)).wait_recv()

    lead = jnp.where(c == 0, leadbuf[0], leadbuf[1])
    remote(p_ref.at[theirs], p_ref.at[theirs], sem_p.at[0], sem_p.at[1], (r, c)).wait_recv()
    panel = p_ref[...]
    swapped = swapped_columns(slab, lead, onehot)
    b_ref[...] = swapped
    inner = hdot(panel, swapped, (0, 0))
    for b in range(4):
        gpart[b] = inner[:, 128 * b : 128 * b + 128]
    to_y(lambda t: gpart.at[t], lambda m: ga.at[m], ga_sem)
    ga[y] = gpart[y]

    pl.semaphore_wait(relay.at[1], 1)
    from_y(lambda t: sa.at[t], sa_sem)
    total = total_of(sa, NY)
    for k in range(NZX):
        ssum[k] = total[9 * k : 9 * k + 9]
    to_zx(lambda t: ssum.at[t], lambda m: sb.at[m], sb_sem)
    sb[w] = ssum[w]

    for t in pair_peers:
        remote(wa.at[t], wa.at[t], wa_sem.at[0, t], wa_sem.at[1, t], (r, c)).wait_recv()
    wsum[...] = two_float_total(wa, 2 * NY)
    to_zx(lambda t: wsum, lambda m: wb.at[m], wb_sem)
    wb[w] = wsum[...]

    tile = lambda t: pl.ds(pl.multiple_of(8 * t, 8), 8)
    from_y(lambda t: ga.at[t], ga_sem)
    gsum[...] = total_of(ga, NY)
    to_zx(lambda t: gsum.at[tile(t)], lambda m: gb.at[m], gb_sem)
    gb[w] = gsum[tile(w)]

    from_zx(lambda t: wb.at[t], wb_sem)
    wtot[...] = two_float_total(wb, NZX)
    for t in pair_peers:
        send(wtot, wfull.at[own], wc_sem.at[0, t], wc_sem.at[1, own], pair_device(t))
    wfull[own] = wtot[...]

    from_zx(lambda t: sb.at[t], sb_sem)
    sfull[y, w] = total_of(sb, NZX)
    to_zx(lambda t: sfull.at[y, w], lambda m: sfull.at[y, m], sc_sem)

    for t in pair_peers:
        remote(wfull.at[t], wfull.at[t], wc_sem.at[0, t], wc_sem.at[1, t], (r, c)).wait_recv()
    packed = jnp.concatenate([wfull[o, 0:16] for o in range(2 * NY)], axis=0)
    diagonal = wfull[0, 16:17]
    high = unpack_symmetric(packed, diagonal)
    low = unpack_symmetric(pltpu.roll(packed, 64, 1), pltpu.roll(diagonal, 64, 1))

    from_zx(lambda t: gb.at[t], gb_sem)
    gfull[y, tile(w)] = total_of(gb, NZX)
    for ty, tw in row_peers:
        t = ty * NZX + tw
        send(gfull.at[y, tile(w)], gfull.at[y, tile(w)], gc_sem.at[0, t], gc_sem.at[1, r], (t, c))

    def sketch_home():
        from_zx(lambda t: sfull.at[y, t], sc_sem)
        to_y(lambda t: sfull.at[y], lambda m: sfull.at[m], sd_sem)

    eliminate(high, r_out.at[0], x_out.at[0], held, {8: sketch_home})
    r_one = r_out[0]
    x_one = x_out[0]

    rowi = lax.broadcasted_iota(jnp.int32, (PANEL, PANEL), 0)
    eye = jnp.where(rowi == lane, 1.0, 0.0).astype(F32)
    l0, l1, l2, l3, l4 = gram_levels(r_one)
    d, e1 = two_sum(high, -l0)
    d, e2 = two_sum(d, -l1)
    delta = (d - l2) + (((e1 + e2) + low) - (l3 + l4))
    gram_two = eye + hdot(hdot(x_one, delta), x_one, (1, 1))
    eliminate(gram_two, r_out.at[1], x_out.at[1], held)

    inverse = hdot(x_out[1], x_out[0])
    inv_ref[...] = inverse
    basis = hdot(p_ref[...], inverse, (1, 1))
    q_ref[...] = basis
    panel_ref[...] = basis * 128.0
    first_ref[...] = r_out[0] * (1.0 / 128.0)
    rfac_ref[...] = hdot(r_out[1], r_out[0])

    from_y(lambda t: sfull.at[t], sd_sem)
    for k in range(NY):
        for t in range(NZX):
            s_ref[9 * t : 9 * t + 9, 128 * k : 128 * k + 128] = sfull[k, t]
    for ty, tw in row_peers:
        t = ty * NZX + tw
        piece = gfull.at[ty, tile(tw)]
        remote(piece, piece, gc_sem.at[0, t], gc_sem.at[1, t], (r, c)).wait_recv()
    for copy in pending:
        copy.wait_send()

    @pl.when(c == 0)
    def _():
        for copy in lead_copies:
            copy.wait_send()


def tree_sum(terms):
    terms = list(terms)
    while len(terms) > 1:
        pairs = [terms[i] + terms[i + 1] for i in range(0, len(terms) - 1, 2)]
        terms = pairs + terms[len(pairs) * 2 :]
    return terms[0]


def spread(v):
    return jnp.broadcast_to(v, (8, 128))


def split_three(x):
    high = x.astype(BF16).astype(F32)
    rest = x - high
    mid = rest.astype(BF16).astype(F32)
    return high, mid, rest - mid


def thin_dot(left, right):
    l0, l1, l2 = split_three(left)
    r0, r1, r2 = split_three(right)
    lefts = jnp.concatenate([l0, l0, l1, l0, l1, l2], axis=0).astype(BF16)
    rights = jnp.concatenate([r0, r1, r0, r2, r1, r0], axis=0).astype(BF16)
    return bdot(lefts, rights, (0, 0))


def block_factor(v, columns, held, first, sub, lane):
    slot = first % 16
    for i in range(8):
        held[slot + i, 0:8] = columns[i]
    a = {(i, j): held[slot + i, pl.ds(j, 8, stride=0), :] for j in range(8) for i in range(j + 1)}
    m = [[None] * 8 for _ in range(8)]
    for i in range(8):
        inv = lax.rsqrt(a[i, i])
        l = {j: a[i, j] * inv for j in range(i + 1, 8)}
        for j in range(i + 1, 8):
            for k in range(j, 8):
                a[j, k] = a[j, k] - l[j] * l[k]
        for j in range(i):
            m[i][j] = m[i][j] * inv
        m[i][i] = inv
        for k in range(i + 1, 8):
            for j in range(i + 1):
                t = l[k] * m[i][j]
                m[k][j] = -t if m[k][j] is None else m[k][j] - t
    terms = []
    inverse = jnp.zeros((8, 128), F32)
    for j in range(8):
        column = m[7][j]
        for k in range(6, j - 1, -1):
            column = jnp.where(sub <= k, m[k][j], column)
        if j > 0:
            column = jnp.where(sub < j, 0.0, column)
        terms.append(column * spread(v[j : j + 1, :]))
        inverse = jnp.where(lane == first + j, column, inverse)
    solved = tree_sum(terms)
    inside = (lane >= first) & (lane < first + 8)
    return solved, jnp.where(inside, inverse, solved), m


def eliminate(w, r_ref, x_ref, held, between={}):
    sub = lax.broadcasted_iota(jnp.int32, (8, 128), 0)
    lane = lax.broadcasted_iota(jnp.int32, (8, 128), 1)
    count = PANEL // 8
    blocks = [w[8 * b : 8 * b + 8, :] for b in range(count)]
    spread_next = [spread(blocks[0][:, j : j + 1]) for j in range(8)]
    for b in range(count):
        if b in between:
            between[b]()
        first = 8 * b
        solved, both, m = block_factor(blocks[b], spread_next, held, first, sub, lane)
        upper = jnp.where(lane >= first + sub, solved, 0.0)
        r_ref[first : first + 8, :] = upper
        x_ref[first : first + 8, :] = jnp.where(lane < first + 8, both, 0.0)
        if b == count - 1:
            break
        inside = (lane >= first) & (lane < first + 8)
        rows = blocks[b + 1]
        columns = [spread(rows[:, first + j : first + j + 1]) for j in range(8)]
        updates, coefs = [], []
        for p in range(8):
            coef = tree_sum([m[p][j] * columns[j] for j in range(p + 1)])
            coefs.append(coef)
            updates.append(coef * spread(both[p : p + 1, :]))
        blocks[b + 1] = jnp.where(inside, 0.0, rows) - tree_sum(updates)
        spread_next = [
            spread(rows[:, first + 8 + j : first + 9 + j])
            - tree_sum([coefs[p] * spread(coefs[p][j : j + 1, :]) for p in range(8)])
            for j in range(8)
        ]
        if b + 2 < count:
            update = thin_dot(upper, both)
            for k in range(b + 2, count):
                blocks[k] = jnp.where(inside, 0.0, blocks[k]) - update[8 * k : 8 * k + 8, :]


def update_kernel(
    b_ref, q_ref, g_ref, s_ref, first_ref, rfac_ref, inv_ref, panel_ref,
    s_hbm, q_hbm, e_hbm, first_hbm, out_hbm,
    ebuf, obuf, sem,
):
    lead_block = lax.axis_index("col") == 0
    copies = []
    scale = 1.0 / 128.0

    def store(k, src, dst):
        copy = pltpu.make_async_copy(src, dst, sem.at[k])
        copy.start()
        copies.append(copy)

    store(0, s_ref, s_hbm.at[0])
    store(1, first_ref, first_hbm.at[0])
    store(2, panel_ref, q_hbm.at[0])
    basis = q_ref[...]
    r_factor = rfac_ref[...]
    inverse = inv_ref[...]
    for k in range(2):
        cols = slice(256 * k, 256 * k + 256)
        projected = hdot(inverse, jnp.concatenate([g_ref[2 * k], g_ref[2 * k + 1]], axis=1))
        rest = b_ref[:, cols] - hdot(basis, projected)
        if k == 0:
            head = jnp.where(lead_block, r_factor, projected[:, :PANEL])
            projected = jnp.concatenate([head, projected[:, PANEL:]], axis=1)
            head = jnp.where(lead_block, 0.0, rest[:, :PANEL])
            rest = jnp.concatenate([head, rest[:, PANEL:]], axis=1)
        ebuf[:, cols] = projected * scale
        obuf[:, cols] = rest
        store(3 + 2 * k, ebuf.at[:, cols], e_hbm.at[0, :, cols])
        store(4 + 2 * k, obuf.at[:, cols], out_hbm.at[:, cols])
    for copy in copies:
        copy.wait()


def shards(matrix_slab, sketch_matrix, pivots):
    rows, width = matrix_slab.shape
    sk = sketch_matrix.shape[0]
    dma = pltpu.SemaphoreType.DMA
    hbm = pl.BlockSpec(memory_space=pltpu.HBM)
    tile = lambda *lead: pltpu.VMEM(lead + (8, 128), F32)
    nine = lambda *lead: pltpu.VMEM(lead + (9, 128), F32)
    part = lambda *lead: pltpu.VMEM(lead + (17, 128), F32)
    square = lambda *lead: pltpu.VMEM(lead + (PANEL, 128), F32)
    tall = lambda *lead: pltpu.VMEM(lead + (sk, 128), F32)
    flat = lambda *shape: jax.ShapeDtypeStruct(shape, F32)
    mid = pl.pallas_call(
        reduce_kernel,
        out_shape=(
            flat(rows, width), flat(rows, PANEL), flat(4, PANEL, PANEL), flat(sk, width),
            flat(PANEL, PANEL), flat(PANEL, PANEL), flat(PANEL, PANEL), flat(rows, PANEL),
        ),
        in_specs=[hbm] * 3,
        out_specs=(VMEM_SPEC,) * 8,
        scratch_shapes=[
            pltpu.VMEM((rows, width), F32), pltpu.VMEM((sk, rows), F32), pltpu.VMEM((1, PANEL), jnp.int32),
            pltpu.VMEM((rows, PANEL), F32), square(2), square(2), pltpu.VMEM((16, 16, 128), F32),
            pltpu.VMEM((rows, PANEL), F32), square(), square(), square(),
            pltpu.VMEM((2, rows, PANEL), F32),
            part(2 * NY), part(2 * NY), part(), part(NZX), part(), part(2 * NY),
            square(NY), square(NY), square(), tile(NZX),
            tall(NY), tall(NY), nine(NZX), nine(NZX), nine(NY, NZX),
            dma((3,)), dma((4,)), dma((2,)), dma((4,)), dma((2, 2 * NY)), dma((2, NZX)), dma((2, 2 * NY)),
            dma((2, NY)), dma((2, NZX)), dma((2, NY * NZX)),
            dma((2, NY)), dma((2, NZX)), dma((2, NZX)), dma((2, NY)), pltpu.SemaphoreType.REGULAR((2,)),
        ],
        compiler_params=pltpu.CompilerParams(
            collective_id=0, has_side_effects=True, vmem_limit_bytes=VMEM_REDUCE
        ),
        name="reduce",
    )(*[pltpu.with_memory_space_constraint(a, pltpu.HBM) for a in (matrix_slab, sketch_matrix, pivots)])
    return pl.pallas_call(
        update_kernel,
        out_shape=(
            flat(1, sk, width), flat(1, rows, PANEL), flat(1, PANEL, width),
            flat(1, PANEL, PANEL), flat(rows, width),
        ),
        in_specs=[VMEM_SPEC] * 8,
        out_specs=(hbm,) * 5,
        scratch_shapes=[
            pltpu.VMEM((PANEL, width), F32), pltpu.VMEM((rows, width), F32), dma((7,)),
        ],
        compiler_params=pltpu.CompilerParams(vmem_limit_bytes=VMEM_UPDATE),
        name="update",
    )(*mid)


def solution(mesh):
    in_specs = (P("row", "col"), P(None, "row"), P())
    out_specs = (
        P(None, None, "col"),
        P(None, "row", None),
        P(None, None, "col"),
        P(),
        P("row", "col"),
    )
    return jax.shard_map(shards, mesh=mesh, in_specs=in_specs, out_specs=out_specs, check_vma=False)
```

```python
import functools
import math

import jax
import jax.numpy as jnp
from jax import lax
from jax.experimental import pallas as pl
from jax.experimental.pallas import tpu as pltpu
from jax.sharding import PartitionSpec as P

PANEL = 128
VMEM_REDUCE = 32 * 1024 * 1024
VMEM_UPDATE = 32 * 1024 * 1024
NY = 4
NZX = 16
NCOL = 4
MESH = pl.DeviceIdType.MESH
F32 = jnp.float32
BF16 = jnp.bfloat16
VMEM_SPEC = pl.BlockSpec(memory_space=pltpu.VMEM)


def hdot(left, right, contract=(1, 0)):
    return lax.dot_general(
        left,
        right,
        (((contract[0],), (contract[1],)), ((), ())),
        precision=lax.Precision.HIGHEST,
        preferred_element_type=F32,
    )


def bdot(left, right, contract=(1, 0)):
    return lax.dot_general(
        left, right, (((contract[0],), (contract[1],)), ((), ())), preferred_element_type=F32
    )


def select_dot(values, onehot, contract=(1, 0)):
    high = values.astype(BF16)
    rest = values - high.astype(F32)
    mid = rest.astype(BF16)
    low = (rest - mid.astype(F32)).astype(BF16)
    return (bdot(high, onehot, contract) + bdot(mid, onehot, contract)) + bdot(low, onehot, contract)


def two_sum(a, b):
    s = a + b
    t = s - a
    return s, (a - (s - t)) + (b - t)


def gram_levels(x):
    n = x.shape[1]
    sigma = jnp.max(jnp.abs(x), axis=0, keepdims=True) * 131072.0
    parts = []
    rest = x
    for _ in range(4):
        part = (rest + sigma) - sigma
        rest = rest - part
        parts.append(part.astype(BF16))
        sigma = sigma * (1.0 / 128.0)
    cat = jnp.concatenate(parts, axis=1)
    full = bdot(cat, cat, (0, 0))
    block = lambda i, j: full[i * n : (i + 1) * n, j * n : (j + 1) * n]
    return (
        block(0, 0),
        block(0, 1) + block(1, 0),
        (block(0, 2) + block(2, 0)) + block(1, 1),
        (block(0, 3) + block(3, 0)) + (block(1, 2) + block(2, 1)),
        (block(1, 3) + block(3, 1)) + block(2, 2),
    )


def pivot_onehot(piv, col_first, width):
    lanes = lax.broadcasted_iota(jnp.int32, (width, PANEL), 0) + col_first
    return jnp.where(lanes == piv, 1.0, 0.0).astype(BF16)


def swapped_columns(slab, lead, onehot):
    picked = bdot(jnp.ones((8, PANEL), BF16), onehot, (1, 1))[0:1, :]
    return jnp.where(picked > 0.5, select_dot(lead, onehot, (1, 1)), slab)


def remote(src, dst, send, recv, device):
    return pltpu.make_async_remote_copy(
        src_ref=src, dst_ref=dst, send_sem=send, recv_sem=recv, device_id=device, device_id_type=MESH
    )


def pack_symmetric(high, low):
    row = lax.broadcasted_iota(jnp.int32, (64, 128), 0)
    lane = lax.broadcasted_iota(jnp.int32, (64, 128), 1)
    join = lambda a, b: jnp.where(lane[: a.shape[0]] < 64, a, pltpu.roll(b, 64, 1))
    corner = lambda v: jnp.where(row > lane, v[:64], pltpu.roll(v[64:], 64, 1))
    diagonal = lambda v: jnp.sum(jnp.where(row == lane, v[:64], 0.0), axis=0, keepdims=True)
    packed = jnp.concatenate([join(high[64:], low[64:]), join(corner(high), corner(low))], axis=0)
    return packed, join(diagonal(high), diagonal(low))


def unpack_symmetric(packed, diagonal):
    row = lax.broadcasted_iota(jnp.int32, (64, 128), 0)
    lane = lax.broadcasted_iota(jnp.int32, (64, 128), 1)
    below, corner = packed[:64], packed[64:]
    top = jnp.where(row == lane, diagonal, corner)
    bottom = jnp.where(lane < 64, below, pltpu.roll(corner, 64, 1))
    part = jnp.concatenate([top, bottom], axis=0)
    row = lax.broadcasted_iota(jnp.int32, (128, 128), 0)
    lane = lax.broadcasted_iota(jnp.int32, (128, 128), 1)
    lower = (lane <= row) & ((row < 64) | (lane < 64))
    upper = (row >= 64) & (lane >= row)
    return jnp.where(lower | upper, part, part.T)


def reduce_kernel(
    slab_hbm, sketch_hbm, piv_hbm,
    b_ref, q_ref, gfull, s_ref, first_ref, rfac_ref, inv_ref, panel_ref,
    slab_ref, sketch_ref, piv_ref, p_ref, r_out, x_out, held,
    pk, pp, rc1, rc2, leadbuf,
    wpart, wa, wsum, wb, wtot, wfull,
    gpart, ga, gsum, gb,
    spart, sa, ssum, sb, sfull,
    sem_in, sem1, sem_p, sem_lead, wa_sem, wb_sem, wc_sem, ga_sem, gb_sem, gc_sem,
    sa_sem, sb_sem, sc_sem, sd_sem, relay,
):
    r = lax.axis_index("row")
    c = lax.axis_index("col")
    y = lax.div(r, NZX)
    w = lax.rem(r, NZX)
    core = lax.rem(c, 2)
    other_core = c + 1 - 2 * core
    other_chip = lax.rem(c + 2, NCOL)
    width = slab_ref.shape[1]
    load_piv = pltpu.make_async_copy(piv_hbm, piv_ref, sem_in.at[0])
    load_slab = pltpu.make_async_copy(slab_hbm, slab_ref, sem_in.at[1])
    load_sketch = pltpu.make_async_copy(sketch_hbm, sketch_ref, sem_in.at[2])
    load_piv.start()
    load_slab.start()
    load_sketch.start()

    ring = lambda d, n: min(d, n - d)
    z, x = lax.div(w, 2), lax.rem(w, 2)
    zx_at = lambda dz, dx: lax.rem(z + dz, NZX // 2) * 2 + (1 - x if dx else x)
    by_hops = lambda offsets: sorted(offsets, key=lambda o: -(ring(o[0], NY) + ring(o[1], NZX // 2) + 2 * o[2]))
    y_peers = [(lax.rem(y + dy, NY), dy) for dy in (2, 1, 3)]
    zx_offsets = by_hops([(0, dz, dx) for dz in range(NZX // 2) for dx in range(2) if dz or dx])
    zx_peers = [zx_at(dz, dx) for _, dz, dx in zx_offsets]
    all_offsets = by_hops(
        [(dy, dz, dx) for dy in range(NY) for dz in range(NZX // 2) for dx in range(2) if dy or dz or dx]
    )
    row_peers = [(lax.rem(y + dy, NY), zx_at(dz, dx)) for dy, dz, dx in all_offsets]
    own = y * 2 + core
    pair_peers = [lax.rem(own + i, 2 * NY) for i in (4, 3, 5, 2, 6, 1, 7)]

    def pair_device(t):
        return (lax.div(t, 2) * NZX + w, c - core + lax.rem(t, 2))

    barrier = pltpu.get_barrier_semaphore()
    z_step = lambda k: lax.rem(w + 2 * k + NZX, NZX)
    across = w + 1 - 2 * lax.rem(w, 2)
    for t in (z_step(2), z_step(-2), across, z_step(1), z_step(-1)):
        pl.semaphore_signal(barrier, inc=1, device_id=(y * NZX + t, c), device_id_type=MESH)
    for t in pair_peers:
        pl.semaphore_signal(barrier, inc=1, device_id=pair_device(t), device_id_type=MESH)
    for d in (other_chip, other_chip + 1 - 2 * core):
        pl.semaphore_signal(barrier, inc=1, device_id=(r, d), device_id_type=MESH)

    load_piv.wait()
    onehot = pivot_onehot(piv_ref[...], c * width, width)
    load_slab.wait()
    slab = slab_ref[...]
    pk[...] = select_dot(slab, onehot)
    load_sketch.wait()
    sketch = hdot(sketch_ref[...], slab)
    for b in range(4):
        spart[b] = sketch[:, 128 * b : 128 * b + 128]
    leadbuf[0] = slab[:, :PANEL]
    pl.semaphore_wait(barrier, 5 + 2 * NY - 1 + 2)
    for t in (z_step(2), z_step(-2)):
        pl.semaphore_signal(relay.at[0], inc=1, device_id=(y * NZX + t, c), device_id_type=MESH)

    pending = []

    def send(src, dst, send_sem, recv_sem, device):
        copy = remote(src, dst, send_sem, recv_sem, device)
        copy.start()
        pending.append(copy)

    def to_y(src, dst, sems):
        for t, _ in y_peers:
            send(src(t), dst(y), sems.at[0, t], sems.at[1, y], (t * NZX + w, c))

    def to_zx(src, dst, sems):
        for t in zx_peers:
            send(src(t), dst(w), sems.at[0, t], sems.at[1, w], (y * NZX + t, c))

    def from_y(dst, sems):
        for t, _ in y_peers:
            remote(dst(t), dst(t), sems.at[0, t], sems.at[1, t], (r, c)).wait_recv()

    def from_zx(dst, sems):
        for t in zx_peers:
            remote(dst(t), dst(t), sems.at[0, t], sems.at[1, t], (r, c)).wait_recv()

    def total_of(buf, count):
        return tree_sum([buf[k] for k in range(count)])

    def two_float_total(buf, count):
        total = buf[0]
        err = jnp.zeros_like(total)
        for k in range(1, count):
            total, e = two_sum(total, buf[k])
            err = err + e
        lanes = lax.broadcasted_iota(jnp.int32, total.shape, 1)
        return jnp.where(lanes < 64, total, total + pltpu.roll(err, 64, 1))

    mine = pl.ds(pl.multiple_of(128 * core, 128), 128)
    theirs = pl.ds(pl.multiple_of(128 - 128 * core, 128), 128)
    first = remote(pk.at[theirs], rc1, sem1.at[0], sem1.at[1], (r, other_core))
    first.start()
    to_y(lambda t: spart.at[t], lambda m: sa.at[m], sa_sem)
    sa[y] = spart[y]
    first.wait_recv()
    pp[...] = pk[mine] + rc1[...]
    second = remote(pp, rc2, sem1.at[2], sem1.at[3], (r, other_chip))
    second.start()
    lead_copies = [
        remote(leadbuf.at[0], leadbuf.at[1], sem_lead.at[j - 1], sem_lead.at[3], (r, j)) for j in range(1, NCOL)
    ]

    @pl.when(c == 0)
    def _():
        for copy in lead_copies:
            copy.start()

    second.wait_recv()
    pending.extend([first, second])
    half = pp[...] + rc2[...]
    p_ref[mine] = half
    third = remote(p_ref.at[mine], p_ref.at[mine], sem_p.at[0], sem_p.at[1], (r, other_core))
    third.start()
    pending.append(third)

    pl.semaphore_wait(relay.at[0], 2)
    pl.semaphore_signal(relay.at[1], inc=1, device_id=(y * NZX + across, c), device_id_type=MESH)

    lane = lax.broadcasted_iota(jnp.int32, (PANEL, PANEL), 1)
    l0, l1, l2, l3, l4 = gram_levels(half)
    high, low = two_sum(l0, l1)
    high, low2 = two_sum(high, l2)
    low = (low + low2) + (l3 + l4)
    packed, diagonal = pack_symmetric(high, low)
    for o in range(2 * NY):
        wpart[o, 0:16] = packed[16 * o : 16 * o + 16]
        wpart[o, 16:17] = diagonal
    for t in pair_peers:
        send(wpart.at[t], wa.at[own], wa_sem.at[0, t], wa_sem.at[1, own], pair_device(t))
    wa[own] = wpart[own]

    @pl.when(c != 0)
    def _():
        remote(leadbuf.at[0], leadbuf.at[1], sem_lead.at[0], sem_lead.at[3], (r, c)).wait_recv()

    lead = jnp.where(c == 0, leadbuf[0], leadbuf[1])
    remote(p_ref.at[theirs], p_ref.at[theirs], sem_p.at[0], sem_p.at[1], (r, c)).wait_recv()
    panel = p_ref[...]
    swapped = swapped_columns(slab, lead, onehot)
    b_ref[...] = swapped
    inner = hdot(panel, swapped, (0, 0))
    for b in range(4):
        gpart[b] = inner[:, 128 * b : 128 * b + 128]
    to_y(lambda t: gpart.at[t], lambda m: ga.at[m], ga_sem)
    ga[y] = gpart[y]

    pl.semaphore_wait(relay.at[1], 1)
    from_y(lambda t: sa.at[t], sa_sem)
    total = total_of(sa, NY)
    for k in range(NZX):
        ssum[k] = total[9 * k : 9 * k + 9]
    to_zx(lambda t: ssum.at[t], lambda m: sb.at[m], sb_sem)
    sb[w] = ssum[w]

    for t in pair_peers:
        remote(wa.at[t], wa.at[t], wa_sem.at[0, t], wa_sem.at[1, t], (r, c)).wait_recv()
    wsum[...] = two_float_total(wa, 2 * NY)
    to_zx(lambda t: wsum, lambda m: wb.at[m], wb_sem)
    wb[w] = wsum[...]

    tile = lambda t: pl.ds(pl.multiple_of(8 * t, 8), 8)
    from_y(lambda t: ga.at[t], ga_sem)
    gsum[...] = total_of(ga, NY)
    to_zx(lambda t: gsum.at[tile(t)], lambda m: gb.at[m], gb_sem)
    gb[w] = gsum[tile(w)]

    from_zx(lambda t: wb.at[t], wb_sem)
    wtot[...] = two_float_total(wb, NZX)
    for t in pair_peers:
        send(wtot, wfull.at[own], wc_sem.at[0, t], wc_sem.at[1, own], pair_device(t))
    wfull[own] = wtot[...]

    from_zx(lambda t: sb.at[t], sb_sem)
    sfull[y, w] = total_of(sb, NZX)
    to_zx(lambda t: sfull.at[y, w], lambda m: sfull.at[y, m], sc_sem)

    for t in pair_peers:
        remote(wfull.at[t], wfull.at[t], wc_sem.at[0, t], wc_sem.at[1, t], (r, c)).wait_recv()
    from_zx(lambda t: gb.at[t], gb_sem)
    gfull[y, tile(w)] = total_of(gb, NZX)
    for ty, tw in row_peers:
        t = ty * NZX + tw
        send(gfull.at[y, tile(w)], gfull.at[y, tile(w)], gc_sem.at[0, t], gc_sem.at[1, r], (t, c))

    packed = jnp.concatenate([wfull[o, 0:16] for o in range(2 * NY)], axis=0)
    diagonal = wfull[0, 16:17]
    high = unpack_symmetric(packed, diagonal)
    low = unpack_symmetric(pltpu.roll(packed, 64, 1), pltpu.roll(diagonal, 64, 1))

    def sketch_home():
        from_zx(lambda t: sfull.at[y, t], sc_sem)
        to_y(lambda t: sfull.at[y], lambda m: sfull.at[m], sd_sem)

    eliminate(high, r_out.at[0], x_out.at[0], held, {8: sketch_home})
    r_one = r_out[0]
    x_one = x_out[0]

    rowi = lax.broadcasted_iota(jnp.int32, (PANEL, PANEL), 0)
    eye = jnp.where(rowi == lane, 1.0, 0.0).astype(F32)
    l0, l1, l2, l3, l4 = gram_levels(r_one)
    d, e1 = two_sum(high, -l0)
    d, e2 = two_sum(d, -l1)
    delta = (d - l2) + (((e1 + e2) + low) - (l3 + l4))
    gram_two = eye + hdot(hdot(x_one, delta), x_one, (1, 1))
    eliminate(gram_two, r_out.at[1], x_out.at[1], held)

    inverse = hdot(x_out[1], x_out[0])
    inv_ref[...] = inverse
    basis = hdot(p_ref[...], inverse, (1, 1))
    q_ref[...] = basis
    panel_ref[...] = basis * 128.0
    first_ref[...] = r_out[0] * (1.0 / 128.0)
    rfac_ref[...] = hdot(r_out[1], r_out[0])

    from_y(lambda t: sfull.at[t], sd_sem)
    for k in range(NY):
        for t in range(NZX):
            s_ref[9 * t : 9 * t + 9, 128 * k : 128 * k + 128] = sfull[k, t]
    for ty, tw in row_peers:
        t = ty * NZX + tw
        piece = gfull.at[ty, tile(tw)]
        remote(piece, piece, gc_sem.at[0, t], gc_sem.at[1, t], (r, c)).wait_recv()
    for copy in pending:
        copy.wait_send()

    @pl.when(c == 0)
    def _():
        for copy in lead_copies:
            copy.wait_send()


def tree_sum(terms):
    terms = list(terms)
    while len(terms) > 1:
        pairs = [terms[i] + terms[i + 1] for i in range(0, len(terms) - 1, 2)]
        terms = pairs + terms[len(pairs) * 2 :]
    return terms[0]


def spread(v):
    return jnp.broadcast_to(v, (8, 128))


def split_three(x):
    high = x.astype(BF16).astype(F32)
    rest = x - high
    mid = rest.astype(BF16).astype(F32)
    return high, mid, rest - mid


def thin_dot(left, right):
    l0, l1, l2 = split_three(left)
    r0, r1, r2 = split_three(right)
    lefts = jnp.concatenate([l0, l0, l1, l0, l1, l2], axis=0).astype(BF16)
    rights = jnp.concatenate([r0, r1, r0, r2, r1, r0], axis=0).astype(BF16)
    return bdot(lefts, rights, (0, 0))


def block_factor(v, columns, held, first, sub, lane):
    slot = first % 16
    for i in range(8):
        held[slot + i, 0:8] = columns[i]
    a = {(i, j): held[slot + i, pl.ds(j, 8, stride=0), :] for j in range(8) for i in range(j + 1)}
    m = [[None] * 8 for _ in range(8)]
    for i in range(8):
        inv = lax.rsqrt(a[i, i])
        l = {j: a[i, j] * inv for j in range(i + 1, 8)}
        for j in range(i + 1, 8):
            for k in range(j, 8):
                a[j, k] = a[j, k] - l[j] * l[k]
        for j in range(i):
            m[i][j] = m[i][j] * inv
        m[i][i] = inv
        for k in range(i + 1, 8):
            for j in range(i + 1):
                t = l[k] * m[i][j]
                m[k][j] = -t if m[k][j] is None else m[k][j] - t
    terms = []
    inverse = jnp.zeros((8, 128), F32)
    for j in range(8):
        column = m[7][j]
        for k in range(6, j - 1, -1):
            column = jnp.where(sub <= k, m[k][j], column)
        if j > 0:
            column = jnp.where(sub < j, 0.0, column)
        terms.append(column * spread(v[j : j + 1, :]))
        inverse = jnp.where(lane == first + j, column, inverse)
    solved = tree_sum(terms)
    inside = (lane >= first) & (lane < first + 8)
    return solved, jnp.where(inside, inverse, solved), m


def eliminate(w, r_ref, x_ref, held, between={}):
    sub = lax.broadcasted_iota(jnp.int32, (8, 128), 0)
    lane = lax.broadcasted_iota(jnp.int32, (8, 128), 1)
    count = PANEL // 8
    blocks = [w[8 * b : 8 * b + 8, :] for b in range(count)]
    spread_next = [spread(blocks[0][:, j : j + 1]) for j in range(8)]
    for b in range(count):
        if b in between:
            between[b]()
        first = 8 * b
        solved, both, m = block_factor(blocks[b], spread_next, held, first, sub, lane)
        upper = jnp.where(lane >= first + sub, solved, 0.0)
        r_ref[first : first + 8, :] = upper
        x_ref[first : first + 8, :] = jnp.where(lane < first + 8, both, 0.0)
        if b == count - 1:
            break
        inside = (lane >= first) & (lane < first + 8)
        rows = blocks[b + 1]
        columns = [spread(rows[:, first + j : first + j + 1]) for j in range(8)]
        updates, coefs = [], []
        for p in range(8):
            coef = tree_sum([m[p][j] * columns[j] for j in range(p + 1)])
            coefs.append(coef)
            updates.append(coef * spread(both[p : p + 1, :]))
        blocks[b + 1] = jnp.where(inside, 0.0, rows) - tree_sum(updates)
        spread_next = [
            spread(rows[:, first + 8 + j : first + 9 + j])
            - tree_sum([coefs[p] * spread(coefs[p][j : j + 1, :]) for p in range(8)])
            for j in range(8)
        ]
        if b + 2 < count:
            update = thin_dot(upper, both)
            for k in range(b + 2, count):
                blocks[k] = jnp.where(inside, 0.0, blocks[k]) - update[8 * k : 8 * k + 8, :]


def update_kernel(
    b_ref, q_ref, g_ref, s_ref, first_ref, rfac_ref, inv_ref, panel_ref,
    s_hbm, q_hbm, e_hbm, first_hbm, out_hbm,
    ebuf, obuf, sem,
):
    lead_block = lax.axis_index("col") == 0
    copies = []
    scale = 1.0 / 128.0

    def store(k, src, dst):
        copy = pltpu.make_async_copy(src, dst, sem.at[k])
        copy.start()
        copies.append(copy)

    store(0, s_ref, s_hbm.at[0])
    store(1, first_ref, first_hbm.at[0])
    store(2, panel_ref, q_hbm.at[0])
    basis = q_ref[...]
    r_factor = rfac_ref[...]
    inverse = inv_ref[...]
    for k in range(2):
        cols = slice(256 * k, 256 * k + 256)
        projected = hdot(inverse, jnp.concatenate([g_ref[2 * k], g_ref[2 * k + 1]], axis=1))
        rest = b_ref[:, cols] - hdot(basis, projected)
        if k == 0:
            head = jnp.where(lead_block, r_factor, projected[:, :PANEL])
            projected = jnp.concatenate([head, projected[:, PANEL:]], axis=1)
            head = jnp.where(lead_block, 0.0, rest[:, :PANEL])
            rest = jnp.concatenate([head, rest[:, PANEL:]], axis=1)
        ebuf[:, cols] = projected * scale
        obuf[:, cols] = rest
        store(3 + 2 * k, ebuf.at[:, cols], e_hbm.at[0, :, cols])
        store(4 + 2 * k, obuf.at[:, cols], out_hbm.at[:, cols])
    for copy in copies:
        copy.wait()


def shards(matrix_slab, sketch_matrix, pivots):
    rows, width = matrix_slab.shape
    sk = sketch_matrix.shape[0]
    dma = pltpu.SemaphoreType.DMA
    hbm = pl.BlockSpec(memory_space=pltpu.HBM)
    tile = lambda *lead: pltpu.VMEM(lead + (8, 128), F32)
    nine = lambda *lead: pltpu.VMEM(lead + (9, 128), F32)
    part = lambda *lead: pltpu.VMEM(lead + (17, 128), F32)
    square = lambda *lead: pltpu.VMEM(lead + (PANEL, 128), F32)
    tall = lambda *lead: pltpu.VMEM(lead + (sk, 128), F32)
    flat = lambda *shape: jax.ShapeDtypeStruct(shape, F32)
    mid = pl.pallas_call(
        reduce_kernel,
        out_shape=(
            flat(rows, width), flat(rows, PANEL), flat(4, PANEL, PANEL), flat(sk, width),
            flat(PANEL, PANEL), flat(PANEL, PANEL), flat(PANEL, PANEL), flat(rows, PANEL),
        ),
        in_specs=[hbm] * 3,
        out_specs=(VMEM_SPEC,) * 8,
        scratch_shapes=[
            pltpu.VMEM((rows, width), F32), pltpu.VMEM((sk, rows), F32), pltpu.VMEM((1, PANEL), jnp.int32),
            pltpu.VMEM((rows, PANEL), F32), square(2), square(2), pltpu.VMEM((16, 16, 128), F32),
            pltpu.VMEM((rows, PANEL), F32), square(), square(), square(),
            pltpu.VMEM((2, rows, PANEL), F32),
            part(2 * NY), part(2 * NY), part(), part(NZX), part(), part(2 * NY),
            square(NY), square(NY), square(), tile(NZX),
            tall(NY), tall(NY), nine(NZX), nine(NZX), nine(NY, NZX),
            dma((3,)), dma((4,)), dma((2,)), dma((4,)), dma((2, 2 * NY)), dma((2, NZX)), dma((2, 2 * NY)),
            dma((2, NY)), dma((2, NZX)), dma((2, NY * NZX)),
            dma((2, NY)), dma((2, NZX)), dma((2, NZX)), dma((2, NY)), pltpu.SemaphoreType.REGULAR((2,)),
        ],
        compiler_params=pltpu.CompilerParams(
            collective_id=0, has_side_effects=True, vmem_limit_bytes=VMEM_REDUCE
        ),
        name="reduce",
    )(*[pltpu.with_memory_space_constraint(a, pltpu.HBM) for a in (matrix_slab, sketch_matrix, pivots)])
    return pl.pallas_call(
        update_kernel,
        out_shape=(
            flat(1, sk, width), flat(1, rows, PANEL), flat(1, PANEL, width),
            flat(1, PANEL, PANEL), flat(rows, width),
        ),
        in_specs=[VMEM_SPEC] * 8,
        out_specs=(hbm,) * 5,
        scratch_shapes=[
            pltpu.VMEM((PANEL, width), F32), pltpu.VMEM((rows, width), F32), dma((7,)),
        ],
        compiler_params=pltpu.CompilerParams(vmem_limit_bytes=VMEM_UPDATE),
        name="update",
    )(*mid)


def solution(mesh):
    in_specs = (P("row", "col"), P(None, "row"), P())
    out_specs = (
        P(None, None, "col"),
        P(None, "row", None),
        P(None, None, "col"),
        P(),
        P("row", "col"),
    )
    return jax.shard_map(shards, mesh=mesh, in_specs=in_specs, out_specs=out_specs, check_vma=False)
```
